32 devices in a mesh: dp: 4 (over x, core), mp: 8 (over z, y).
Axes of the slice: x: 2, y: 2, z: 4, core: 2. Of those that a mesh axis runs over, the one named last changes fastest.
Arguments:
- patches: bfloat16 [7680, 2048], P('dp'), may hold values from -6 to 6
- query_proj: bfloat16 [2048, 1024], P(None, 'mp'), may hold values from -0.3125 to 0.3125
- output_proj: bfloat16 [1024, 2048], P('mp'), may hold values from -0.1875 to 0.1875
- encoder_cache: bfloat16 [512, 128, 16, 128], P(('dp', 'mp')), may hold values from -28 to 28
- block_lengths: int32 [512], P(('dp', 'mp')), may hold values from 16 to 128
- neighbours: int32 [16, 32], replicated, may hold values from 0 to 511, as said below
- cotangent: bfloat16 [7680, 2048], P('dp'), may hold values from -6 to 6
Outputs:
- attended: bfloat16 [7680, 2048], P('dp', 'mp')
- patch_grad: bfloat16 [7680, 2048], P('dp', 'mp')
- query_grad: float32 [2048, 1024], P('dp', 'mp')
- output_grad: float32 [1024, 2048], P('mp', 'dp')
The draws below stay inside these ranges and needn't reach their ends.
Inputs may be any that keep to these rules, and one draw needn't show every extreme that they name: `neighbours`: each row names 32 different blocks. Device k (in dp+mp order) holds blocks k * 16 to k * 16 + 15; the 4 rows of one index of dp name the blocks of any one device at most 8 times in all, and some device's blocks exactly 8 times.
All inputs are finite; a program needn't handle non-finite values.
Results may differ from the reference program's by a relative error of at most 0.02.
The reference program's roundings to bfloat16 on the way (of `queries`, `back_heads`, `probs_low`, `heads_out`, `dscores` and `dquery`) count: a program that leaves them out, or rounds other values in their place, can miss the bound.
Values may be sent and summed in bfloat16 or wider, within the bound.
No kernel may reach another device: no remote copies, remote signals or barrier semaphores. Data moves between devices by JAX's collectives and lax.ppermute only.
A program may use at most 128 MiB of HBM per device.

```python
import math
import jax
import jax.numpy as jnp
import numpy as np
from jax import lax

D = 2048
HEADS = 16
HS = 64
BLK = 128
NB = 32
QB = 4
KB = 16
QROWS = 480
NQB = 16
TOKENS = 7680
OWNERS = 32
NKB = 512
CAP = 8


def draw_encoder_cache(key, part):
    shape = (NKB, BLK, HEADS, 2 * HS)
    values = jnp.clip(jax.random.normal(key, shape, jnp.float32), -6.0, 6.0)
    return values.astype(jnp.bfloat16)


def draw_block_lengths(key, part):
    raw = jax.random.randint(key, (NKB,), BLK // 8, BLK + BLK // 4 + 1)
    return jnp.minimum(raw, BLK).astype(jnp.int32)


def one_permutation(subkey):
    return jax.random.permutation(subkey, OWNERS)


def draw_neighbours(key, part):
    entry_count = QB * NB
    full_owners = entry_count // (2 * CAP)
    remainder = entry_count - full_owners * CAP
    others = OWNERS - full_owners
    base_count = remainder // others
    extra_count = remainder % others
    counts = np.array([CAP] * full_owners + [base_count + 1] * extra_count + [base_count] * (others - extra_count))
    bounds = np.cumsum(counts)
    positions = np.arange(entry_count)
    rank_of = np.sum(bounds[None, :] <= positions[:, None], axis=1)
    slot_index = np.arange(NB)
    patch_index = np.arange(QB)
    order_table = slot_index[None, :] * QB + patch_index[:, None]
    rank_table = rank_of[order_table]
    group_total = NQB // QB
    subkeys = jax.random.split(key, group_total + 1)
    permutes = jax.vmap(one_permutation)(subkeys[:group_total])
    owner_ids = permutes[:, rank_table]
    offsets = jax.random.randint(subkeys[group_total], (group_total, QB, 1), 0, KB)
    local_ids = (offsets + jnp.arange(NB, dtype=jnp.int32)[None, None, :]) % KB
    return (owner_ids * KB + local_ids).reshape(NQB, NB).astype(jnp.int32)


def block_scale(rng, shape, cuts, low, top_value):
    level = 1.0
    for position, parts in cuts:
        heights = jax.random.uniform(jax.random.fold_in(jax.random.fold_in(rng, 6), position), (parts,), jnp.float32, low / len(cuts), top_value / len(cuts))
        level = level * jnp.repeat(jnp.exp(heights), shape[position] // parts).reshape((-1,) + (1,) * (len(shape) - 1 - position))
    return level


def noise(stream_key, dims, scale, bound, cuts=(), held_as=jnp.bfloat16):
    gain = block_scale(stream_key, dims, cuts, -0.22, 0.18) if cuts else 1.0
    drawn = jax.random.normal(stream_key, dims, jnp.float32) * scale * gain
    return jnp.minimum(jnp.maximum(drawn, -bound), bound).astype(held_as)


def setup_inputs(seed: int = 0) -> dict:
    splits = jax.random.split(jax.random.key(seed), 8)
    patches = noise(splits[0], (TOKENS, D), 1.0, 6.0, ((0, 4),))
    query_proj = noise(splits[1], (D, HEADS * HS), (D * 4 // 25) ** -0.5, 0.3125, ((1, 8),))
    output_proj = noise(splits[2], (HEADS * HS, D), (HEADS * HS) ** -0.5, 0.1875, ((0, 8),))
    encoder_cache = draw_encoder_cache(jax.random.fold_in(splits[7], 71), 0)
    block_lengths = draw_block_lengths(jax.random.fold_in(splits[7], 71), 0)
    neighbours = draw_neighbours(jax.random.fold_in(splits[7], 71), 0)
    cotangent = noise(splits[6], (TOKENS, D), 1.0, 6.0, ((0, 4),))
    return dict(patches=patches, query_proj=query_proj, output_proj=output_proj, encoder_cache=encoder_cache, block_lengths=block_lengths, neighbours=neighbours, cotangent=cotangent)


masked_value = -1e+30

def rounded(array):
    return lax.optimization_barrier(array.astype(jnp.bfloat16))

def reference(patches, query_proj, output_proj, encoder_cache, block_lengths, neighbours, cotangent):
    head_scale = 1.0 / math.sqrt(HS)
    grad_scale = 1.0 / math.sqrt(TOKENS)
    queries = rounded(jnp.dot(patches, query_proj, preferred_element_type=jnp.float32) * head_scale)
    back_heads = rounded(jnp.dot(cotangent, output_proj.T, preferred_element_type=jnp.float32))
    queries = queries.reshape(NQB, QROWS, HEADS, HS)
    back_heads = back_heads.reshape(NQB, QROWS, HEADS, HS)

    def one_block(inputs):
        query_blk, back_blk, block_ids = inputs
        gathered = encoder_cache[block_ids].astype(jnp.float32)
        key_rows = gathered[..., :HS]
        value_rows = gathered[..., HS:]
        lengths = block_lengths[block_ids]
        visible = jnp.arange(BLK, dtype=jnp.int32)[None, :] < lengths[:, None]
        scores = jnp.einsum('rhd,sbhd->hrsb', query_blk.astype(jnp.float32), key_rows)
        scores = jnp.where(visible[None, None], scores, masked_value)
        row_max = lax.optimization_barrier(jnp.max(scores, axis=(2, 3), keepdims=True))
        weights = jnp.exp(scores - row_max)
        att_weights = weights / lax.optimization_barrier(jnp.sum(weights, axis=(2, 3), keepdims=True))
        probs_low = rounded(att_weights)
        heads_blk = rounded(jnp.einsum('hrsb,sbhd->rhd', probs_low.astype(jnp.float32), value_rows))
        dprobs = jnp.einsum('rhd,sbhd->hrsb', back_blk.astype(jnp.float32), value_rows)
        row_inner = lax.optimization_barrier(jnp.sum(att_weights * dprobs, axis=(2, 3), keepdims=True))
        dscores = rounded(att_weights * (dprobs - row_inner) * head_scale)
        dquery = rounded(jnp.einsum('hrsb,sbhd->rhd', dscores.astype(jnp.float32), key_rows))
        return (heads_blk, dquery)
    heads_all, dquery_all = lax.map(one_block, (queries, back_heads, neighbours))
    heads_out = heads_all.reshape(TOKENS, HEADS * HS)
    dquery_rows = dquery_all.reshape(TOKENS, HEADS * HS)
    attended = jnp.dot(heads_out, output_proj, preferred_element_type=jnp.float32).astype(jnp.bfloat16)
    patch_grad = jnp.dot(dquery_rows, query_proj.T, preferred_element_type=jnp.float32).astype(jnp.bfloat16)
    query_grad = jnp.dot(patches.T, dquery_rows, preferred_element_type=jnp.float32) * grad_scale
    output_grad = jnp.dot(heads_out.T, cotangent, preferred_element_type=jnp.float32) * grad_scale
    return (attended, patch_grad, query_grad, output_grad)
```

```python
import functools
import math

import jax
import jax.numpy as jnp
from jax import lax
from jax.experimental import pallas as pl
from jax.experimental.pallas import tpu as pltpu
from jax.sharding import Mesh
from jax.sharding import PartitionSpec as P

masked_value = -1e30
LANES = 128


def pack_kernel(chosen, counts, cache_ref, out_ref, *, chunk, local_heads, inner, capacity):
    slot = pl.program_id(0) * capacity + pl.program_id(1)

    @pl.when(pl.program_id(1) < counts[pl.program_id(0)])
    def _():
        by_head = pltpu.einshape("rhd->hrd", cache_ref[0])
        for r in range(inner):
            for half in range(2):
                out_ref[0, r, 0, half] = by_head[(half * inner + r) * local_heads + chunk]


def pack_blocks(chosen, counts, cache, chunk, groups, inner, capacity, local_heads):
    _, block_rows, heads, width = cache.shape
    return pl.pallas_call(
        functools.partial(
            pack_kernel, chunk=chunk, local_heads=local_heads, inner=inner, capacity=capacity
        ),
        grid_spec=pltpu.PrefetchScalarGridSpec(
            num_scalar_prefetch=2,
            grid=(groups, capacity),
            in_specs=[
                pl.BlockSpec(
                    (1, block_rows, heads, width),
                    lambda g, s, ch, ct: (ch[g * capacity + s], 0, 0, 0),
                )
            ],
            out_specs=pl.BlockSpec(
                (1, inner, 1, 2, block_rows, width), lambda g, s, ch, ct: (g, 0, s, 0, 0, 0)
            ),
        ),
        out_shape=jax.ShapeDtypeStruct(
            (groups, inner, capacity, 2, block_rows, width), cache.dtype
        ),
        compiler_params=pltpu.CompilerParams(vmem_limit_bytes=32 << 20),
        cost_estimate=pl.CostEstimate(
            flops=0, transcendentals=0, bytes_accessed=groups * capacity * 2 * 262144
        ),
    )(chosen, counts, cache)


def nt_dot(left, right):
    return lax.dot_general(
        left, right, (((1,), (1,)), ((), ())), preferred_element_type=jnp.float32
    )


def attention_kernel(
    places, lens, counts, q_ref, b_ref, recv_ref, co_ref, ds_ref,
    kv, scores, probs, top, acc, total, dacc, sems, *, slots, scale,
):
    patch = pl.program_id(0)
    patches = pl.num_programs(0)
    block_rows = recv_ref.shape[2]
    pair = 2 * block_rows

    def copy(which, j, place):
        return pltpu.make_async_copy(
            recv_ref.at[place],
            kv.at[which % 2, :, pl.ds(pl.multiple_of(j * block_rows, block_rows), block_rows), :],
            sems.at[which % 2, j],
        )

    def start(which):
        @pl.loop(0, counts[which])
        def _(j):
            copy(which, j, places[which * slots + j]).start()

    @pl.when(patch == 0)
    def _():
        start(patch)

    @pl.when(patch + 1 < patches)
    def _():
        start(patch + 1)

    here = counts[patch]
    tiles = jnp.maximum((here + 1) // 2, 1)

    @pl.loop(here, 2 * tiles)
    def _(j):
        kv[patch % 2, :, pl.ds(pl.multiple_of(j * block_rows, block_rows), block_rows), :] = (
            jnp.zeros((2, block_rows, kv.shape[3]), kv.dtype)
        )

    @pl.loop(0, here)
    def _(j):
        copy(patch, j, 0).wait()

    def key_tile(t, head):
        return kv[patch % 2, head, pl.ds(pl.multiple_of(t * pair, pair), pair), :]

    rows = q_ref.shape[0]
    for head in range(2):
        lanes = pl.ds(head * LANES, LANES)
        q = q_ref[:, lanes]
        back = b_ref[:, lanes]
        top[...] = jnp.full_like(top, masked_value)
        acc[...] = jnp.zeros_like(acc)
        total[...] = jnp.zeros_like(total)
        dacc[...] = jnp.zeros_like(dacc)

        @pl.loop(0, tiles)
        def _(t):
            place = lax.broadcasted_iota(jnp.int32, (1, block_rows), 1)
            seen_lo = place < lens[patch * slots + 2 * t]
            seen_hi = place < lens[patch * slots + 2 * t + 1]
            score = nt_dot(q, key_tile(t, head))
            low = jnp.where(seen_lo, score[:, :block_rows], masked_value)
            high = jnp.where(seen_hi, score[:, block_rows:], masked_value)
            scores[t, :, :block_rows] = low
            scores[t, :, block_rows:] = high
            top[...] = jnp.maximum(top[...], jnp.maximum(low, high))

        row_max = jnp.max(top[...], axis=1, keepdims=True)

        @pl.loop(0, tiles)
        def _(t):
            weights = jnp.exp(scores[t] - row_max).astype(jnp.bfloat16)
            probs[t] = weights
            wide = weights.astype(jnp.float32)
            total[...] += wide[:, :block_rows] + wide[:, block_rows:]
            acc[...] += jnp.dot(
                weights, key_tile(t, head), preferred_element_type=jnp.float32
            )

        row_sum = jnp.sum(total[...], axis=1, keepdims=True)
        inverse = 1.0 / row_sum
        outs = acc[...] * inverse
        inner = jnp.sum(outs * back.astype(jnp.float32), axis=1, keepdims=True)

        @pl.loop(0, tiles)
        def _(t):
            dprobs = nt_dot(back, key_tile(t, head))
            dscores = (probs[t].astype(jnp.float32) * (dprobs - inner)).astype(jnp.bfloat16)
            dacc[...] += jnp.dot(
                dscores, key_tile(t, head), preferred_element_type=jnp.float32
            )

        co_ref[:, lanes] = outs
        lane = lax.broadcasted_iota(jnp.int32, (rows, LANES), 1)
        stat = jnp.where(lane < 96, row_max + jnp.log(row_sum), inner)
        ds_ref[:, lanes] = jnp.where(lane < 64, dacc[...] * (inverse * scale), stat)


def attention(places, lens, counts, queries, backs, received, chunk, patch_blocks, slots, scale):
    rows = queries.shape[0] // patch_blocks
    total_rows = queries.shape[0]
    block_rows, width = received.shape[2:]
    wide = pl.BlockSpec((rows, 2 * LANES), lambda p, *_: (p, chunk))
    out = pl.BlockSpec((rows, 2 * LANES), lambda p, *_: (p, 0))
    tiles = (slots + 1) // 2
    return pl.pallas_call(
        functools.partial(attention_kernel, slots=slots, scale=scale),
        grid_spec=pltpu.PrefetchScalarGridSpec(
            num_scalar_prefetch=3,
            grid=(patch_blocks,),
            in_specs=[wide, wide, pl.BlockSpec(memory_space=pl.ANY)],
            out_specs=[out, out],
            scratch_shapes=[
                pltpu.VMEM((2, 2, tiles * 2 * block_rows, width), jnp.bfloat16),
                pltpu.VMEM((tiles, rows, 2 * block_rows), jnp.float32),
                pltpu.VMEM((tiles, rows, 2 * block_rows), jnp.bfloat16),
                pltpu.VMEM((rows, block_rows), jnp.float32),
                pltpu.VMEM((rows, width), jnp.float32),
                pltpu.VMEM((rows, block_rows), jnp.float32),
                pltpu.VMEM((rows, width), jnp.float32),
                pltpu.SemaphoreType.DMA((2, slots)),
            ],
        ),
        out_shape=[jax.ShapeDtypeStruct((total_rows, 2 * LANES), jnp.float32)] * 2,
        compiler_params=pltpu.CompilerParams(vmem_limit_bytes=44 << 20),
        cost_estimate=pl.CostEstimate(
            flops=8 * total_rows * slots * block_rows * width,
            transcendentals=total_rows * slots * block_rows,
            bytes_accessed=40 << 20,
        ),
    )(places, lens, counts, queries, backs, received)


def swap(x, axis):
    return lax.ppermute(x, axis, [(0, 1), (1, 0)])


def gather_half(x, zl_size, y_size):
    if zl_size == 2 and y_size == 2:
        place = 2 * lax.axis_index("zl") + lax.axis_index("y")
        cut = x.shape[0] // 2
        by_y = swap(x, "y")
        by_zl = swap(x, "zl")
        corner = jnp.concatenate([swap(by_y[:cut], "zl"), swap(by_zl[cut:], "y")], axis=0)
        return [x, by_y, by_zl, corner], jnp.stack([place, place ^ 1, place ^ 2, place ^ 3])
    whole = lax.all_gather(x, ("zl", "y"), axis=0, tiled=False)
    count = zl_size * y_size
    return [whole[i] for i in range(count)], jnp.arange(count, dtype=jnp.int32)


def scatter_sum(x, size, dim):
    index = lax.axis_index("dp")
    step = size // 2
    while step >= 1:
        half = x.shape[dim] // 2
        upper = (index // step) % 2
        keep = lax.dynamic_slice_in_dim(x, upper * half, half, dim)
        give = lax.dynamic_slice_in_dim(x, (1 - upper) * half, half, dim)
        got = lax.ppermute(
            give.astype(jnp.bfloat16), "dp", [(i, i ^ step) for i in range(size)]
        )
        x = keep + got.astype(jnp.float32)
        step //= 2
    return x


def local(
    patches, query_proj, output_proj, cache, block_lengths, neighbours, cotangent, *, sizes
):
    groups, zl_size, y_size = sizes
    inner = zl_size * y_size
    model = 2 * inner
    owner_count = groups * model
    group = lax.axis_index("dp")
    zh = lax.axis_index("zh")
    spot = lax.axis_index("zl") * y_size + lax.axis_index("y")
    me = group * model + zh * inner + spot
    local_blocks, block_rows, heads, width = cache.shape
    head_size = width // 2
    local_heads = query_proj.shape[1] // head_size
    features = patches.shape[1]
    columns = features // model
    slots = neighbours.shape[1]
    patch_blocks = neighbours.shape[0] // groups
    entry_count = patch_blocks * slots
    capacity = 2 * entry_count // owner_count
    row_count = patches.shape[0]
    head_scale = 1.0 / math.sqrt(head_size)
    grad_scale = 1.0 / math.sqrt(row_count * groups)

    all_ids = neighbours.reshape(groups, entry_count)
    match = all_ids // local_blocks == me
    order = jnp.arange(entry_count, dtype=jnp.int32)
    earlier = order[None, :] < order[:, None]
    rank = jnp.sum((match[:, None, :] & earlier[None]).astype(jnp.int32), axis=2)
    slot_range = jnp.arange(capacity, dtype=jnp.int32)
    placed = match[:, :, None] & (rank[:, :, None] == slot_range)
    chosen = jnp.sum(
        jnp.where(placed, (all_ids % local_blocks)[:, :, None], 0), axis=1
    ).reshape(groups * capacity)
    send_counts = jnp.sum(match.astype(jnp.int32), axis=1)

    packed = [
        pack_blocks(
            chosen, send_counts, cache, c, groups, inner, capacity, local_heads
        ).reshape(groups * inner, capacity * 2 * block_rows, width)
        for c in range(local_heads)
    ]
    received = [
        lax.all_to_all(x, ("dp", "zl", "y"), split_axis=0, concat_axis=0, tiled=True).reshape(
            groups * inner * capacity, 2, block_rows, width
        )
        for x in packed
    ]

    my_ids = lax.dynamic_slice_in_dim(
        neighbours, group * patch_blocks, patch_blocks, 0
    ).reshape(entry_count)
    owners = my_ids // local_blocks
    slot_of = jnp.sum(((owners[:, None] == owners[None, :]) & earlier).astype(jnp.int32), axis=1)
    source = (owners // model) * inner + owners % inner
    in_half = ((owners % model) // inner == zh).reshape(patch_blocks, slots)
    arrival = (source * capacity + slot_of).reshape(patch_blocks, slots)
    every_length = lax.all_gather(
        block_lengths, ("dp", "zh", "zl", "y"), axis=0, tiled=True
    )
    entry_length = every_length[my_ids].reshape(patch_blocks, slots)
    spots = jnp.arange(slots, dtype=jnp.int32)
    before = jnp.sum(
        (in_half[:, None, :] & (spots[None, :] < spots[:, None])[None]).astype(jnp.int32), axis=2
    )
    at = in_half[:, :, None] & (before[:, :, None] == spots)
    places = jnp.sum(jnp.where(at, arrival[:, :, None], 0), axis=1).reshape(entry_count)
    lens = jnp.sum(jnp.where(at, entry_length[:, :, None], 0), axis=1).reshape(entry_count)
    counts = jnp.sum(in_half.astype(jnp.int32), axis=1)

    def both_halves(own):
        other = swap(own, "zh")
        return jnp.where(zh == 0, own, other), jnp.where(zh == 0, other, own)

    q_halves = [
        w.reshape(features, local_heads, head_size) for w in both_halves(query_proj)
    ]
    q_wide = jnp.stack(q_halves, axis=2)
    q_wide = jnp.pad(q_wide, ((0, 0), (0, 0), (0, 0), (0, LANES - head_size)))
    q_wide = q_wide.reshape(features, local_heads * 2 * LANES)
    o_halves = [
        w.reshape(local_heads, head_size, features) for w in both_halves(output_proj)
    ]
    o_wide = jnp.stack(o_halves, axis=1)
    o_wide = jnp.pad(o_wide, ((0, 0), (0, 0), (LANES - head_size, 0), (0, 0)))
    o_wide = o_wide.reshape(local_heads * 2 * LANES, features)
    queries = (
        jnp.dot(patches, q_wide, preferred_element_type=jnp.float32) * head_scale
    ).astype(jnp.bfloat16)
    backs = nt_dot(cotangent, o_wide).astype(jnp.bfloat16)

    mp = ("zh", "zl", "y")
    o_cols = output_proj.reshape(local_heads * head_size, model, columns).transpose(1, 0, 2)
    o_cols = lax.all_to_all(o_cols, mp, split_axis=0, concat_axis=0, tiled=True)
    o_cols = o_cols.reshape(2, inner, local_heads, head_size, columns)
    q_cols = query_proj.reshape(model, columns, local_heads * head_size).transpose(0, 2, 1)
    q_cols = lax.all_to_all(q_cols, mp, split_axis=0, concat_axis=0, tiled=True)
    q_cols = q_cols.reshape(2, inner, local_heads, head_size, columns)

    def tail_weights(cols, c, first, order):
        piece = jnp.moveaxis(cols[:, :, c], 0, 1)
        empty = jnp.zeros_like(piece)
        pair = [piece, empty] if first else [empty, piece]
        stacked = jnp.stack(pair, axis=2).reshape(inner, 2 * LANES, columns)
        return stacked[order].reshape(inner * 2 * LANES, columns)

    lane = jnp.arange(2 * LANES, dtype=jnp.int32)
    lower = (lane % LANES < head_size)[None, :]
    first_head = (lane < LANES)[None, :]
    attended = None
    patch_grad = None
    own = []
    for c in range(local_heads):
        outs, douts = attention(
            places, lens, counts, queries, backs, received[c], c, patch_blocks, slots, head_scale
        )
        lse = douts[:, 64], douts[:, LANES + 64]
        inner_sum = douts[:, 96], douts[:, LANES + 96]
        theirs = swap(jnp.stack(lse + inner_sum), "zh")

        def per_head(pair):
            return jnp.where(first_head, pair[0][:, None], pair[1][:, None])

        weight = per_head([jax.nn.sigmoid(lse[i] - theirs[i]) for i in range(2)])
        shift = per_head(
            [
                jax.nn.sigmoid(theirs[i] - lse[i]) * (inner_sum[i] - theirs[2 + i]) * head_scale
                for i in range(2)
            ]
        )
        part = weight * jnp.where(lower, douts + shift * outs, outs)
        merged = (part + swap(part.astype(jnp.bfloat16), "zh").astype(jnp.float32)).astype(
            jnp.bfloat16
        )
        pieces, order = gather_half(merged, zl_size, y_size)
        every = jnp.concatenate(pieces, axis=1)
        att = jnp.dot(
            every, tail_weights(o_cols, c, False, order), preferred_element_type=jnp.float32
        )
        grad = jnp.dot(
            every, tail_weights(q_cols, c, True, order), preferred_element_type=jnp.float32
        )
        attended = att if attended is None else attended + att
        patch_grad = grad if patch_grad is None else patch_grad + grad
        own.append(lax.dynamic_slice_in_dim(merged, zh * LANES, LANES, 1))

    dquery = jnp.concatenate([x[:, :head_size] for x in own], axis=1)
    heads_out = jnp.concatenate([x[:, head_size:] for x in own], axis=1)
    query_term = (
        lax.dot_general(
            patches, dquery, (((0,), (0,)), ((), ())), preferred_element_type=jnp.float32
        )
        * grad_scale
    )
    output_term = (
        lax.dot_general(
            heads_out, cotangent, (((0,), (0,)), ((), ())), preferred_element_type=jnp.float32
        )
        * grad_scale
    )
    return (
        attended.astype(jnp.bfloat16),
        patch_grad.astype(jnp.bfloat16),
        scatter_sum(query_term, groups, 0),
        scatter_sum(output_term, groups, 1),
    )


def solution(mesh):
    groups, model = mesh.shape["dp"], mesh.shape["mp"]
    sizes = (groups, model // 4, 2)
    split = Mesh(
        mesh.devices.reshape(groups, 2, model // 4, 2), ("dp", "zh", "zl", "y")
    )
    mp = ("zh", "zl", "y")
    every = ("dp",) + mp
    return jax.shard_map(
        functools.partial(local, sizes=sizes),
        mesh=split,
        in_specs=(
            P("dp", None),
            P(None, mp),
            P(mp, None),
            P(every, None, None, None),
            P(every),
            P(),
            P("dp", None),
        ),
        out_specs=(P("dp", mp), P("dp", mp), P("dp", mp), P(mp, "dp")),
        check_vma=False,
    )
```

```python
import functools
import math

import jax
import jax.numpy as jnp
from jax import lax
from jax.experimental import pallas as pl
from jax.experimental.pallas import tpu as pltpu
from jax.sharding import Mesh
from jax.sharding import PartitionSpec as P

masked_value = -1e30
LANES = 128


def pack_kernel(chosen, counts, cache_ref, out_ref, *, chunk, local_heads, inner, capacity):
    slot = pl.program_id(0) * capacity + pl.program_id(1)

    @pl.when(pl.program_id(1) < counts[pl.program_id(0)])
    def _():
        by_head = pltpu.einshape("rhd->hrd", cache_ref[0])
        for r in range(inner):
            for half in range(2):
                out_ref[0, r, 0, half] = by_head[(half * inner + r) * local_heads + chunk]


def pack_blocks(chosen, counts, cache, chunk, groups, inner, capacity, local_heads):
    _, block_rows, heads, width = cache.shape
    return pl.pallas_call(
        functools.partial(
            pack_kernel, chunk=chunk, local_heads=local_heads, inner=inner, capacity=capacity
        ),
        grid_spec=pltpu.PrefetchScalarGridSpec(
            num_scalar_prefetch=2,
            grid=(groups, capacity),
            in_specs=[
                pl.BlockSpec(
                    (1, block_rows, heads, width),
                    lambda g, s, ch, ct: (ch[g * capacity + s], 0, 0, 0),
                )
            ],
            out_specs=pl.BlockSpec(
                (1, inner, 1, 2, block_rows, width), lambda g, s, ch, ct: (g, 0, s, 0, 0, 0)
            ),
        ),
        out_shape=jax.ShapeDtypeStruct(
            (groups, inner, capacity, 2, block_rows, width), cache.dtype
        ),
        compiler_params=pltpu.CompilerParams(vmem_limit_bytes=32 << 20),
        cost_estimate=pl.CostEstimate(
            flops=0, transcendentals=0, bytes_accessed=groups * capacity * 2 * 262144
        ),
    )(chosen, counts, cache)


def nt_dot(left, right):
    return lax.dot_general(
        left, right, (((1,), (1,)), ((), ())), preferred_element_type=jnp.float32
    )


def attention_kernel(
    places, lens, counts, q_ref, b_ref, recv_ref, co_ref, ds_ref, stat_ref,
    kv, scores, probs, top, acc, total, dacc, columns, sems, *, slots, scale,
):
    patch = pl.program_id(0)
    patches = pl.num_programs(0)
    block_rows = recv_ref.shape[2]
    pair = 2 * block_rows

    def copy(which, j, place):
        return pltpu.make_async_copy(
            recv_ref.at[place],
            kv.at[which % 2, :, pl.ds(pl.multiple_of(j * block_rows, block_rows), block_rows), :],
            sems.at[which % 2, j],
        )

    def start(which):
        @pl.loop(0, counts[which])
        def _(j):
            copy(which, j, places[which * slots + j]).start()

    @pl.when(patch == 0)
    def _():
        start(patch)

    @pl.when(patch + 1 < patches)
    def _():
        start(patch + 1)

    here = counts[patch]
    tiles = jnp.maximum((here + 1) // 2, 1)

    @pl.loop(here, 2 * tiles)
    def _(j):
        kv[patch % 2, :, pl.ds(pl.multiple_of(j * block_rows, block_rows), block_rows), :] = (
            jnp.zeros((2, block_rows, kv.shape[3]), kv.dtype)
        )

    @pl.loop(0, here)
    def _(j):
        copy(patch, j, 0).wait()

    def key_tile(t, head):
        return kv[patch % 2, head, pl.ds(pl.multiple_of(t * pair, pair), pair), :]

    rows = q_ref.shape[0]
    lanes = [pl.ds(head * LANES, LANES) for head in range(2)]
    top[...] = jnp.full_like(top, masked_value)
    acc[...] = jnp.zeros_like(acc)
    total[...] = jnp.zeros_like(total)
    dacc[...] = jnp.zeros_like(dacc)

    @pl.loop(0, tiles)
    def _(t):
        place = lax.broadcasted_iota(jnp.int32, (1, block_rows), 1)
        seen_lo = place < lens[patch * slots + 2 * t]
        seen_hi = place < lens[patch * slots + 2 * t + 1]
        for head in range(2):
            score = nt_dot(q_ref[:, lanes[head]], key_tile(t, head))
            low = jnp.where(seen_lo, score[:, :block_rows], masked_value)
            high = jnp.where(seen_hi, score[:, block_rows:], masked_value)
            scores[head, t, :, :block_rows] = low
            scores[head, t, :, block_rows:] = high
            top[head] = jnp.maximum(top[head], jnp.maximum(low, high))

    row_max = [jnp.max(top[head], axis=1, keepdims=True) for head in range(2)]

    @pl.loop(0, tiles)
    def _(t):
        for head in range(2):
            weights = jnp.exp(scores[head, t] - row_max[head]).astype(jnp.bfloat16)
            probs[head, t] = weights
            wide = weights.astype(jnp.float32)
            total[head] += wide[:, :block_rows] + wide[:, block_rows:]
            acc[head] += jnp.dot(weights, key_tile(t, head), preferred_element_type=jnp.float32)

    inverse, inner, stats = [], [], []
    for head in range(2):
        row_sum = jnp.sum(total[head], axis=1, keepdims=True)
        inverse.append(1.0 / row_sum)
        outs = acc[head] * inverse[head]
        co_ref[:, lanes[head]] = outs
        inner.append(
            jnp.sum(outs * b_ref[:, lanes[head]].astype(jnp.float32), axis=1, keepdims=True)
        )
        stats += [row_max[head] + jnp.log(row_sum), inner[head]]

    @pl.loop(0, tiles)
    def _(t):
        for head in range(2):
            dprobs = nt_dot(b_ref[:, lanes[head]], key_tile(t, head))
            dscores = (probs[head, t].astype(jnp.float32) * (dprobs - inner[head])).astype(
                jnp.bfloat16
            )
            dacc[head] += jnp.dot(dscores, key_tile(t, head), preferred_element_type=jnp.float32)

    for head in range(2):
        ds_ref[:, lanes[head]] = dacc[head] * (inverse[head] * scale)
    lane = lax.broadcasted_iota(jnp.int32, (rows, LANES), 1)
    columns[rows:, :] = jnp.zeros((columns.shape[0] - rows, LANES), jnp.float32)
    picked = jnp.where(lane == 0, stats[0], stats[1])
    picked = jnp.where(lane == 2, stats[2], picked)
    columns[:rows, :] = jnp.where(lane == 3, stats[3], picked)
    stat_ref[0] = jnp.transpose(columns[...])[:8]


def attention(places, lens, counts, queries, backs, received, chunk, patch_blocks, slots, scale):
    rows = queries.shape[0] // patch_blocks
    total_rows = queries.shape[0]
    padded = pl.cdiv(rows, LANES) * LANES
    block_rows, width = received.shape[2:]
    wide = pl.BlockSpec((rows, 2 * LANES), lambda p, *_: (p, chunk))
    out = pl.BlockSpec((rows, 2 * LANES), lambda p, *_: (p, 0))
    tiles = (slots + 1) // 2
    return pl.pallas_call(
        functools.partial(attention_kernel, slots=slots, scale=scale),
        grid_spec=pltpu.PrefetchScalarGridSpec(
            num_scalar_prefetch=3,
            grid=(patch_blocks,),
            in_specs=[wide, wide, pl.BlockSpec(memory_space=pl.ANY)],
            out_specs=[out, out, pl.BlockSpec((1, 8, padded), lambda p, *_: (p, 0, 0))],
            scratch_shapes=[
                pltpu.VMEM((2, 2, tiles * 2 * block_rows, width), jnp.bfloat16),
                pltpu.VMEM((2, tiles, rows, 2 * block_rows), jnp.float32),
                pltpu.VMEM((2, tiles, rows, 2 * block_rows), jnp.bfloat16),
                pltpu.VMEM((2, rows, block_rows), jnp.float32),
                pltpu.VMEM((2, rows, width), jnp.float32),
                pltpu.VMEM((2, rows, block_rows), jnp.float32),
                pltpu.VMEM((2, rows, width), jnp.float32),
                pltpu.VMEM((padded, LANES), jnp.float32),
                pltpu.SemaphoreType.DMA((2, slots)),
            ],
        ),
        out_shape=[jax.ShapeDtypeStruct((total_rows, 2 * LANES), jnp.float32)] * 2
        + [jax.ShapeDtypeStruct((patch_blocks, 8, padded), jnp.float32)],
        compiler_params=pltpu.CompilerParams(vmem_limit_bytes=48 << 20),
        cost_estimate=pl.CostEstimate(
            flops=8 * total_rows * slots * block_rows * width,
            transcendentals=total_rows * slots * block_rows,
            bytes_accessed=40 << 20,
        ),
    )(places, lens, counts, queries, backs, received)


def merge_kernel(co_ref, ds_ref, mine_ref, theirs_ref, out_ref, *, scale, split):
    rows = co_ref.shape[0]
    mine, theirs = mine_ref[0], theirs_ref[0]
    kind = lax.broadcasted_iota(jnp.int32, mine.shape, 0)
    gap = mine - theirs
    share = 1.0 / (1.0 + jnp.exp(-gap))
    rest = 1.0 / (1.0 + jnp.exp(gap))
    rest_below = jnp.concatenate([rest[:1], rest[:-1]], axis=0)
    table = jnp.where(kind % 2 == 0, share, rest_below * gap * scale)
    tall = jnp.transpose(
        jnp.concatenate([table, jnp.zeros((LANES - 8, table.shape[1]), jnp.float32)], axis=0)
    )[:rows]
    lower = lax.broadcasted_iota(jnp.int32, (rows, LANES), 1) < split
    for head in range(2):
        lanes = pl.ds(head * LANES, LANES)
        weight = tall[:, 2 * head : 2 * head + 1]
        shift = tall[:, 2 * head + 1 : 2 * head + 2]
        outs = co_ref[:, lanes]
        value = weight * jnp.where(lower, ds_ref[:, lanes] + shift * outs, outs)
        out_ref[:, lanes] = value.astype(jnp.bfloat16)


def merge(outs, douts, mine, theirs, scale, split):
    patch_blocks, _, padded = mine.shape
    rows = outs.shape[0] // patch_blocks
    wide = pl.BlockSpec((rows, 2 * LANES), lambda p: (p, 0))
    flat = pl.BlockSpec((1, 8, padded), lambda p: (p, 0, 0))
    return pl.pallas_call(
        functools.partial(merge_kernel, scale=scale, split=split),
        grid=(patch_blocks,),
        in_specs=[wide, wide, flat, flat],
        out_specs=wide,
        out_shape=jax.ShapeDtypeStruct(outs.shape, jnp.bfloat16),
        cost_estimate=pl.CostEstimate(
            flops=10 * outs.size, transcendentals=0, bytes_accessed=10 * outs.size
        ),
    )(outs, douts, mine, theirs)


def project_kernel(*refs, count, last):
    pieces, weights = refs[:count], refs[count]
    value = jnp.dot(pieces[0][...], weights[0], preferred_element_type=jnp.float32)
    for i in range(1, count):
        value += jnp.dot(pieces[i][...], weights[i], preferred_element_type=jnp.float32)
    rest = refs[count + 1 :]
    if not last:
        rest[-1][...] = value if len(rest) == 1 else rest[0][...] + value
        return
    if len(rest) == 3:
        value += rest[0][...]
    width = rest[-1].shape[1]
    rest[-2][...] = value[:, :width].astype(jnp.bfloat16)
    rest[-1][...] = value[:, width:].astype(jnp.bfloat16)


def project(pieces, weights, before, last):
    count = len(pieces)
    total_rows, depth = pieces[0].shape
    width = weights.shape[2]
    tile = total_rows // 4
    rowwise = lambda w: pl.BlockSpec((tile, w), lambda i: (i, 0))
    halves = jax.ShapeDtypeStruct((total_rows, width // 2), jnp.bfloat16)
    return pl.pallas_call(
        functools.partial(project_kernel, count=count, last=last),
        grid=(4,),
        in_specs=[rowwise(depth)] * count
        + [pl.BlockSpec(weights.shape, lambda i: (0, 0, 0))]
        + ([] if before is None else [rowwise(width)]),
        out_specs=[rowwise(width // 2)] * 2 if last else rowwise(width),
        out_shape=[halves] * 2
        if last
        else jax.ShapeDtypeStruct((total_rows, width), jnp.float32),
        compiler_params=pltpu.CompilerParams(vmem_limit_bytes=40 << 20),
        cost_estimate=pl.CostEstimate(
            flops=2 * total_rows * depth * count * width,
            transcendentals=0,
            bytes_accessed=2 * total_rows * (depth * count + 2 * width),
        ),
    )(*pieces, weights, *([] if before is None else [before]))


def swap(x, axis):
    return lax.ppermute(x, axis, [(0, 1), (1, 0)])


def gather_half(x, zl_size, y_size):
    if zl_size == 2 and y_size == 2:
        cut = x.shape[0] // 2
        by_y = swap(x, "y")
        by_zl = swap(x, "zl")
        corner = jnp.concatenate([swap(by_y[:cut], "zl"), swap(by_zl[cut:], "y")], axis=0)
        return [x, by_y, by_zl, corner]
    whole = lax.all_gather(x, ("zl", "y"), axis=0, tiled=False)
    return [whole[i] for i in range(zl_size * y_size)]


def scatter_sum(x, size, dim):
    index = lax.axis_index("dp")
    step = size // 2
    while step >= 1:
        half = x.shape[dim] // 2
        upper = (index // step) % 2
        keep = lax.dynamic_slice_in_dim(x, upper * half, half, dim)
        give = lax.dynamic_slice_in_dim(x, (1 - upper) * half, half, dim)
        got = lax.ppermute(
            give.astype(jnp.bfloat16), "dp", [(i, i ^ step) for i in range(size)]
        )
        x = keep + got.astype(jnp.float32)
        step //= 2
    return x


def local(
    patches, query_proj, output_proj, cache, block_lengths, neighbours, cotangent, *, sizes
):
    groups, zl_size, y_size = sizes
    inner = zl_size * y_size
    model = 2 * inner
    owner_count = groups * model
    group = lax.axis_index("dp")
    zh = lax.axis_index("zh")
    spot = lax.axis_index("zl") * y_size + lax.axis_index("y")
    me = group * model + zh * inner + spot
    local_blocks, block_rows, heads, width = cache.shape
    head_size = width // 2
    local_heads = query_proj.shape[1] // head_size
    features = patches.shape[1]
    columns = features // model
    slots = neighbours.shape[1]
    patch_blocks = neighbours.shape[0] // groups
    entry_count = patch_blocks * slots
    capacity = 2 * entry_count // owner_count
    row_count = patches.shape[0]
    head_scale = 1.0 / math.sqrt(head_size)
    grad_scale = 1.0 / math.sqrt(row_count * groups)

    all_ids = neighbours.reshape(groups, entry_count)
    match = all_ids // local_blocks == me
    order = jnp.arange(entry_count, dtype=jnp.int32)
    earlier = order[None, :] < order[:, None]
    rank = jnp.sum((match[:, None, :] & earlier[None]).astype(jnp.int32), axis=2)
    slot_range = jnp.arange(capacity, dtype=jnp.int32)
    placed = match[:, :, None] & (rank[:, :, None] == slot_range)
    chosen = jnp.sum(
        jnp.where(placed, (all_ids % local_blocks)[:, :, None], 0), axis=1
    ).reshape(groups * capacity)
    send_counts = jnp.sum(match.astype(jnp.int32), axis=1)

    def pack(c):
        return pack_blocks(
            chosen, send_counts, cache, c, groups, inner, capacity, local_heads
        ).reshape(groups * inner, capacity * 2 * block_rows, width)

    def exchange(x):
        return lax.all_to_all(
            x, ("dp", "zl", "y"), split_axis=0, concat_axis=0, tiled=True
        ).reshape(groups * inner * capacity, 2, block_rows, width)

    received = [exchange(pack(0))]

    my_ids = lax.dynamic_slice_in_dim(
        neighbours, group * patch_blocks, patch_blocks, 0
    ).reshape(entry_count)
    owners = my_ids // local_blocks
    slot_of = jnp.sum(((owners[:, None] == owners[None, :]) & earlier).astype(jnp.int32), axis=1)
    source = (owners // model) * inner + owners % inner
    in_half = ((owners % model) // inner == zh).reshape(patch_blocks, slots)
    arrival = (source * capacity + slot_of).reshape(patch_blocks, slots)
    every_length = lax.dynamic_update_slice_in_dim(
        jnp.zeros((owner_count * local_blocks,), jnp.int32), block_lengths, me * local_blocks, 0
    )
    for axis, size in (("y", y_size), ("zl", zl_size), ("dp", groups)):
        step = 1
        while step < size:
            every_length += lax.ppermute(
                every_length, axis, [(i, i ^ step) for i in range(size)]
            )
            step *= 2
    entry_length = every_length[my_ids].reshape(patch_blocks, slots)
    spots = jnp.arange(slots, dtype=jnp.int32)
    before = jnp.sum(
        (in_half[:, None, :] & (spots[None, :] < spots[:, None])[None]).astype(jnp.int32), axis=2
    )
    at = in_half[:, :, None] & (before[:, :, None] == spots)
    places = jnp.sum(jnp.where(at, arrival[:, :, None], 0), axis=1).reshape(entry_count)
    lens = jnp.sum(jnp.where(at, entry_length[:, :, None], 0), axis=1).reshape(entry_count)
    counts = jnp.sum(in_half.astype(jnp.int32), axis=1)

    def both_halves(own):
        other = swap(own, "zh")
        return jnp.where(zh == 0, own, other), jnp.where(zh == 0, other, own)

    q_halves = [
        w.reshape(features, local_heads, head_size) for w in both_halves(query_proj)
    ]
    q_wide = jnp.stack(q_halves, axis=2)
    q_wide = jnp.pad(q_wide, ((0, 0), (0, 0), (0, 0), (0, LANES - head_size)))
    q_wide = q_wide.reshape(features, local_heads * 2 * LANES)
    o_halves = [
        w.reshape(local_heads, head_size, features) for w in both_halves(output_proj)
    ]
    o_wide = jnp.stack(o_halves, axis=1)
    o_wide = jnp.pad(o_wide, ((0, 0), (0, 0), (LANES - head_size, 0), (0, 0)))
    o_wide = o_wide.reshape(local_heads * 2 * LANES, features)
    queries = (
        jnp.dot(patches, q_wide, preferred_element_type=jnp.float32) * head_scale
    ).astype(jnp.bfloat16)
    backs = nt_dot(cotangent, o_wide).astype(jnp.bfloat16)

    places, lens, counts, queries, backs, cache = lax.optimization_barrier(
        (places, lens, counts, queries, backs, cache)
    )
    for c in range(1, local_heads):
        received.append(exchange(pack(c)))

    cols = jnp.concatenate(
        [
            output_proj.reshape(local_heads * head_size, model, columns).transpose(1, 0, 2),
            query_proj.reshape(model, columns, local_heads * head_size).transpose(0, 2, 1),
        ],
        axis=2,
    )
    cols, received[-1] = lax.optimization_barrier((cols, received[-1]))
    cols = lax.all_to_all(cols, ("zh", "zl", "y"), split_axis=0, concat_axis=0, tiled=True)
    cols = cols.reshape(2, inner, local_heads, head_size, 2 * columns)
    right = jnp.arange(2 * columns)[None, None, None, :] >= columns
    if zl_size == 2 and y_size == 2:
        order = jnp.stack([spot, spot ^ 1, spot ^ 2, spot ^ 3])
    else:
        order = jnp.arange(inner, dtype=jnp.int32)

    def tail_weights(c):
        both = jnp.moveaxis(cols[:, :, c], 0, 1)
        pair = [jnp.where(right, both, 0), jnp.where(right, 0, both)]
        return jnp.stack(pair, axis=2).reshape(inner, 2 * LANES, 2 * columns)[order]

    finals = [tail_weights(c) for c in range(local_heads)]

    result = None
    own = []
    for c in range(local_heads):
        outs, douts, mine = attention(
            places, lens, counts, queries, backs, received[c], c, patch_blocks, slots, head_scale
        )
        theirs = swap(mine, "zh")
        part = merge(outs, douts, mine, theirs, head_scale, head_size)
        merged = (part.astype(jnp.float32) + swap(part, "zh").astype(jnp.float32)).astype(
            jnp.bfloat16
        )
        if c + 1 < local_heads:
            merged, received[c + 1] = lax.optimization_barrier((merged, received[c + 1]))
        pieces = gather_half(merged, zl_size, y_size)
        result = project(pieces, finals[c], result, c + 1 == local_heads)
        own.append(lax.dynamic_slice_in_dim(merged, zh * LANES, LANES, 1))
    attended, patch_grad = result

    dquery = jnp.concatenate([x[:, :head_size] for x in own], axis=1)
    heads_out = jnp.concatenate([x[:, head_size:] for x in own], axis=1)
    query_term = (
        lax.dot_general(
            patches, dquery, (((0,), (0,)), ((), ())), preferred_element_type=jnp.float32
        )
        * grad_scale
    )
    output_term = (
        lax.dot_general(
            heads_out, cotangent, (((0,), (0,)), ((), ())), preferred_element_type=jnp.float32
        )
        * grad_scale
    )
    return (
        attended,
        patch_grad,
        scatter_sum(query_term, groups, 0),
        scatter_sum(output_term, groups, 1),
    )


def solution(mesh):
    groups, model = mesh.shape["dp"], mesh.shape["mp"]
    sizes = (groups, model // 4, 2)
    split = Mesh(
        mesh.devices.reshape(groups, 2, model // 4, 2), ("dp", "zh", "zl", "y")
    )
    mp = ("zh", "zl", "y")
    every = ("dp",) + mp
    return jax.shard_map(
        functools.partial(local, sizes=sizes),
        mesh=split,
        in_specs=(
            P("dp", None),
            P(None, mp),
            P(mp, None),
            P(every, None, None, None),
            P(every),
            P(),
            P("dp", None),
        ),
        out_specs=(P("dp", mp), P("dp", mp), P("dp", mp), P(mp, "dp")),
        check_vma=False,
    )
```

```python
import functools
import math

import jax
import jax.numpy as jnp
from jax import lax
from jax.experimental import pallas as pl
from jax.experimental.pallas import tpu as pltpu
from jax.sharding import Mesh
from jax.sharding import PartitionSpec as P

masked_value = -1e30
LANES = 128


def pack_kernel(chosen, counts, cache_ref, out_ref, *, chunk, local_heads, inner, capacity):
    slot = pl.program_id(0) * capacity + pl.program_id(1)

    @pl.when(pl.program_id(1) < counts[pl.program_id(0)])
    def _():
        by_head = pltpu.einshape("rhd->hrd", cache_ref[0])
        for r in range(inner):
            for half in range(2):
                out_ref[0, r, 0, half] = by_head[(half * inner + r) * local_heads + chunk]


def pack_blocks(chosen, counts, cache, chunk, groups, inner, capacity, local_heads):
    _, block_rows, heads, width = cache.shape
    return pl.pallas_call(
        functools.partial(
            pack_kernel, chunk=chunk, local_heads=local_heads, inner=inner, capacity=capacity
        ),
        grid_spec=pltpu.PrefetchScalarGridSpec(
            num_scalar_prefetch=2,
            grid=(groups, capacity),
            in_specs=[
                pl.BlockSpec(
                    (1, block_rows, heads, width),
                    lambda g, s, ch, ct: (ch[g * capacity + s], 0, 0, 0),
                )
            ],
            out_specs=pl.BlockSpec(
                (1, inner, 1, 2, block_rows, width), lambda g, s, ch, ct: (g, 0, s, 0, 0, 0)
            ),
        ),
        out_shape=jax.ShapeDtypeStruct(
            (groups, inner, capacity, 2, block_rows, width), cache.dtype
        ),
        compiler_params=pltpu.CompilerParams(vmem_limit_bytes=58 << 20),
        cost_estimate=pl.CostEstimate(
            flops=0, transcendentals=0, bytes_accessed=groups * capacity * 2 * 262144
        ),
    )(chosen, counts, cache)


def nt_dot(left, right):
    return lax.dot_general(
        left, right, (((1,), (1,)), ((), ())), preferred_element_type=jnp.float32
    )


def attention_kernel(
    places, lens, counts, q_ref, b_ref, recv_ref, co_ref, ds_ref, stat_ref,
    kv, scores, probs, top, acc, total, dacc, columns, sems, *, slots, scale, first,
):
    patch = first + pl.program_id(0)
    patches = first + pl.num_programs(0)
    block_rows = recv_ref.shape[2]
    pair = 2 * block_rows

    def copy(which, j, place):
        return pltpu.make_async_copy(
            recv_ref.at[place],
            kv.at[which % 2, :, pl.ds(pl.multiple_of(j * block_rows, block_rows), block_rows), :],
            sems.at[which % 2, j],
        )

    def start(which):
        @pl.loop(0, counts[which])
        def _(j):
            copy(which, j, places[which * slots + j]).start()

    @pl.when(patch == first)
    def _():
        start(patch)

    @pl.when(patch + 1 < patches)
    def _():
        start(patch + 1)

    here = counts[patch]
    tiles = jnp.maximum((here + 1) // 2, 1)

    @pl.loop(here, 2 * tiles)
    def _(j):
        kv[patch % 2, :, pl.ds(pl.multiple_of(j * block_rows, block_rows), block_rows), :] = (
            jnp.zeros((2, block_rows, kv.shape[3]), kv.dtype)
        )

    @pl.loop(0, here)
    def _(j):
        copy(patch, j, 0).wait()

    def key_tile(t, head):
        return kv[patch % 2, head, pl.ds(pl.multiple_of(t * pair, pair), pair), :]

    rows = q_ref.shape[0]
    lanes = [pl.ds(head * LANES, LANES) for head in range(2)]
    top[...] = jnp.full_like(top, masked_value)
    acc[...] = jnp.zeros_like(acc)
    total[...] = jnp.zeros_like(total)
    dacc[...] = jnp.zeros_like(dacc)

    @pl.loop(0, tiles)
    def _(t):
        place = lax.broadcasted_iota(jnp.int32, (1, block_rows), 1)
        seen_lo = place < lens[patch * slots + 2 * t]
        seen_hi = place < lens[patch * slots + 2 * t + 1]
        for head in range(2):
            score = nt_dot(q_ref[:, lanes[head]], key_tile(t, head))
            low = jnp.where(seen_lo, score[:, :block_rows], masked_value)
            high = jnp.where(seen_hi, score[:, block_rows:], masked_value)
            scores[head, t, :, :block_rows] = low
            scores[head, t, :, block_rows:] = high
            top[head] = jnp.maximum(top[head], jnp.maximum(low, high))

    row_max = [jnp.max(top[head], axis=1, keepdims=True) for head in range(2)]

    @pl.loop(0, tiles)
    def _(t):
        for head in range(2):
            weights = jnp.exp(scores[head, t] - row_max[head]).astype(jnp.bfloat16)
            probs[head, t] = weights
            wide = weights.astype(jnp.float32)
            total[head] += wide[:, :block_rows] + wide[:, block_rows:]
            acc[head] += jnp.dot(weights, key_tile(t, head), preferred_element_type=jnp.float32)

    inverse, inner, stats = [], [], []
    for head in range(2):
        row_sum = jnp.sum(total[head], axis=1, keepdims=True)
        inverse.append(1.0 / row_sum)
        outs = acc[head] * inverse[head]
        co_ref[:, lanes[head]] = outs
        inner.append(
            jnp.sum(outs * b_ref[:, lanes[head]].astype(jnp.float32), axis=1, keepdims=True)
        )
        stats += [row_max[head] + jnp.log(row_sum), inner[head]]

    @pl.loop(0, tiles)
    def _(t):
        for head in range(2):
            dprobs = nt_dot(b_ref[:, lanes[head]], key_tile(t, head))
            dscores = (probs[head, t].astype(jnp.float32) * (dprobs - inner[head])).astype(
                jnp.bfloat16
            )
            dacc[head] += jnp.dot(dscores, key_tile(t, head), preferred_element_type=jnp.float32)

    for head in range(2):
        ds_ref[:, lanes[head]] = dacc[head] * (inverse[head] * scale)
    lane = lax.broadcasted_iota(jnp.int32, (rows, LANES), 1)
    columns[rows:, :] = jnp.zeros((columns.shape[0] - rows, LANES), jnp.float32)
    picked = jnp.where(lane == 0, stats[0], stats[1])
    picked = jnp.where(lane == 2, stats[2], picked)
    columns[:rows, :] = jnp.where(lane == 3, stats[3], picked)
    stat_ref[0] = jnp.transpose(columns[...])[:8]


def attention(
    places, lens, counts, queries, backs, received, chunk, first, patch_blocks, rows, slots, scale
):
    total_rows = patch_blocks * rows
    padded = pl.cdiv(rows, LANES) * LANES
    block_rows, width = received.shape[2:]
    wide = pl.BlockSpec((rows, 2 * LANES), lambda p, *_: (first + p, chunk))
    out = pl.BlockSpec((rows, 2 * LANES), lambda p, *_: (p, 0))
    tiles = (slots + 1) // 2
    return pl.pallas_call(
        functools.partial(attention_kernel, slots=slots, scale=scale, first=first),
        grid_spec=pltpu.PrefetchScalarGridSpec(
            num_scalar_prefetch=3,
            grid=(patch_blocks,),
            in_specs=[wide, wide, pl.BlockSpec(memory_space=pl.ANY)],
            out_specs=[out, out, pl.BlockSpec((1, 8, padded), lambda p, *_: (p, 0, 0))],
            scratch_shapes=[
                pltpu.VMEM((2, 2, tiles * 2 * block_rows, width), jnp.bfloat16),
                pltpu.VMEM((2, tiles, rows, 2 * block_rows), jnp.float32),
                pltpu.VMEM((2, tiles, rows, 2 * block_rows), jnp.bfloat16),
                pltpu.VMEM((2, rows, block_rows), jnp.float32),
                pltpu.VMEM((2, rows, width), jnp.float32),
                pltpu.VMEM((2, rows, block_rows), jnp.float32),
                pltpu.VMEM((2, rows, width), jnp.float32),
                pltpu.VMEM((padded, LANES), jnp.float32),
                pltpu.SemaphoreType.DMA((2, slots)),
            ],
        ),
        out_shape=[jax.ShapeDtypeStruct((total_rows, 2 * LANES), jnp.float32)] * 2
        + [jax.ShapeDtypeStruct((patch_blocks, 8, padded), jnp.float32)],
        compiler_params=pltpu.CompilerParams(vmem_limit_bytes=58 << 20),
        cost_estimate=pl.CostEstimate(
            flops=8 * total_rows * slots * block_rows * width,
            transcendentals=total_rows * slots * block_rows,
            bytes_accessed=40 << 20,
        ),
    )(places, lens, counts, queries, backs, received)


def merge_kernel(co_ref, ds_ref, mine_ref, theirs_ref, out_ref, *, scale, split):
    rows = co_ref.shape[0]
    mine, theirs = mine_ref[0], theirs_ref[0]
    kind = lax.broadcasted_iota(jnp.int32, mine.shape, 0)
    gap = mine - theirs
    share = 1.0 / (1.0 + jnp.exp(-gap))
    rest = 1.0 / (1.0 + jnp.exp(gap))
    rest_below = jnp.concatenate([rest[:1], rest[:-1]], axis=0)
    table = jnp.where(kind % 2 == 0, share, rest_below * gap * scale)
    tall = jnp.transpose(
        jnp.concatenate([table, jnp.zeros((LANES - 8, table.shape[1]), jnp.float32)], axis=0)
    )[:rows]
    lower = lax.broadcasted_iota(jnp.int32, (rows, LANES), 1) < split
    for head in range(2):
        lanes = pl.ds(head * LANES, LANES)
        weight = tall[:, 2 * head : 2 * head + 1]
        shift = tall[:, 2 * head + 1 : 2 * head + 2]
        outs = co_ref[:, lanes]
        value = weight * jnp.where(lower, ds_ref[:, lanes] + shift * outs, outs)
        out_ref[:, lanes] = value.astype(jnp.bfloat16)


def merge(outs, douts, mine, theirs, first, count, scale, split):
    patch_blocks, _, padded = mine.shape
    rows = outs.shape[0] // patch_blocks
    wide = pl.BlockSpec((rows, 2 * LANES), lambda p: (first + p, 0))
    flat = pl.BlockSpec((1, 8, padded), lambda p: (first + p, 0, 0))
    return pl.pallas_call(
        functools.partial(merge_kernel, scale=scale, split=split),
        grid=(count,),
        in_specs=[wide, wide, flat, flat],
        out_specs=pl.BlockSpec((rows, 2 * LANES), lambda p: (p, 0)),
        out_shape=jax.ShapeDtypeStruct((count * rows, 2 * LANES), jnp.bfloat16),
        cost_estimate=pl.CostEstimate(
            flops=20 * count * rows * LANES,
            transcendentals=0,
            bytes_accessed=20 * count * rows * LANES,
        ),
    )(outs, douts, mine, theirs)


def project_kernel(*refs, count, parts, last):
    step = pl.program_id(0)
    weights = refs[count * parts]
    rest = refs[count * parts + 1 :]
    before = rest[0] if len(rest) == (3 if last else 2) else None

    def part(pieces):
        value = jnp.dot(pieces[0][...], weights[0], preferred_element_type=jnp.float32)
        for i in range(1, count):
            value += jnp.dot(pieces[i][...], weights[i], preferred_element_type=jnp.float32)
        if before is not None:
            value += before[...]
        if last:
            width = rest[-1].shape[1]
            rest[-2][...] = value[:, :width].astype(jnp.bfloat16)
            rest[-1][...] = value[:, width:].astype(jnp.bfloat16)
        else:
            rest[-1][...] = value

    for i in range(parts):
        pl.when(step * parts // pl.num_programs(0) == i)(
            functools.partial(part, refs[i * count : (i + 1) * count])
        )


def project(parts, weights, before, last):
    count = len(parts[0])
    rows, depth = parts[0][0].shape
    total_rows = rows * len(parts)
    width = weights.shape[2]
    steps = 4 // len(parts)
    tile = rows // steps
    rowwise = lambda w: pl.BlockSpec((tile, w), lambda i: (i, 0))

    def within(which):
        return pl.BlockSpec(
            (tile, depth), lambda i: (jnp.clip(i - which * steps, 0, steps - 1), 0)
        )

    halves = jax.ShapeDtypeStruct((total_rows, width // 2), jnp.bfloat16)
    return pl.pallas_call(
        functools.partial(project_kernel, count=count, parts=len(parts), last=last),
        grid=(4,),
        in_specs=[within(i) for i in range(len(parts)) for _ in range(count)]
        + [pl.BlockSpec(weights.shape, lambda i: (0, 0, 0))]
        + ([] if before is None else [rowwise(width)]),
        out_specs=[rowwise(width // 2)] * 2 if last else rowwise(width),
        out_shape=[halves] * 2
        if last
        else jax.ShapeDtypeStruct((total_rows, width), jnp.float32),
        compiler_params=pltpu.CompilerParams(vmem_limit_bytes=40 << 20),
        cost_estimate=pl.CostEstimate(
            flops=2 * total_rows * depth * count * width,
            transcendentals=0,
            bytes_accessed=2 * total_rows * (depth * count + 2 * width),
        ),
    )(*[x for pieces in parts for x in pieces], weights, *([] if before is None else [before]))


def swap(x, axis):
    return lax.ppermute(x, axis, [(0, 1), (1, 0)])


def gather_half(x, zl_size, y_size, y_first):
    if zl_size == 2 and y_size == 2:
        by_y = swap(x, "y")
        by_zl = swap(x, "zl")
        corner = swap(by_y, "zl") if y_first else swap(by_zl, "y")
        return [x, by_y, by_zl, corner]
    whole = lax.all_gather(x, ("zl", "y"), axis=0, tiled=False)
    return [whole[i] for i in range(zl_size * y_size)]


def scatter_sum(x, size, dim):
    index = lax.axis_index("dp")
    step = size // 2
    while step >= 1:
        half = x.shape[dim] // 2
        upper = (index // step) % 2
        keep = lax.dynamic_slice_in_dim(x, upper * half, half, dim)
        give = lax.dynamic_slice_in_dim(x, (1 - upper) * half, half, dim)
        got = lax.ppermute(
            give.astype(jnp.bfloat16), "dp", [(i, i ^ step) for i in range(size)]
        )
        x = keep + got.astype(jnp.float32)
        step //= 2
    return x


def local(
    patches, query_proj, output_proj, cache, block_lengths, neighbours, cotangent, *, sizes
):
    groups, zl_size, y_size = sizes
    inner = zl_size * y_size
    model = 2 * inner
    owner_count = groups * model
    group = lax.axis_index("dp")
    zh = lax.axis_index("zh")
    spot = lax.axis_index("zl") * y_size + lax.axis_index("y")
    me = group * model + zh * inner + spot
    local_blocks, block_rows, heads, width = cache.shape
    head_size = width // 2
    local_heads = query_proj.shape[1] // head_size
    features = patches.shape[1]
    columns = features // model
    slots = neighbours.shape[1]
    patch_blocks = neighbours.shape[0] // groups
    entry_count = patch_blocks * slots
    capacity = 2 * entry_count // owner_count
    row_count = patches.shape[0]
    head_scale = 1.0 / math.sqrt(head_size)
    grad_scale = 1.0 / math.sqrt(row_count * groups)

    all_ids = neighbours.reshape(groups, entry_count)
    match = all_ids // local_blocks == me
    order = jnp.arange(entry_count, dtype=jnp.int32)
    earlier = order[None, :] < order[:, None]
    rank = jnp.sum((match[:, None, :] & earlier[None]).astype(jnp.int32), axis=2)
    slot_range = jnp.arange(capacity, dtype=jnp.int32)
    placed = match[:, :, None] & (rank[:, :, None] == slot_range)
    chosen = jnp.sum(
        jnp.where(placed, (all_ids % local_blocks)[:, :, None], 0), axis=1
    ).reshape(groups * capacity)
    send_counts = jnp.sum(match.astype(jnp.int32), axis=1)

    def pack(c):
        return pack_blocks(
            chosen, send_counts, cache, c, groups, inner, capacity, local_heads
        ).reshape(groups * inner, capacity * 2 * block_rows, width)

    def exchange(x):
        return lax.all_to_all(
            x, ("dp", "zl", "y"), split_axis=0, concat_axis=0, tiled=True
        ).reshape(groups * inner * capacity, 2, block_rows, width)

    cols = jnp.concatenate(
        [
            output_proj.reshape(local_heads * head_size, model, columns).transpose(1, 0, 2),
            query_proj.reshape(model, columns, local_heads * head_size).transpose(0, 2, 1),
        ],
        axis=2,
    )
    cols = lax.all_to_all(cols, ("zh", "zl", "y"), split_axis=0, concat_axis=0, tiled=True)

    every_length = lax.dynamic_update_slice_in_dim(
        jnp.zeros((owner_count * local_blocks,), jnp.int32), block_lengths, me * local_blocks, 0
    )
    for axis, size in (("y", y_size), ("zl", zl_size), ("dp", groups)):
        step = 1
        while step < size:
            every_length += lax.ppermute(
                every_length, axis, [(i, i ^ step) for i in range(size)]
            )
            step *= 2

    packed, cols, every_length = lax.optimization_barrier((pack(0), cols, every_length))
    received = [exchange(packed)]
    cols = cols.reshape(2, inner, local_heads, head_size, 2 * columns)


    my_ids = lax.dynamic_slice_in_dim(
        neighbours, group * patch_blocks, patch_blocks, 0
    ).reshape(entry_count)
    owners = my_ids // local_blocks
    slot_of = jnp.sum(((owners[:, None] == owners[None, :]) & earlier).astype(jnp.int32), axis=1)
    source = (owners // model) * inner + owners % inner
    in_half = ((owners % model) // inner == zh).reshape(patch_blocks, slots)
    arrival = (source * capacity + slot_of).reshape(patch_blocks, slots)
    entry_length = every_length[my_ids].reshape(patch_blocks, slots)
    spots = jnp.arange(slots, dtype=jnp.int32)
    before = jnp.sum(
        (in_half[:, None, :] & (spots[None, :] < spots[:, None])[None]).astype(jnp.int32), axis=2
    )
    at = in_half[:, :, None] & (before[:, :, None] == spots)
    places = jnp.sum(jnp.where(at, arrival[:, :, None], 0), axis=1).reshape(entry_count)
    lens = jnp.sum(jnp.where(at, entry_length[:, :, None], 0), axis=1).reshape(entry_count)
    counts = jnp.sum(in_half.astype(jnp.int32), axis=1)

    def both_halves(own):
        other = swap(own, "zh")
        return jnp.where(zh == 0, own, other), jnp.where(zh == 0, other, own)

    q_halves = [
        w.reshape(features, local_heads, head_size) for w in both_halves(query_proj)
    ]
    q_wide = jnp.stack(q_halves, axis=2)
    q_wide = jnp.pad(q_wide, ((0, 0), (0, 0), (0, 0), (0, LANES - head_size)))
    q_wide = q_wide.reshape(features, local_heads * 2 * LANES)
    o_halves = [
        w.reshape(local_heads, head_size, features) for w in both_halves(output_proj)
    ]
    o_wide = jnp.stack(o_halves, axis=1)
    o_wide = jnp.pad(o_wide, ((0, 0), (0, 0), (LANES - head_size, 0), (0, 0)))
    o_wide = o_wide.reshape(local_heads * 2 * LANES, features)
    queries = (
        jnp.dot(patches, q_wide, preferred_element_type=jnp.float32) * head_scale
    ).astype(jnp.bfloat16)
    backs = nt_dot(cotangent, o_wide).astype(jnp.bfloat16)

    right = jnp.arange(2 * columns)[None, None, None, :] >= columns
    if zl_size == 2 and y_size == 2:
        order = jnp.stack([spot, spot ^ 1, spot ^ 2, spot ^ 3])
    else:
        order = jnp.arange(inner, dtype=jnp.int32)

    def tail_weights(c):
        both = jnp.moveaxis(cols[:, :, c], 0, 1)
        pair = [jnp.where(right, both, 0), jnp.where(right, 0, both)]
        return jnp.stack(pair, axis=2).reshape(inner, 2 * LANES, 2 * columns)[order]

    finals = [tail_weights(c) for c in range(local_heads)]

    places, lens, counts, queries, backs, finals, cache = lax.optimization_barrier(
        (places, lens, counts, queries, backs, finals, cache)
    )
    for c in range(1, local_heads):
        received.append(exchange(pack(c)))


    rows = row_count // patch_blocks
    part_count = 2 if patch_blocks % 2 == 0 else 1
    part_patches = patch_blocks // part_count
    result = None
    own = []
    for c in range(local_heads):
        final = c + 1 == local_heads
        calls = part_count if final else 1
        call_patches = patch_blocks // calls
        sums = []
        for call in range(calls):
            outs, douts, mine = attention(
                places, lens, counts, queries, backs, received[c], c,
                call * call_patches, call_patches, rows, slots, head_scale,
            )
            theirs = swap(mine, "zh")
            for start in range(0, call_patches, part_patches):
                part = merge(
                    outs, douts, mine, theirs, start, part_patches, head_scale, head_size
                )
                sums.append((part, swap(part, "zh")))
            if call + 1 < calls:
                part, places = lax.optimization_barrier((part, places))
        if not final:
            part, places = lax.optimization_barrier((part, places))
        merged = [
            (part.astype(jnp.float32) + other.astype(jnp.float32)).astype(jnp.bfloat16)
            for part, other in sums
        ]
        pieces = [
            gather_half(x, zl_size, y_size, i % 2 == 0) for i, x in enumerate(merged)
        ]
        result = project(pieces, finals[c], result, final)
        own.append(
            jnp.concatenate(
                [lax.dynamic_slice_in_dim(x, zh * LANES, LANES, 1) for x in merged], axis=0
            )
        )
    attended, patch_grad = result

    dquery = jnp.concatenate([x[:, :head_size] for x in own], axis=1)
    heads_out = jnp.concatenate([x[:, head_size:] for x in own], axis=1)
    query_term = (
        lax.dot_general(
            patches, dquery, (((0,), (0,)), ((), ())), preferred_element_type=jnp.float32
        )
        * grad_scale
    )
    output_term = (
        lax.dot_general(
            heads_out, cotangent, (((0,), (0,)), ((), ())), preferred_element_type=jnp.float32
        )
        * grad_scale
    )
    return (
        attended,
        patch_grad,
        scatter_sum(query_term, groups, 0),
        scatter_sum(output_term, groups, 1),
    )


def solution(mesh):
    groups, model = mesh.shape["dp"], mesh.shape["mp"]
    sizes = (groups, model // 4, 2)
    split = Mesh(
        mesh.devices.reshape(groups, 2, model // 4, 2), ("dp", "zh", "zl", "y")
    )
    mp = ("zh", "zl", "y")
    every = ("dp",) + mp
    return jax.shard_map(
        functools.partial(local, sizes=sizes),
        mesh=split,
        in_specs=(
            P("dp", None),
            P(None, mp),
            P(mp, None),
            P(every, None, None, None),
            P(every),
            P(),
            P("dp", None),
        ),
        out_specs=(P("dp", mp), P("dp", mp), P("dp", mp), P(mp, "dp")),
        check_vma=False,
    )
```

```python
import functools
import math

import jax
import jax.numpy as jnp
from jax import lax
from jax.experimental import pallas as pl
from jax.experimental.pallas import tpu as pltpu
from jax.sharding import Mesh
from jax.sharding import PartitionSpec as P

masked_value = -1e30
LANES = 128
MARK_ROWS = 16
MARK_BASE = 100.0
MARK_LEAST = 64.0


def pack_kernel(
    chosen, counts, lengths, cache_ref, out_ref, *, chunk, local_heads, inner, capacity
):
    slot = pl.program_id(0) * capacity + pl.program_id(1)

    @pl.when(pl.program_id(1) < counts[pl.program_id(0)])
    def _():
        by_head = pltpu.einshape("rhd->hrd", cache_ref[0])
        block_rows, width = by_head.shape[1:]
        valid = lengths[chosen[slot]]
        shape = (MARK_ROWS, width)
        corner = (lax.broadcasted_iota(jnp.int32, shape, 0) == MARK_ROWS - 1) & (
            lax.broadcasted_iota(jnp.int32, shape, 1) == 0
        )
        corner = corner & (valid < block_rows)
        mark = valid.astype(jnp.float32) + MARK_BASE
        for r in range(inner):
            for half in range(2):
                tile = by_head[(half * inner + r) * local_heads + chunk]
                out_ref[0, r, 0, half] = tile
                last = tile[block_rows - MARK_ROWS :].astype(jnp.float32)
                out_ref[0, r, 0, half, block_rows - MARK_ROWS :, :] = jnp.where(
                    corner, mark, last
                ).astype(jnp.bfloat16)


def pack_blocks(chosen, counts, lengths, cache, chunk, groups, inner, capacity, local_heads):
    _, block_rows, heads, width = cache.shape
    return pl.pallas_call(
        functools.partial(
            pack_kernel, chunk=chunk, local_heads=local_heads, inner=inner, capacity=capacity
        ),
        grid_spec=pltpu.PrefetchScalarGridSpec(
            num_scalar_prefetch=3,
            grid=(groups, capacity),
            in_specs=[
                pl.BlockSpec(
                    (1, block_rows, heads, width),
                    lambda g, s, ch, ct, ln: (ch[g * capacity + s], 0, 0, 0),
                )
            ],
            out_specs=pl.BlockSpec(
                (1, inner, 1, 2, block_rows, width),
                lambda g, s, ch, ct, ln: (g, 0, s, 0, 0, 0),
            ),
        ),
        out_shape=jax.ShapeDtypeStruct(
            (groups, inner, capacity, 2, block_rows, width), cache.dtype
        ),
        compiler_params=pltpu.CompilerParams(vmem_limit_bytes=32 << 20),
        cost_estimate=pl.CostEstimate(
            flops=0, transcendentals=0, bytes_accessed=groups * capacity * 2 * 262144
        ),
    )(chosen, counts, lengths, cache)


def nt_dot(left, right):
    return lax.dot_general(
        left, right, (((1,), (1,)), ((), ())), preferred_element_type=jnp.float32
    )


def attention_kernel(
    places, counts, q_ref, b_ref, recv_ref, co_ref, ds_ref, stat_ref,
    kv, scores, probs, top, acc, total, dacc, columns, bias, sems, *, slots, scale, first,
):
    patch = first + pl.program_id(0)
    patches = first + pl.num_programs(0)
    block_rows = recv_ref.shape[2]
    pair = 2 * block_rows

    def copy(which, j, place):
        return pltpu.make_async_copy(
            recv_ref.at[place],
            kv.at[which % 2, :, pl.ds(pl.multiple_of(j * block_rows, block_rows), block_rows), :],
            sems.at[which % 2, j],
        )

    def start(which):
        @pl.loop(0, counts[which])
        def _(j):
            copy(which, j, places[which * slots + j]).start()

    @pl.when(patch == first)
    def _():
        start(patch)

    @pl.when(patch + 1 < patches)
    def _():
        start(patch + 1)

    here = counts[patch]
    tiles = jnp.maximum((here + 1) // 2, 1)

    @pl.loop(here, 2 * tiles)
    def _(j):
        kv[patch % 2, :, pl.ds(pl.multiple_of(j * block_rows, block_rows), block_rows), :] = (
            jnp.zeros((2, block_rows, kv.shape[3]), kv.dtype)
        )
        bias[pl.ds(j, 1), :] = jnp.full((1, block_rows), masked_value, jnp.float32)

    lane = lax.broadcasted_iota(jnp.int32, (1, block_rows), 1)

    @pl.loop(0, here)
    def _(j):
        copy(patch, j, 0).wait()
        end = pl.multiple_of(j * block_rows + block_rows - MARK_ROWS, MARK_ROWS)
        last = kv[patch % 2, 0, pl.ds(end, MARK_ROWS), :].astype(jnp.float32)[MARK_ROWS - 1 :]
        mark = jnp.sum(jnp.where(lane == 0, last, 0.0), axis=1, keepdims=True)
        valid = jnp.where(mark > MARK_LEAST, mark - MARK_BASE, float(block_rows))
        bias[pl.ds(j, 1), :] = jnp.where(lane.astype(jnp.float32) < valid, 0.0, masked_value)

    def key_tile(t, head):
        return kv[patch % 2, head, pl.ds(pl.multiple_of(t * pair, pair), pair), :]

    rows = q_ref.shape[0]
    lanes = [pl.ds(head * LANES, LANES) for head in range(2)]
    top[...] = jnp.full_like(top, masked_value)
    acc[...] = jnp.zeros_like(acc)
    total[...] = jnp.zeros_like(total)
    dacc[...] = jnp.zeros_like(dacc)

    @pl.loop(0, tiles)
    def _(t):
        bias_lo = bias[pl.ds(2 * t, 1), :]
        bias_hi = bias[pl.ds(2 * t + 1, 1), :]
        for head in range(2):
            score = nt_dot(q_ref[:, lanes[head]], key_tile(t, head))
            low = score[:, :block_rows] + bias_lo
            high = score[:, block_rows:] + bias_hi
            scores[head, t, :, :block_rows] = low
            scores[head, t, :, block_rows:] = high
            top[head] = jnp.maximum(top[head], jnp.maximum(low, high))

    row_max = [jnp.max(top[head], axis=1, keepdims=True) for head in range(2)]

    @pl.loop(0, tiles)
    def _(t):
        for head in range(2):
            weights = jnp.exp(scores[head, t] - row_max[head]).astype(jnp.bfloat16)
            probs[head, t] = weights
            wide = weights.astype(jnp.float32)
            total[head] += wide[:, :block_rows] + wide[:, block_rows:]
            acc[head] += jnp.dot(weights, key_tile(t, head), preferred_element_type=jnp.float32)

    inverse, inner, stats = [], [], []
    for head in range(2):
        row_sum = jnp.sum(total[head], axis=1, keepdims=True)
        inverse.append(1.0 / row_sum)
        outs = acc[head] * inverse[head]
        co_ref[:, lanes[head]] = outs
        inner.append(
            jnp.sum(outs * b_ref[:, lanes[head]].astype(jnp.float32), axis=1, keepdims=True)
        )
        stats += [row_max[head] + jnp.log(row_sum), inner[head]]

    @pl.loop(0, tiles)
    def _(t):
        for head in range(2):
            dprobs = nt_dot(b_ref[:, lanes[head]], key_tile(t, head))
            dscores = (probs[head, t].astype(jnp.float32) * (dprobs - inner[head])).astype(
                jnp.bfloat16
            )
            dacc[head] += jnp.dot(dscores, key_tile(t, head), preferred_element_type=jnp.float32)

    for head in range(2):
        ds_ref[:, lanes[head]] = dacc[head] * (inverse[head] * scale)
    lane = lax.broadcasted_iota(jnp.int32, (rows, LANES), 1)
    columns[rows:, :] = jnp.zeros((columns.shape[0] - rows, LANES), jnp.float32)
    picked = jnp.where(lane == 0, stats[0], stats[1])
    picked = jnp.where(lane == 2, stats[2], picked)
    columns[:rows, :] = jnp.where(lane == 3, stats[3], picked)
    stat_ref[0] = jnp.transpose(columns[...])[:8]


def attention(
    places, counts, queries, backs, received, chunk, first, patch_blocks, rows, slots, scale
):
    total_rows = patch_blocks * rows
    padded = pl.cdiv(rows, LANES) * LANES
    block_rows, width = received.shape[2:]
    wide = pl.BlockSpec((rows, 2 * LANES), lambda p, *_: (first + p, chunk))
    out = pl.BlockSpec((rows, 2 * LANES), lambda p, *_: (p, 0))
    tiles = (slots + 1) // 2
    return pl.pallas_call(
        functools.partial(attention_kernel, slots=slots, scale=scale, first=first),
        grid_spec=pltpu.PrefetchScalarGridSpec(
            num_scalar_prefetch=2,
            grid=(patch_blocks,),
            in_specs=[wide, wide, pl.BlockSpec(memory_space=pl.ANY)],
            out_specs=[out, out, pl.BlockSpec((1, 8, padded), lambda p, *_: (p, 0, 0))],
            scratch_shapes=[
                pltpu.VMEM((2, 2, tiles * 2 * block_rows, width), jnp.bfloat16),
                pltpu.VMEM((2, tiles, rows, 2 * block_rows), jnp.float32),
                pltpu.VMEM((2, tiles, rows, 2 * block_rows), jnp.bfloat16),
                pltpu.VMEM((2, rows, block_rows), jnp.float32),
                pltpu.VMEM((2, rows, width), jnp.float32),
                pltpu.VMEM((2, rows, block_rows), jnp.float32),
                pltpu.VMEM((2, rows, width), jnp.float32),
                pltpu.VMEM((padded, LANES), jnp.float32),
                pltpu.VMEM((2 * tiles, block_rows), jnp.float32),
                pltpu.SemaphoreType.DMA((2, slots)),
            ],
        ),
        out_shape=[jax.ShapeDtypeStruct((total_rows, 2 * LANES), jnp.float32)] * 2
        + [jax.ShapeDtypeStruct((patch_blocks, 8, padded), jnp.float32)],
        compiler_params=pltpu.CompilerParams(vmem_limit_bytes=58 << 20),
        cost_estimate=pl.CostEstimate(
            flops=8 * total_rows * slots * block_rows * width,
            transcendentals=total_rows * slots * block_rows,
            bytes_accessed=40 << 20,
        ),
    )(places, counts, queries, backs, received)


def merge_kernel(co_ref, ds_ref, mine_ref, theirs_ref, out_ref, *, scale, split):
    rows = co_ref.shape[0]
    mine, theirs = mine_ref[0], theirs_ref[0]
    kind = lax.broadcasted_iota(jnp.int32, mine.shape, 0)
    gap = mine - theirs
    share = 1.0 / (1.0 + jnp.exp(-gap))
    rest = 1.0 / (1.0 + jnp.exp(gap))
    rest_below = jnp.concatenate([rest[:1], rest[:-1]], axis=0)
    table = jnp.where(kind % 2 == 0, share, rest_below * gap * scale)
    tall = jnp.transpose(
        jnp.concatenate([table, jnp.zeros((LANES - 8, table.shape[1]), jnp.float32)], axis=0)
    )[:rows]
    lower = lax.broadcasted_iota(jnp.int32, (rows, LANES), 1) < split
    for head in range(2):
        lanes = pl.ds(head * LANES, LANES)
        weight = tall[:, 2 * head : 2 * head + 1]
        shift = tall[:, 2 * head + 1 : 2 * head + 2]
        outs = co_ref[:, lanes]
        value = weight * jnp.where(lower, ds_ref[:, lanes] + shift * outs, outs)
        out_ref[:, lanes] = value.astype(jnp.bfloat16)


def merge(outs, douts, mine, theirs, first, count, scale, split):
    patch_blocks, _, padded = mine.shape
    rows = outs.shape[0] // patch_blocks
    wide = pl.BlockSpec((rows, 2 * LANES), lambda p: (first + p, 0))
    flat = pl.BlockSpec((1, 8, padded), lambda p: (first + p, 0, 0))
    return pl.pallas_call(
        functools.partial(merge_kernel, scale=scale, split=split),
        grid=(count,),
        in_specs=[wide, wide, flat, flat],
        out_specs=pl.BlockSpec((rows, 2 * LANES), lambda p: (p, 0)),
        out_shape=jax.ShapeDtypeStruct((count * rows, 2 * LANES), jnp.bfloat16),
        cost_estimate=pl.CostEstimate(
            flops=20 * count * rows * LANES,
            transcendentals=0,
            bytes_accessed=20 * count * rows * LANES,
        ),
    )(outs, douts, mine, theirs)


def project_kernel(order, *refs, count, parts, last, chunk, depth):
    step = pl.program_id(0)
    cols = refs[count * parts]
    rest, weights = refs[count * parts + 1 : -1], refs[-1]
    before = rest[0] if len(rest) == (3 if last else 2) else None
    half = cols.shape[2] // 2

    @pl.when(step == 0)
    def _():
        empty = jnp.zeros((depth, half), weights.dtype)
        for i in range(count):
            for z in range(2):
                own = cols[z * count + order[i], pl.ds(chunk * depth, depth), :]
                grad_rows = pl.ds(2 * z * depth, depth)
                out_rows = pl.ds((2 * z + 1) * depth, depth)
                weights[i, grad_rows, :half] = empty
                weights[i, grad_rows, half:] = own[:, half:]
                weights[i, out_rows, :half] = own[:, :half]
                weights[i, out_rows, half:] = empty

    def part(pieces):
        value = jnp.dot(pieces[0][...], weights[0], preferred_element_type=jnp.float32)
        for i in range(1, count):
            value += jnp.dot(pieces[i][...], weights[i], preferred_element_type=jnp.float32)
        if before is not None:
            value += before[...]
        if last:
            rest[-2][...] = value[:, :half].astype(jnp.bfloat16)
            rest[-1][...] = value[:, half:].astype(jnp.bfloat16)
        else:
            rest[-1][...] = value

    for i in range(parts):
        pl.when(step * parts // pl.num_programs(0) == i)(
            functools.partial(part, refs[i * count : (i + 1) * count])
        )


def project(parts, cols, order, before, last, chunk):
    count = len(parts[0])
    rows, depth = parts[0][0].shape
    total_rows = rows * len(parts)
    width = cols.shape[2]
    steps = 4 // len(parts)
    tile = rows // steps
    rowwise = lambda w: pl.BlockSpec((tile, w), lambda i, *_: (i, 0))

    def within(which):
        return pl.BlockSpec(
            (tile, depth), lambda i, *_: (jnp.clip(i - which * steps, 0, steps - 1), 0)
        )

    halves = jax.ShapeDtypeStruct((total_rows, width // 2), jnp.bfloat16)
    return pl.pallas_call(
        functools.partial(
            project_kernel, count=count, parts=len(parts), last=last, chunk=chunk,
            depth=depth // 4,
        ),
        grid_spec=pltpu.PrefetchScalarGridSpec(
            num_scalar_prefetch=1,
            grid=(4,),
            in_specs=[within(i) for i in range(len(parts)) for _ in range(count)]
            + [pl.BlockSpec(cols.shape, lambda i, *_: (0, 0, 0))]
            + ([] if before is None else [rowwise(width)]),
            out_specs=[rowwise(width // 2)] * 2 if last else rowwise(width),
            scratch_shapes=[pltpu.VMEM((count, depth, width), jnp.bfloat16)],
        ),
        out_shape=[halves] * 2
        if last
        else jax.ShapeDtypeStruct((total_rows, width), jnp.float32),
        compiler_params=pltpu.CompilerParams(vmem_limit_bytes=40 << 20),
        cost_estimate=pl.CostEstimate(
            flops=2 * total_rows * depth * count * width,
            transcendentals=0,
            bytes_accessed=2 * total_rows * (depth * count + 2 * width),
        ),
    )(
        order, *[x for pieces in parts for x in pieces], cols,
        *([] if before is None else [before]),
    )


def swap(x, axis):
    return lax.ppermute(x, axis, [(0, 1), (1, 0)])


def gather_half(x, zl_size, y_size, y_first):
    if zl_size == 2 and y_size == 2:
        by_y = swap(x, "y")
        by_zl = swap(x, "zl")
        corner = swap(by_y, "zl") if y_first else swap(by_zl, "y")
        return [x, by_y, by_zl, corner]
    whole = lax.all_gather(x, ("zl", "y"), axis=0, tiled=False)
    return [whole[i] for i in range(zl_size * y_size)]


def scatter_sum(x, size, dim):
    index = lax.axis_index("dp")
    step = size // 2
    while step >= 1:
        half = x.shape[dim] // 2
        upper = (index // step) % 2
        keep = lax.dynamic_slice_in_dim(x, upper * half, half, dim)
        give = lax.dynamic_slice_in_dim(x, (1 - upper) * half, half, dim)
        got = lax.ppermute(
            give.astype(jnp.bfloat16), "dp", [(i, i ^ step) for i in range(size)]
        )
        x = keep + got.astype(jnp.float32)
        step //= 2
    return x


def local(
    patches, query_proj, output_proj, cache, block_lengths, neighbours, cotangent, *, sizes
):
    groups, zl_size, y_size = sizes
    inner = zl_size * y_size
    model = 2 * inner
    owner_count = groups * model
    group = lax.axis_index("dp")
    zh = lax.axis_index("zh")
    spot = lax.axis_index("zl") * y_size + lax.axis_index("y")
    me = group * model + zh * inner + spot
    local_blocks, block_rows, heads, width = cache.shape
    head_size = width // 2
    local_heads = query_proj.shape[1] // head_size
    features = patches.shape[1]
    columns = features // model
    slots = neighbours.shape[1]
    patch_blocks = neighbours.shape[0] // groups
    entry_count = patch_blocks * slots
    capacity = 2 * entry_count // owner_count
    row_count = patches.shape[0]
    head_scale = 1.0 / math.sqrt(head_size)
    grad_scale = 1.0 / math.sqrt(row_count * groups)

    all_ids = neighbours.reshape(groups, entry_count)
    match = all_ids // local_blocks == me
    order = jnp.arange(entry_count, dtype=jnp.int32)
    earlier = order[None, :] < order[:, None]
    rank = jnp.sum((match[:, None, :] & earlier[None]).astype(jnp.int32), axis=2)
    slot_range = jnp.arange(capacity, dtype=jnp.int32)
    placed = match[:, :, None] & (rank[:, :, None] == slot_range)
    chosen = jnp.sum(
        jnp.where(placed, (all_ids % local_blocks)[:, :, None], 0), axis=1
    ).reshape(groups * capacity)
    send_counts = jnp.sum(match.astype(jnp.int32), axis=1)

    def pack(c):
        return pack_blocks(
            chosen, send_counts, block_lengths, cache, c, groups, inner, capacity, local_heads
        ).reshape(groups * inner, capacity * 2 * block_rows, width)

    def exchange(x):
        return lax.all_to_all(
            x, ("dp", "zl", "y"), split_axis=0, concat_axis=0, tiled=True
        ).reshape(groups * inner * capacity, 2, block_rows, width)

    received = [exchange(pack(0))]
    q_other, o_other = swap(query_proj, "zh"), swap(output_proj, "zh")
    for c in range(1, local_heads):
        packed, q_other, o_other = lax.optimization_barrier((pack(c), q_other, o_other))
        received.append(exchange(packed))

    my_ids = lax.dynamic_slice_in_dim(
        neighbours, group * patch_blocks, patch_blocks, 0
    ).reshape(entry_count)
    owners = my_ids // local_blocks
    slot_of = jnp.sum(((owners[:, None] == owners[None, :]) & earlier).astype(jnp.int32), axis=1)
    source = (owners // model) * inner + owners % inner
    in_half = ((owners % model) // inner == zh).reshape(patch_blocks, slots)
    arrival = (source * capacity + slot_of).reshape(patch_blocks, slots)
    spots = jnp.arange(slots, dtype=jnp.int32)
    before = jnp.sum(
        (in_half[:, None, :] & (spots[None, :] < spots[:, None])[None]).astype(jnp.int32), axis=2
    )
    at = in_half[:, :, None] & (before[:, :, None] == spots)
    places = jnp.sum(jnp.where(at, arrival[:, :, None], 0), axis=1).reshape(entry_count)
    counts = jnp.sum(in_half.astype(jnp.int32), axis=1)

    q_other, o_other, received[0] = lax.optimization_barrier(
        (q_other, o_other, received[0])
    )

    def both_halves(own, other):
        return jnp.where(zh == 0, own, other), jnp.where(zh == 0, other, own)

    q_halves = [
        w.reshape(features, local_heads, head_size) for w in both_halves(query_proj, q_other)
    ]
    q_wide = jnp.stack(q_halves, axis=2)
    q_wide = jnp.pad(q_wide, ((0, 0), (0, 0), (0, 0), (0, LANES - head_size)))
    q_wide = q_wide.reshape(features, local_heads * 2 * LANES)
    o_halves = [
        w.reshape(local_heads, head_size, features) for w in both_halves(output_proj, o_other)
    ]
    o_wide = jnp.stack(o_halves, axis=1)
    o_wide = jnp.pad(o_wide, ((0, 0), (0, 0), (LANES - head_size, 0), (0, 0)))
    o_wide = o_wide.reshape(local_heads * 2 * LANES, features)
    queries = (
        jnp.dot(patches, q_wide, preferred_element_type=jnp.float32) * head_scale
    ).astype(jnp.bfloat16)
    backs = nt_dot(cotangent, o_wide).astype(jnp.bfloat16)

    cols = jnp.concatenate(
        [
            output_proj.reshape(local_heads * head_size, model, columns).transpose(1, 0, 2),
            query_proj.reshape(model, columns, local_heads * head_size).transpose(0, 2, 1),
        ],
        axis=2,
    )
    if zl_size == 2 and y_size == 2:
        order = jnp.stack([spot, spot ^ 1, spot ^ 2, spot ^ 3])
    else:
        order = jnp.arange(inner, dtype=jnp.int32)

    rows = row_count // patch_blocks
    part_count = 2 if patch_blocks % 2 == 0 else 1
    part_patches = patch_blocks // part_count
    gathered = []
    own = []
    for c in range(local_heads):
        final = c + 1 == local_heads
        if final:
            cols, places, received[c] = lax.optimization_barrier((cols, places, received[c]))
            cols = lax.all_to_all(cols, ("zh", "zl", "y"), split_axis=0, concat_axis=0, tiled=True)
        outs, douts, mine = attention(
            places, counts, queries, backs, received[c], c, 0, patch_blocks, rows, slots, head_scale
        )
        theirs = swap(mine, "zh")
        if final:
            theirs, cols = lax.optimization_barrier((theirs, cols))
        parts = [
            merge(outs, douts, mine, theirs, start, part_patches, head_scale, head_size)
            for start in range(0, patch_blocks, part_patches)
        ]
        if not final:
            parts, places = lax.optimization_barrier((parts, places))
        merged = [
            (part.astype(jnp.float32) + swap(part, "zh").astype(jnp.float32)).astype(jnp.bfloat16)
            for part in parts
        ]
        pieces = [
            gather_half(x, zl_size, y_size, i % 2 == 0) for i, x in enumerate(merged)
        ]
        gathered.append(pieces)
        if final:
            merged, pieces[0][1] = lax.optimization_barrier((merged, pieces[0][1]))
        own.append(
            jnp.concatenate(
                [lax.dynamic_slice_in_dim(x, zh * LANES, LANES, 1) for x in merged], axis=0
            )
        )
    result = None
    for c, pieces in enumerate(gathered):
        result = project(pieces, cols, order, result, c + 1 == local_heads, c)
    attended, patch_grad = result

    dquery = jnp.concatenate([x[:, :head_size] for x in own], axis=1)
    heads_out = jnp.concatenate([x[:, head_size:] for x in own], axis=1)
    query_term = (
        lax.dot_general(
            patches, dquery, (((0,), (0,)), ((), ())), preferred_element_type=jnp.float32
        )
        * grad_scale
    )
    output_term = (
        lax.dot_general(
            heads_out, cotangent, (((0,), (0,)), ((), ())), preferred_element_type=jnp.float32
        )
        * grad_scale
    )
    return (
        attended,
        patch_grad,
        scatter_sum(query_term, groups, 0),
        scatter_sum(output_term, groups, 1),
    )


def solution(mesh):
    groups, model = mesh.shape["dp"], mesh.shape["mp"]
    sizes = (groups, model // 4, 2)
    split = Mesh(
        mesh.devices.reshape(groups, 2, model // 4, 2), ("dp", "zh", "zl", "y")
    )
    mp = ("zh", "zl", "y")
    every = ("dp",) + mp
    return jax.shard_map(
        functools.partial(local, sizes=sizes),
        mesh=split,
        in_specs=(
            P("dp", None),
            P(None, mp),
            P(mp, None),
            P(every, None, None, None),
            P(every),
            P(),
            P("dp", None),
        ),
        out_specs=(P("dp", mp), P("dp", mp), P("dp", mp), P(mp, "dp")),
        check_vma=False,
    )
```

```python
import functools
import math

import jax
import jax.numpy as jnp
from jax import lax
from jax.experimental import pallas as pl
from jax.experimental.pallas import tpu as pltpu
from jax.sharding import Mesh
from jax.sharding import PartitionSpec as P

masked_value = -1e30
LANES = 128
MARK_ROWS = 16
MARK_BASE = 100.0
MARK_LEAST = 64.0
GRANULE = 32
KEY_TILE = 512


def pack_kernel(
    chosen, counts, lengths, cache_ref, out_ref, *, chunk, local_heads, inner, capacity
):
    slot = pl.program_id(0) * capacity + pl.program_id(1)

    @pl.when(pl.program_id(1) < counts[pl.program_id(0)])
    def _():
        by_head = pltpu.einshape("rhd->hrd", cache_ref[0])
        block_rows, width = by_head.shape[1:]
        valid = lengths[chosen[slot]]
        shape = (MARK_ROWS, width)
        corner = (lax.broadcasted_iota(jnp.int32, shape, 0) == MARK_ROWS - 1) & (
            lax.broadcasted_iota(jnp.int32, shape, 1) == 0
        )
        corner = corner & (valid < block_rows)
        mark = valid.astype(jnp.float32) + MARK_BASE
        for r in range(inner):
            for half in range(2):
                tile = by_head[(half * inner + r) * local_heads + chunk]
                out_ref[0, r, 0, half] = tile
                last = tile[block_rows - MARK_ROWS :].astype(jnp.float32)
                out_ref[0, r, 0, half, block_rows - MARK_ROWS :, :] = jnp.where(
                    corner, mark, last
                ).astype(jnp.bfloat16)


def pack_blocks(chosen, counts, lengths, cache, chunk, groups, inner, capacity, local_heads):
    _, block_rows, heads, width = cache.shape
    return pl.pallas_call(
        functools.partial(
            pack_kernel, chunk=chunk, local_heads=local_heads, inner=inner, capacity=capacity
        ),
        grid_spec=pltpu.PrefetchScalarGridSpec(
            num_scalar_prefetch=3,
            grid=(groups, capacity),
            in_specs=[
                pl.BlockSpec(
                    (1, block_rows, heads, width),
                    lambda g, s, ch, ct, ln: (ch[g * capacity + s], 0, 0, 0),
                )
            ],
            out_specs=pl.BlockSpec(
                (1, inner, 1, 2, block_rows, width),
                lambda g, s, ch, ct, ln: (g, 0, s, 0, 0, 0),
            ),
        ),
        out_shape=jax.ShapeDtypeStruct(
            (groups, inner, capacity, 2, block_rows, width), cache.dtype
        ),
        compiler_params=pltpu.CompilerParams(vmem_limit_bytes=32 << 20),
        cost_estimate=pl.CostEstimate(
            flops=0, transcendentals=0, bytes_accessed=groups * capacity * 2 * 262144
        ),
    )(chosen, counts, lengths, cache)


def nt_dot(left, right):
    return lax.dot_general(
        left, right, (((1,), (1,)), ((), ())), preferred_element_type=jnp.float32
    )


def attention_kernel(
    places, counts, offsets, sizes, q_ref, b_ref, bias_ref, recv_ref, co_ref, ds_ref, stat_ref,
    kv, scores, probs, top, acc, dacc, columns, sems, *, slots, scale,
):
    patch = pl.program_id(0)
    block_rows, width = recv_ref.shape[2:]
    steps = block_rows // GRANULE
    folds = KEY_TILE // LANES

    def each_copy(which, act):
        @pl.loop(0, counts[which])
        def _(j):
            entry = which * slots + j
            at = pl.multiple_of(offsets[entry] * GRANULE, GRANULE)
            for size in range(1, steps + 1):

                @pl.when(sizes[entry] == size)
                def _():
                    act(
                        pltpu.make_async_copy(
                            recv_ref.at[places[entry], :, pl.ds(0, size * GRANULE), :],
                            kv.at[which % 2, :, pl.ds(at, size * GRANULE), :],
                            sems.at[which % 2, j],
                        )
                    )

    @pl.when(patch == 0)
    def _():
        each_copy(patch, lambda copy: copy.start())

    @pl.when(patch + 1 < pl.num_programs(0))
    def _():
        each_copy(patch + 1, lambda copy: copy.start())

    filled = offsets[patch * slots + slots - 1] + sizes[patch * slots + slots - 1]
    per_tile = KEY_TILE // GRANULE
    tiles = jnp.maximum((filled + per_tile - 1) // per_tile, 1)

    @pl.loop(filled, tiles * per_tile)
    def _(g):
        kv[patch % 2, :, pl.ds(pl.multiple_of(g * GRANULE, GRANULE), GRANULE), :] = jnp.zeros(
            (2, GRANULE, width), kv.dtype
        )

    each_copy(patch, lambda copy: copy.wait())

    def key_tile(t, head):
        return kv[patch % 2, head, pl.ds(pl.multiple_of(t * KEY_TILE, KEY_TILE), KEY_TILE), :]

    rows = q_ref.shape[0]
    lanes = [pl.ds(head * LANES, LANES) for head in range(2)]
    top[...] = jnp.full_like(top, masked_value)
    acc[...] = jnp.zeros_like(acc)
    dacc[...] = jnp.zeros_like(dacc)

    @pl.loop(0, tiles)
    def _(t):
        for head in range(2):
            score = nt_dot(q_ref[:, lanes[head]], key_tile(t, head))
            best = top[head]
            for fold in range(folds):
                part = score[:, fold * LANES : (fold + 1) * LANES]
                part = part + bias_ref[0, pl.ds(t * folds + fold, 1), :]
                scores[head, t, :, fold * LANES : (fold + 1) * LANES] = part
                best = jnp.maximum(best, part)
            top[head] = best

    row_max = [jnp.max(top[head], axis=1, keepdims=True) for head in range(2)]
    ones = jnp.ones((KEY_TILE, LANES), jnp.bfloat16)

    @pl.loop(0, tiles)
    def _(t):
        for head in range(2):
            weights = jnp.exp(scores[head, t] - row_max[head]).astype(jnp.bfloat16)
            probs[head, t] = weights
            acc[head] += jnp.dot(
                weights,
                jnp.concatenate([key_tile(t, head), ones], axis=1),
                preferred_element_type=jnp.float32,
            )

    inverse, inner, stats = [], [], []
    for head in range(2):
        row_sum = acc[head, :, width : width + 1]
        inverse.append(1.0 / row_sum)
        outs = acc[head, :, :width] * inverse[head]
        co_ref[:, lanes[head]] = outs
        inner.append(
            jnp.sum(outs * b_ref[:, lanes[head]].astype(jnp.float32), axis=1, keepdims=True)
        )
        stats += [row_max[head] + jnp.log(row_sum), inner[head]]

    @pl.loop(0, tiles)
    def _(t):
        for head in range(2):
            dprobs = nt_dot(b_ref[:, lanes[head]], key_tile(t, head))
            dscores = (probs[head, t].astype(jnp.float32) * (dprobs - inner[head])).astype(
                jnp.bfloat16
            )
            dacc[head] += jnp.dot(dscores, key_tile(t, head), preferred_element_type=jnp.float32)

    for head in range(2):
        ds_ref[:, lanes[head]] = dacc[head] * (inverse[head] * scale)
    lane = lax.broadcasted_iota(jnp.int32, (rows, LANES), 1)
    columns[rows:, :] = jnp.zeros((columns.shape[0] - rows, LANES), jnp.float32)
    picked = jnp.where(lane == 0, stats[0], stats[1])
    picked = jnp.where(lane == 2, stats[2], picked)
    columns[:rows, :] = jnp.where(lane == 3, stats[3], picked)
    stat_ref[0] = jnp.transpose(columns[...])[:8]


def attention(tables, bias, queries, backs, received, chunk, slots, scale):
    patch_blocks = bias.shape[0]
    total_rows = queries.shape[0]
    rows = total_rows // patch_blocks
    padded = pl.cdiv(rows, LANES) * LANES
    block_rows, width = received.shape[2:]
    tiles = pl.cdiv(slots * block_rows, KEY_TILE)
    wide = pl.BlockSpec((rows, 2 * LANES), lambda p, *_: (p, chunk))
    out = pl.BlockSpec((rows, 2 * LANES), lambda p, *_: (p, 0))
    return pl.pallas_call(
        functools.partial(attention_kernel, slots=slots, scale=scale),
        grid_spec=pltpu.PrefetchScalarGridSpec(
            num_scalar_prefetch=4,
            grid=(patch_blocks,),
            in_specs=[
                wide,
                wide,
                pl.BlockSpec((1,) + bias.shape[1:], lambda p, *_: (p, 0, 0)),
                pl.BlockSpec(memory_space=pl.ANY),
            ],
            out_specs=[out, out, pl.BlockSpec((1, 8, padded), lambda p, *_: (p, 0, 0))],
            scratch_shapes=[
                pltpu.VMEM((2, 2, tiles * KEY_TILE, width), jnp.bfloat16),
                pltpu.VMEM((2, tiles, rows, KEY_TILE), jnp.float32),
                pltpu.VMEM((2, tiles, rows, KEY_TILE), jnp.bfloat16),
                pltpu.VMEM((2, rows, LANES), jnp.float32),
                pltpu.VMEM((2, rows, width + LANES), jnp.float32),
                pltpu.VMEM((2, rows, width), jnp.float32),
                pltpu.VMEM((padded, LANES), jnp.float32),
                pltpu.SemaphoreType.DMA((2, slots)),
            ],
        ),
        out_shape=[jax.ShapeDtypeStruct((total_rows, 2 * LANES), jnp.float32)] * 2
        + [jax.ShapeDtypeStruct((patch_blocks, 8, padded), jnp.float32)],
        compiler_params=pltpu.CompilerParams(vmem_limit_bytes=58 << 20),
        cost_estimate=pl.CostEstimate(
            flops=8 * total_rows * slots * block_rows * width,
            transcendentals=total_rows * slots * block_rows,
            bytes_accessed=40 << 20,
        ),
    )(*tables, queries, backs, bias, received)


def merge_kernel(co_ref, ds_ref, mine_ref, theirs_ref, out_ref, *, scale, split):
    rows = co_ref.shape[0]
    mine, theirs = mine_ref[0], theirs_ref[0]
    kind = lax.broadcasted_iota(jnp.int32, mine.shape, 0)
    gap = mine - theirs
    share = 1.0 / (1.0 + jnp.exp(-gap))
    rest = 1.0 / (1.0 + jnp.exp(gap))
    rest_below = jnp.concatenate([rest[:1], rest[:-1]], axis=0)
    table = jnp.where(kind % 2 == 0, share, rest_below * gap * scale)
    tall = jnp.transpose(
        jnp.concatenate([table, jnp.zeros((LANES - 8, table.shape[1]), jnp.float32)], axis=0)
    )[:rows]
    lower = lax.broadcasted_iota(jnp.int32, (rows, LANES), 1) < split
    for head in range(2):
        lanes = pl.ds(head * LANES, LANES)
        weight = tall[:, 2 * head : 2 * head + 1]
        shift = tall[:, 2 * head + 1 : 2 * head + 2]
        outs = co_ref[:, lanes]
        value = weight * jnp.where(lower, ds_ref[:, lanes] + shift * outs, outs)
        out_ref[:, lanes] = value.astype(jnp.bfloat16)


def merge(outs, douts, mine, theirs, first, count, scale, split):
    patch_blocks, _, padded = mine.shape
    rows = outs.shape[0] // patch_blocks
    wide = pl.BlockSpec((rows, 2 * LANES), lambda p: (first + p, 0))
    flat = pl.BlockSpec((1, 8, padded), lambda p: (first + p, 0, 0))
    return pl.pallas_call(
        functools.partial(merge_kernel, scale=scale, split=split),
        grid=(count,),
        in_specs=[wide, wide, flat, flat],
        out_specs=pl.BlockSpec((rows, 2 * LANES), lambda p: (p, 0)),
        out_shape=jax.ShapeDtypeStruct((count * rows, 2 * LANES), jnp.bfloat16),
        cost_estimate=pl.CostEstimate(
            flops=20 * count * rows * LANES,
            transcendentals=0,
            bytes_accessed=20 * count * rows * LANES,
        ),
    )(outs, douts, mine, theirs)


def project_kernel(order, *refs, count, parts, last, chunk, depth):
    step = pl.program_id(0)
    cols = refs[count * parts]
    rest, weights = refs[count * parts + 1 : -1], refs[-1]
    before = rest[0] if len(rest) == (3 if last else 2) else None
    half = cols.shape[2] // 2

    @pl.when(step == 0)
    def _():
        empty = jnp.zeros((depth, half), weights.dtype)
        for i in range(count):
            for z in range(2):
                own = cols[z * count + order[i], pl.ds(chunk * depth, depth), :]
                grad_rows = pl.ds(2 * z * depth, depth)
                out_rows = pl.ds((2 * z + 1) * depth, depth)
                weights[i, grad_rows, :half] = empty
                weights[i, grad_rows, half:] = own[:, half:]
                weights[i, out_rows, :half] = own[:, :half]
                weights[i, out_rows, half:] = empty

    def part(pieces):
        value = jnp.dot(pieces[0][...], weights[0], preferred_element_type=jnp.float32)
        for i in range(1, count):
            value += jnp.dot(pieces[i][...], weights[i], preferred_element_type=jnp.float32)
        if before is not None:
            value += before[...]
        if last:
            rest[-2][...] = value[:, :half].astype(jnp.bfloat16)
            rest[-1][...] = value[:, half:].astype(jnp.bfloat16)
        else:
            rest[-1][...] = value

    for i in range(parts):
        pl.when(step * parts // pl.num_programs(0) == i)(
            functools.partial(part, refs[i * count : (i + 1) * count])
        )


def project(parts, cols, order, before, last, chunk):
    count = len(parts[0])
    rows, depth = parts[0][0].shape
    total_rows = rows * len(parts)
    width = cols.shape[2]
    steps = 4 // len(parts)
    tile = rows // steps
    rowwise = lambda w: pl.BlockSpec((tile, w), lambda i, *_: (i, 0))

    def within(which):
        return pl.BlockSpec(
            (tile, depth), lambda i, *_: (jnp.clip(i - which * steps, 0, steps - 1), 0)
        )

    halves = jax.ShapeDtypeStruct((total_rows, width // 2), jnp.bfloat16)
    return pl.pallas_call(
        functools.partial(
            project_kernel, count=count, parts=len(parts), last=last, chunk=chunk,
            depth=depth // 4,
        ),
        grid_spec=pltpu.PrefetchScalarGridSpec(
            num_scalar_prefetch=1,
            grid=(4,),
            in_specs=[within(i) for i in range(len(parts)) for _ in range(count)]
            + [pl.BlockSpec(cols.shape, lambda i, *_: (0, 0, 0))]
            + ([] if before is None else [rowwise(width)]),
            out_specs=[rowwise(width // 2)] * 2 if last else rowwise(width),
            scratch_shapes=[pltpu.VMEM((count, depth, width), jnp.bfloat16)],
        ),
        out_shape=[halves] * 2
        if last
        else jax.ShapeDtypeStruct((total_rows, width), jnp.float32),
        compiler_params=pltpu.CompilerParams(vmem_limit_bytes=40 << 20),
        cost_estimate=pl.CostEstimate(
            flops=2 * total_rows * depth * count * width,
            transcendentals=0,
            bytes_accessed=2 * total_rows * (depth * count + 2 * width),
        ),
    )(
        order, *[x for pieces in parts for x in pieces], cols,
        *([] if before is None else [before]),
    )


def swap(x, axis):
    return lax.ppermute(x, axis, [(0, 1), (1, 0)])


def gather_half(x, zl_size, y_size):
    if zl_size == 2 and y_size == 2:
        by_y = swap(x, "y")
        by_zl = swap(x, "zl")
        cut = x.shape[0] // 2
        corner = jnp.concatenate([swap(by_y[:cut], "zl"), swap(by_zl[cut:], "y")], axis=0)
        return [x, by_y, by_zl, corner]
    whole = lax.all_gather(x, ("zl", "y"), axis=0, tiled=False)
    return [whole[i] for i in range(zl_size * y_size)]


def scatter_sum(x, size, dim):
    index = lax.axis_index("dp")
    step = size // 2
    while step >= 1:
        half = x.shape[dim] // 2
        upper = (index // step) % 2
        keep = lax.dynamic_slice_in_dim(x, upper * half, half, dim)
        give = lax.dynamic_slice_in_dim(x, (1 - upper) * half, half, dim)
        got = lax.ppermute(
            give.astype(jnp.bfloat16), "dp", [(i, i ^ step) for i in range(size)]
        )
        x = keep + got.astype(jnp.float32)
        step //= 2
    return x


def local(
    patches, query_proj, output_proj, cache, block_lengths, neighbours, cotangent, *, sizes
):
    groups, zl_size, y_size = sizes
    inner = zl_size * y_size
    model = 2 * inner
    owner_count = groups * model
    group = lax.axis_index("dp")
    zh = lax.axis_index("zh")
    spot = lax.axis_index("zl") * y_size + lax.axis_index("y")
    me = group * model + zh * inner + spot
    local_blocks, block_rows, heads, width = cache.shape
    head_size = width // 2
    local_heads = query_proj.shape[1] // head_size
    features = patches.shape[1]
    columns = features // model
    slots = neighbours.shape[1]
    patch_blocks = neighbours.shape[0] // groups
    entry_count = patch_blocks * slots
    capacity = 2 * entry_count // owner_count
    row_count = patches.shape[0]
    head_scale = 1.0 / math.sqrt(head_size)
    grad_scale = 1.0 / math.sqrt(row_count * groups)

    all_ids = neighbours.reshape(groups, entry_count)
    match = all_ids // local_blocks == me
    order = jnp.arange(entry_count, dtype=jnp.int32)
    earlier = order[None, :] < order[:, None]
    rank = jnp.sum((match[:, None, :] & earlier[None]).astype(jnp.int32), axis=2)
    slot_range = jnp.arange(capacity, dtype=jnp.int32)
    placed = match[:, :, None] & (rank[:, :, None] == slot_range)
    chosen = jnp.sum(
        jnp.where(placed, (all_ids % local_blocks)[:, :, None], 0), axis=1
    ).reshape(groups * capacity)
    send_counts = jnp.sum(match.astype(jnp.int32), axis=1)

    def pack(c):
        return pack_blocks(
            chosen, send_counts, block_lengths, cache, c, groups, inner, capacity, local_heads
        ).reshape(groups * inner, capacity * 2 * block_rows, width)

    def exchange(x):
        return lax.all_to_all(
            x, ("dp", "zl", "y"), split_axis=0, concat_axis=0, tiled=True
        ).reshape(groups * inner * capacity, 2, block_rows, width)

    received = [exchange(pack(0))]
    q_other, o_other = swap(query_proj, "zh"), swap(output_proj, "zh")
    for c in range(1, local_heads):
        packed, q_other, o_other = lax.optimization_barrier((pack(c), q_other, o_other))
        received.append(exchange(packed))

    my_ids = lax.dynamic_slice_in_dim(
        neighbours, group * patch_blocks, patch_blocks, 0
    ).reshape(entry_count)
    owners = my_ids // local_blocks
    slot_of = jnp.sum(((owners[:, None] == owners[None, :]) & earlier).astype(jnp.int32), axis=1)
    source = (owners // model) * inner + owners % inner
    in_half = ((owners % model) // inner == zh).reshape(patch_blocks, slots)
    arrival = (source * capacity + slot_of).reshape(patch_blocks, slots)
    spots = jnp.arange(slots, dtype=jnp.int32)
    before = jnp.sum(
        (in_half[:, None, :] & (spots[None, :] < spots[:, None])[None]).astype(jnp.int32), axis=2
    )
    at = in_half[:, :, None] & (before[:, :, None] == spots)
    places = jnp.sum(jnp.where(at, arrival[:, :, None], 0), axis=1).reshape(entry_count)
    counts = jnp.sum(in_half.astype(jnp.int32), axis=1)

    marks = received[0][:, 0, block_rows - MARK_ROWS :, :].astype(jnp.float32)
    marks = marks[:, MARK_ROWS - 1, 0]
    rows_of = jnp.where(marks > MARK_LEAST, marks - MARK_BASE, float(block_rows)).astype(jnp.int32)
    arrivals = jnp.arange(rows_of.shape[0], dtype=jnp.int32)
    valid = jnp.sum(
        jnp.where(places[:, None] == arrivals[None, :], rows_of[None, :], 0), axis=1
    ).reshape(patch_blocks, slots)
    valid = jnp.where(spots[None, :] < counts[:, None], valid, 0)
    sizes_of = (valid + GRANULE - 1) // GRANULE
    offsets = jnp.sum(
        jnp.where(spots[None, None, :] < spots[None, :, None], sizes_of[:, None, :], 0), axis=2
    )
    tile_count = pl.cdiv(slots * block_rows, KEY_TILE)
    bias_shape = (patch_blocks, tile_count * KEY_TILE // LANES, LANES)
    key_at = LANES * lax.broadcasted_iota(jnp.int32, bias_shape, 1) + lax.broadcasted_iota(
        jnp.int32, bias_shape, 2
    )
    first_key = (offsets * GRANULE)[:, :, None, None]
    seen = (key_at[:, None] >= first_key) & (key_at[:, None] < first_key + valid[:, :, None, None])
    bias = jnp.where(jnp.any(seen, axis=1), 0.0, masked_value).astype(jnp.float32)
    tables = (places, counts, offsets.reshape(entry_count), sizes_of.reshape(entry_count))

    q_other, o_other, received[0] = lax.optimization_barrier(
        (q_other, o_other, received[0])
    )

    def both_halves(own, other):
        return jnp.where(zh == 0, own, other), jnp.where(zh == 0, other, own)

    q_halves = [
        w.reshape(features, local_heads, head_size) for w in both_halves(query_proj, q_other)
    ]
    q_wide = jnp.stack(q_halves, axis=2)
    q_wide = jnp.pad(q_wide, ((0, 0), (0, 0), (0, 0), (0, LANES - head_size)))
    q_wide = q_wide.reshape(features, local_heads * 2 * LANES)
    o_halves = [
        w.reshape(local_heads, head_size, features) for w in both_halves(output_proj, o_other)
    ]
    o_wide = jnp.stack(o_halves, axis=1)
    o_wide = jnp.pad(o_wide, ((0, 0), (0, 0), (LANES - head_size, 0), (0, 0)))
    o_wide = o_wide.reshape(local_heads * 2 * LANES, features)
    queries = (
        jnp.dot(patches, q_wide, preferred_element_type=jnp.float32) * head_scale
    ).astype(jnp.bfloat16)
    backs = nt_dot(cotangent, o_wide).astype(jnp.bfloat16)

    cols = jnp.concatenate(
        [
            output_proj.reshape(local_heads * head_size, model, columns).transpose(1, 0, 2),
            query_proj.reshape(model, columns, local_heads * head_size).transpose(0, 2, 1),
        ],
        axis=2,
    )
    if zl_size == 2 and y_size == 2:
        order = jnp.stack([spot, spot ^ 1, spot ^ 2, spot ^ 3])
    else:
        order = jnp.arange(inner, dtype=jnp.int32)

    part_count = 2 if patch_blocks % 2 == 0 else 1
    part_patches = patch_blocks // part_count
    gathered = []
    own = []
    for c in range(local_heads):
        final = c + 1 == local_heads
        if final:
            cols, bias, received[c] = lax.optimization_barrier((cols, bias, received[c]))
            cols = lax.all_to_all(cols, ("zh", "zl", "y"), split_axis=0, concat_axis=0, tiled=True)
        outs, douts, mine = attention(
            tables, bias, queries, backs, received[c], c, slots, head_scale
        )
        theirs = swap(mine, "zh")
        if final:
            theirs, cols = lax.optimization_barrier((theirs, cols))
        parts = [
            merge(outs, douts, mine, theirs, start, part_patches, head_scale, head_size)
            for start in range(0, patch_blocks, part_patches)
        ]
        if not final:
            parts, bias = lax.optimization_barrier((parts, bias))
        merged = [
            (part.astype(jnp.float32) + swap(part, "zh").astype(jnp.float32)).astype(jnp.bfloat16)
            for part in parts
        ]
        pieces = [gather_half(x, zl_size, y_size) for x in merged]
        gathered.append(pieces)
        if final:
            merged, pieces[0][1] = lax.optimization_barrier((merged, pieces[0][1]))
        own.append(
            jnp.concatenate(
                [lax.dynamic_slice_in_dim(x, zh * LANES, LANES, 1) for x in merged], axis=0
            )
        )
    result = None
    for c, pieces in enumerate(gathered):
        result = project(pieces, cols, order, result, c + 1 == local_heads, c)
    attended, patch_grad = result

    dquery = jnp.concatenate([x[:, :head_size] for x in own], axis=1)
    heads_out = jnp.concatenate([x[:, head_size:] for x in own], axis=1)
    query_term = (
        lax.dot_general(
            patches, dquery, (((0,), (0,)), ((), ())), preferred_element_type=jnp.float32
        )
        * grad_scale
    )
    output_term = (
        lax.dot_general(
            heads_out, cotangent, (((0,), (0,)), ((), ())), preferred_element_type=jnp.float32
        )
        * grad_scale
    )
    return (
        attended,
        patch_grad,
        scatter_sum(query_term, groups, 0),
        scatter_sum(output_term, groups, 1),
    )


def solution(mesh):
    groups, model = mesh.shape["dp"], mesh.shape["mp"]
    sizes = (groups, model // 4, 2)
    split = Mesh(
        mesh.devices.reshape(groups, 2, model // 4, 2), ("dp", "zh", "zl", "y")
    )
    mp = ("zh", "zl", "y")
    every = ("dp",) + mp
    return jax.shard_map(
        functools.partial(local, sizes=sizes),
        mesh=split,
        in_specs=(
            P("dp", None),
            P(None, mp),
            P(mp, None),
            P(every, None, None, None),
            P(every),
            P(),
            P("dp", None),
        ),
        out_specs=(P("dp", mp), P("dp", mp), P("dp", mp), P(mp, "dp")),
        check_vma=False,
    )
```

```python
import functools
import math

import jax
import jax.numpy as jnp
from jax import lax
from jax.experimental import pallas as pl
from jax.experimental.pallas import tpu as pltpu
from jax.sharding import Mesh
from jax.sharding import PartitionSpec as P

masked_value = -1e30
LANES = 128
MARK_ROWS = 16
MARK_BASE = 100.0
MARK_LEAST = 64.0
GRANULE = 32
KEY_TILE = 512


def pack_kernel(
    chosen, counts, lengths, cache_ref, out_ref, *, chunk, local_heads, inner, capacity
):
    slot = pl.program_id(0) * capacity + pl.program_id(1)

    @pl.when(pl.program_id(1) < counts[pl.program_id(0)])
    def _():
        by_head = pltpu.einshape("rhd->hrd", cache_ref[0])
        block_rows, width = by_head.shape[1:]
        valid = lengths[chosen[slot]]
        shape = (MARK_ROWS, width)
        corner = (lax.broadcasted_iota(jnp.int32, shape, 0) == MARK_ROWS - 1) & (
            lax.broadcasted_iota(jnp.int32, shape, 1) == 0
        )
        corner = corner & (valid < block_rows)
        mark = valid.astype(jnp.float32) + MARK_BASE
        for r in range(inner):
            for half in range(2):
                tile = by_head[(half * inner + r) * local_heads + chunk]
                out_ref[0, r, 0, half] = tile
                last = tile[block_rows - MARK_ROWS :].astype(jnp.float32)
                out_ref[0, r, 0, half, block_rows - MARK_ROWS :, :] = jnp.where(
                    corner, mark, last
                ).astype(jnp.bfloat16)


def pack_blocks(chosen, counts, lengths, cache, chunk, groups, inner, capacity, local_heads):
    _, block_rows, heads, width = cache.shape
    return pl.pallas_call(
        functools.partial(
            pack_kernel, chunk=chunk, local_heads=local_heads, inner=inner, capacity=capacity
        ),
        grid_spec=pltpu.PrefetchScalarGridSpec(
            num_scalar_prefetch=3,
            grid=(groups, capacity),
            in_specs=[
                pl.BlockSpec(
                    (1, block_rows, heads, width),
                    lambda g, s, ch, ct, ln: (ch[g * capacity + s], 0, 0, 0),
                )
            ],
            out_specs=pl.BlockSpec(
                (1, inner, 1, 2, block_rows, width),
                lambda g, s, ch, ct, ln: (g, 0, s, 0, 0, 0),
            ),
        ),
        out_shape=jax.ShapeDtypeStruct(
            (groups, inner, capacity, 2, block_rows, width), cache.dtype
        ),
        compiler_params=pltpu.CompilerParams(vmem_limit_bytes=32 << 20),
        cost_estimate=pl.CostEstimate(
            flops=0, transcendentals=0, bytes_accessed=groups * capacity * 2 * 262144
        ),
    )(chosen, counts, lengths, cache)


def nt_dot(left, right):
    return lax.dot_general(
        left, right, (((1,), (1,)), ((), ())), preferred_element_type=jnp.float32
    )


def attention_kernel(
    places, counts, offsets, sizes, q_ref, b_ref, bias_ref, recv_ref, co_ref, ds_ref, stat_ref,
    kv, scores, probs, top, acc, dacc, columns, sems, *, slots, scale,
):
    patch = pl.program_id(0)
    block_rows, width = recv_ref.shape[2:]
    steps = block_rows // GRANULE
    folds = KEY_TILE // LANES

    def each_copy(which, act):
        @pl.loop(0, counts[which])
        def _(j):
            entry = which * slots + j
            at = pl.multiple_of(offsets[entry] * GRANULE, GRANULE)
            for size in range(1, steps + 1):

                @pl.when(sizes[entry] == size)
                def _():
                    act(
                        pltpu.make_async_copy(
                            recv_ref.at[places[entry], :, pl.ds(0, size * GRANULE), :],
                            kv.at[which % 2, :, pl.ds(at, size * GRANULE), :],
                            sems.at[which % 2, j],
                        )
                    )

    @pl.when(patch == 0)
    def _():
        each_copy(patch, lambda copy: copy.start())

    @pl.when(patch + 1 < pl.num_programs(0))
    def _():
        each_copy(patch + 1, lambda copy: copy.start())

    filled = offsets[patch * slots + slots - 1] + sizes[patch * slots + slots - 1]
    per_tile = KEY_TILE // GRANULE
    tiles = jnp.maximum((filled + per_tile - 1) // per_tile, 1)

    @pl.loop(filled, tiles * per_tile)
    def _(g):
        kv[patch % 2, :, pl.ds(pl.multiple_of(g * GRANULE, GRANULE), GRANULE), :] = jnp.zeros(
            (2, GRANULE, width), kv.dtype
        )

    each_copy(patch, lambda copy: copy.wait())

    def key_tile(t, head):
        return kv[patch % 2, head, pl.ds(pl.multiple_of(t * KEY_TILE, KEY_TILE), KEY_TILE), :]

    rows = q_ref.shape[0]
    lanes = [pl.ds(head * LANES, LANES) for head in range(2)]
    top[...] = jnp.full_like(top, masked_value)
    acc[...] = jnp.zeros_like(acc)
    dacc[...] = jnp.zeros_like(dacc)

    @pl.loop(0, tiles)
    def _(t):
        for head in range(2):
            score = nt_dot(q_ref[:, lanes[head]], key_tile(t, head))
            best = top[head]
            for fold in range(folds):
                part = score[:, fold * LANES : (fold + 1) * LANES]
                part = part + bias_ref[0, pl.ds(t * folds + fold, 1), :]
                scores[head, t, :, fold * LANES : (fold + 1) * LANES] = part
                best = jnp.maximum(best, part)
            top[head] = best

    row_max = [jnp.max(top[head], axis=1, keepdims=True) for head in range(2)]
    ones = jnp.ones((KEY_TILE, LANES), jnp.bfloat16)

    @pl.loop(0, tiles)
    def _(t):
        for head in range(2):
            weights = jnp.exp(scores[head, t] - row_max[head]).astype(jnp.bfloat16)
            probs[head, t] = weights
            acc[head] += jnp.dot(
                weights,
                jnp.concatenate([key_tile(t, head), ones], axis=1),
                preferred_element_type=jnp.float32,
            )

    inverse, inner, stats = [], [], []
    for head in range(2):
        row_sum = acc[head, :, width : width + 1]
        inverse.append(1.0 / row_sum)
        outs = acc[head, :, :width] * inverse[head]
        co_ref[:, lanes[head]] = outs
        inner.append(
            jnp.sum(outs * b_ref[:, lanes[head]].astype(jnp.float32), axis=1, keepdims=True)
        )
        stats += [row_max[head] + jnp.log(row_sum), inner[head]]

    @pl.loop(0, tiles)
    def _(t):
        for head in range(2):
            dprobs = nt_dot(b_ref[:, lanes[head]], key_tile(t, head))
            dscores = (probs[head, t].astype(jnp.float32) * (dprobs - inner[head])).astype(
                jnp.bfloat16
            )
            dacc[head] += jnp.dot(dscores, key_tile(t, head), preferred_element_type=jnp.float32)

    for head in range(2):
        ds_ref[:, lanes[head]] = dacc[head] * (inverse[head] * scale)
    lane = lax.broadcasted_iota(jnp.int32, (rows, LANES), 1)
    columns[rows:, :] = jnp.zeros((columns.shape[0] - rows, LANES), jnp.float32)
    picked = jnp.where(lane == 0, stats[0], stats[1])
    picked = jnp.where(lane == 2, stats[2], picked)
    columns[:rows, :] = jnp.where(lane == 3, stats[3], picked)
    stat_ref[0] = jnp.transpose(columns[...])[:8]


def attention(tables, bias, queries, backs, received, chunk, slots, scale):
    patch_blocks = bias.shape[0]
    total_rows = queries.shape[0]
    rows = total_rows // patch_blocks
    padded = pl.cdiv(rows, LANES) * LANES
    block_rows, width = received.shape[2:]
    tiles = pl.cdiv(slots * block_rows, KEY_TILE)
    wide = pl.BlockSpec((rows, 2 * LANES), lambda p, *_: (p, chunk))
    out = pl.BlockSpec((rows, 2 * LANES), lambda p, *_: (p, 0))
    return pl.pallas_call(
        functools.partial(attention_kernel, slots=slots, scale=scale),
        grid_spec=pltpu.PrefetchScalarGridSpec(
            num_scalar_prefetch=4,
            grid=(patch_blocks,),
            in_specs=[
                wide,
                wide,
                pl.BlockSpec((1,) + bias.shape[1:], lambda p, *_: (p, 0, 0)),
                pl.BlockSpec(memory_space=pl.ANY),
            ],
            out_specs=[out, out, pl.BlockSpec((1, 8, padded), lambda p, *_: (p, 0, 0))],
            scratch_shapes=[
                pltpu.VMEM((2, 2, tiles * KEY_TILE, width), jnp.bfloat16),
                pltpu.VMEM((2, tiles, rows, KEY_TILE), jnp.float32),
                pltpu.VMEM((2, tiles, rows, KEY_TILE), jnp.bfloat16),
                pltpu.VMEM((2, rows, LANES), jnp.float32),
                pltpu.VMEM((2, rows, width + LANES), jnp.float32),
                pltpu.VMEM((2, rows, width), jnp.float32),
                pltpu.VMEM((padded, LANES), jnp.float32),
                pltpu.SemaphoreType.DMA((2, slots)),
            ],
        ),
        out_shape=[jax.ShapeDtypeStruct((total_rows, 2 * LANES), jnp.float32)] * 2
        + [jax.ShapeDtypeStruct((patch_blocks, 8, padded), jnp.float32)],
        compiler_params=pltpu.CompilerParams(vmem_limit_bytes=58 << 20),
        cost_estimate=pl.CostEstimate(
            flops=8 * total_rows * slots * block_rows * width,
            transcendentals=total_rows * slots * block_rows,
            bytes_accessed=40 << 20,
        ),
    )(*tables, queries, backs, bias, received)


def merge_kernel(co_ref, ds_ref, mine_ref, theirs_ref, out_ref, *, scale, split):
    rows = co_ref.shape[0]
    mine, theirs = mine_ref[0], theirs_ref[0]
    kind = lax.broadcasted_iota(jnp.int32, mine.shape, 0)
    gap = mine - theirs
    share = 1.0 / (1.0 + jnp.exp(-gap))
    rest = 1.0 / (1.0 + jnp.exp(gap))
    rest_below = jnp.concatenate([rest[:1], rest[:-1]], axis=0)
    table = jnp.where(kind % 2 == 0, share, rest_below * gap * scale)
    tall = jnp.transpose(
        jnp.concatenate([table, jnp.zeros((LANES - 8, table.shape[1]), jnp.float32)], axis=0)
    )[:rows]
    lower = lax.broadcasted_iota(jnp.int32, (rows, LANES), 1) < split
    for head in range(2):
        lanes = pl.ds(head * LANES, LANES)
        weight = tall[:, 2 * head : 2 * head + 1]
        shift = tall[:, 2 * head + 1 : 2 * head + 2]
        outs = co_ref[:, lanes]
        value = weight * jnp.where(lower, ds_ref[:, lanes] + shift * outs, outs)
        out_ref[:, lanes] = value.astype(jnp.bfloat16)


def merge(outs, douts, mine, theirs, first, count, scale, split):
    patch_blocks, _, padded = mine.shape
    rows = outs.shape[0] // patch_blocks
    wide = pl.BlockSpec((rows, 2 * LANES), lambda p: (first + p, 0))
    flat = pl.BlockSpec((1, 8, padded), lambda p: (first + p, 0, 0))
    return pl.pallas_call(
        functools.partial(merge_kernel, scale=scale, split=split),
        grid=(count,),
        in_specs=[wide, wide, flat, flat],
        out_specs=pl.BlockSpec((rows, 2 * LANES), lambda p: (p, 0)),
        out_shape=jax.ShapeDtypeStruct((count * rows, 2 * LANES), jnp.bfloat16),
        cost_estimate=pl.CostEstimate(
            flops=20 * count * rows * LANES,
            transcendentals=0,
            bytes_accessed=20 * count * rows * LANES,
        ),
    )(outs, douts, mine, theirs)


def project_kernel(*refs, count, parts, last, chunk, depth):
    step = pl.program_id(0)
    cols = refs[count * parts]
    rest, weights = refs[count * parts + 1 : -1], refs[-1]
    before = rest[0] if len(rest) == (3 if last else 2) else None
    half = cols.shape[3] // 2

    @pl.when(step == 0)
    def _():
        empty = jnp.zeros((depth, half), weights.dtype)
        for i in range(count):
            for z in range(2):
                own = cols[i, z, pl.ds(chunk * depth, depth), :]
                grad_rows = pl.ds(2 * z * depth, depth)
                out_rows = pl.ds((2 * z + 1) * depth, depth)
                weights[i, grad_rows, :half] = empty
                weights[i, grad_rows, half:] = own[:, half:]
                weights[i, out_rows, :half] = own[:, :half]
                weights[i, out_rows, half:] = empty

    def part(pieces):
        value = jnp.dot(pieces[0][...], weights[0], preferred_element_type=jnp.float32)
        for i in range(1, count):
            value += jnp.dot(pieces[i][...], weights[i], preferred_element_type=jnp.float32)
        if before is not None:
            value += before[...]
        if last:
            rest[-2][...] = value[:, :half].astype(jnp.bfloat16)
            rest[-1][...] = value[:, half:].astype(jnp.bfloat16)
        else:
            rest[-1][...] = value

    for i in range(parts):
        pl.when(step * parts // pl.num_programs(0) == i)(
            functools.partial(part, refs[i * count : (i + 1) * count])
        )


def project(parts, cols, before, last, chunk):
    count = len(parts[0])
    rows, depth = parts[0][0].shape
    total_rows = rows * len(parts)
    width = cols.shape[3]
    steps = 4 // len(parts)
    tile = rows // steps
    rowwise = lambda w: pl.BlockSpec((tile, w), lambda i: (i, 0))

    def within(which):
        return pl.BlockSpec(
            (tile, depth), lambda i: (jnp.clip(i - which * steps, 0, steps - 1), 0)
        )

    halves = jax.ShapeDtypeStruct((total_rows, width // 2), jnp.bfloat16)
    return pl.pallas_call(
        functools.partial(
            project_kernel, count=count, parts=len(parts), last=last, chunk=chunk,
            depth=depth // 4,
        ),
        grid=(4,),
        in_specs=[within(i) for i in range(len(parts)) for _ in range(count)]
        + [pl.BlockSpec(cols.shape, lambda i: (0, 0, 0, 0))]
        + ([] if before is None else [rowwise(width)]),
        out_specs=[rowwise(width // 2)] * 2 if last else rowwise(width),
        scratch_shapes=[pltpu.VMEM((count, depth, width), jnp.bfloat16)],
        out_shape=[halves] * 2
        if last
        else jax.ShapeDtypeStruct((total_rows, width), jnp.float32),
        compiler_params=pltpu.CompilerParams(vmem_limit_bytes=40 << 20),
        cost_estimate=pl.CostEstimate(
            flops=2 * total_rows * depth * count * width,
            transcendentals=0,
            bytes_accessed=2 * total_rows * (depth * count + 2 * width),
        ),
    )(*[x for pieces in parts for x in pieces], cols, *([] if before is None else [before]))


def swap(x, axis):
    return lax.ppermute(x, axis, [(0, 1), (1, 0)])


def first_hop(x, small):
    if small:
        return [x, swap(x, "y"), swap(x, "zl")]
    whole = lax.all_gather(x, ("zl", "y"), axis=0, tiled=False)
    return [whole[i] for i in range(whole.shape[0])]


def second_hop(pieces, small):
    if not small:
        return pieces
    x, by_y, by_zl = pieces
    cut = x.shape[0] // 2
    corner = jnp.concatenate([swap(by_y[:cut], "zl"), swap(by_zl[cut:], "y")], axis=0)
    return [x, by_y, by_zl, corner]


def scatter_sum(x, size, dim):
    index = lax.axis_index("dp")
    step = size // 2
    while step >= 1:
        half = x.shape[dim] // 2
        upper = (index // step) % 2
        keep = lax.dynamic_slice_in_dim(x, upper * half, half, dim)
        give = lax.dynamic_slice_in_dim(x, (1 - upper) * half, half, dim)
        got = lax.ppermute(
            give.astype(jnp.bfloat16), "dp", [(i, i ^ step) for i in range(size)]
        )
        x = keep + got.astype(jnp.float32)
        step //= 2
    return x


def local(
    patches, query_proj, output_proj, cache, block_lengths, neighbours, cotangent, *, sizes
):
    groups, zl_size, y_size = sizes
    inner = zl_size * y_size
    model = 2 * inner
    owner_count = groups * model
    group = lax.axis_index("dp")
    zh = lax.axis_index("zh")
    spot = lax.axis_index("zl") * y_size + lax.axis_index("y")
    me = group * model + zh * inner + spot
    local_blocks, block_rows, heads, width = cache.shape
    head_size = width // 2
    local_heads = query_proj.shape[1] // head_size
    features = patches.shape[1]
    columns = features // model
    slots = neighbours.shape[1]
    patch_blocks = neighbours.shape[0] // groups
    entry_count = patch_blocks * slots
    capacity = 2 * entry_count // owner_count
    row_count = patches.shape[0]
    head_scale = 1.0 / math.sqrt(head_size)
    grad_scale = 1.0 / math.sqrt(row_count * groups)

    all_ids = neighbours.reshape(groups, entry_count)
    match = all_ids // local_blocks == me
    order = jnp.arange(entry_count, dtype=jnp.int32)
    earlier = order[None, :] < order[:, None]
    rank = jnp.sum((match[:, None, :] & earlier[None]).astype(jnp.int32), axis=2)
    slot_range = jnp.arange(capacity, dtype=jnp.int32)
    placed = match[:, :, None] & (rank[:, :, None] == slot_range)
    chosen = jnp.sum(
        jnp.where(placed, (all_ids % local_blocks)[:, :, None], 0), axis=1
    ).reshape(groups * capacity)
    send_counts = jnp.sum(match.astype(jnp.int32), axis=1)

    def pack(c):
        return pack_blocks(
            chosen, send_counts, block_lengths, cache, c, groups, inner, capacity, local_heads
        ).reshape(groups * inner, capacity * 2 * block_rows, width)

    def exchange(x):
        return lax.all_to_all(
            x, ("dp", "zl", "y"), split_axis=0, concat_axis=0, tiled=True
        ).reshape(groups * inner * capacity, 2, block_rows, width)

    received = [exchange(pack(0))]
    q_other, o_other = swap(query_proj, "zh"), swap(output_proj, "zh")
    for c in range(1, local_heads):
        packed, q_other, o_other = lax.optimization_barrier((pack(c), q_other, o_other))
        received.append(exchange(packed))

    my_ids = lax.dynamic_slice_in_dim(
        neighbours, group * patch_blocks, patch_blocks, 0
    ).reshape(entry_count)
    owners = my_ids // local_blocks
    slot_of = jnp.sum(((owners[:, None] == owners[None, :]) & earlier).astype(jnp.int32), axis=1)
    source = (owners // model) * inner + owners % inner
    in_half = ((owners % model) // inner == zh).reshape(patch_blocks, slots)
    arrival = (source * capacity + slot_of).reshape(patch_blocks, slots)
    spots = jnp.arange(slots, dtype=jnp.int32)
    before = jnp.sum(
        (in_half[:, None, :] & (spots[None, :] < spots[:, None])[None]).astype(jnp.int32), axis=2
    )
    at = in_half[:, :, None] & (before[:, :, None] == spots)
    places = jnp.sum(jnp.where(at, arrival[:, :, None], 0), axis=1).reshape(entry_count)
    counts = jnp.sum(in_half.astype(jnp.int32), axis=1)

    marks = received[0][:, 0, block_rows - MARK_ROWS :, :].astype(jnp.float32)
    marks = marks[:, MARK_ROWS - 1, 0]
    rows_of = jnp.where(marks > MARK_LEAST, marks - MARK_BASE, float(block_rows)).astype(jnp.int32)
    arrivals = jnp.arange(rows_of.shape[0], dtype=jnp.int32)
    valid = jnp.sum(
        jnp.where(places[:, None] == arrivals[None, :], rows_of[None, :], 0), axis=1
    ).reshape(patch_blocks, slots)
    valid = jnp.where(spots[None, :] < counts[:, None], valid, 0)
    sizes_of = (valid + GRANULE - 1) // GRANULE
    offsets = jnp.sum(
        jnp.where(spots[None, None, :] < spots[None, :, None], sizes_of[:, None, :], 0), axis=2
    )
    tile_count = pl.cdiv(slots * block_rows, KEY_TILE)
    bias_shape = (patch_blocks, tile_count * KEY_TILE // LANES, LANES)
    key_at = LANES * lax.broadcasted_iota(jnp.int32, bias_shape, 1) + lax.broadcasted_iota(
        jnp.int32, bias_shape, 2
    )
    first_key = (offsets * GRANULE)[:, :, None, None]
    seen = (key_at[:, None] >= first_key) & (key_at[:, None] < first_key + valid[:, :, None, None])
    bias = jnp.where(jnp.any(seen, axis=1), 0.0, masked_value).astype(jnp.float32)
    tables = (places, counts, offsets.reshape(entry_count), sizes_of.reshape(entry_count))

    q_other, o_other, received[0] = lax.optimization_barrier(
        (q_other, o_other, received[0])
    )

    def both_halves(own, other):
        return jnp.where(zh == 0, own, other), jnp.where(zh == 0, other, own)

    q_both = both_halves(query_proj, q_other)
    q_wide = jnp.stack([w.reshape(features, local_heads, head_size) for w in q_both], axis=2)
    q_wide = jnp.pad(q_wide, ((0, 0), (0, 0), (0, 0), (0, LANES - head_size)))
    q_wide = q_wide.reshape(features, local_heads * 2 * LANES)
    o_both = both_halves(output_proj, o_other)
    o_wide = jnp.stack([w.reshape(local_heads, head_size, features) for w in o_both], axis=1)
    o_wide = jnp.pad(o_wide, ((0, 0), (0, 0), (LANES - head_size, 0), (0, 0)))
    o_wide = o_wide.reshape(local_heads * 2 * LANES, features)
    queries = (
        jnp.dot(patches, q_wide, preferred_element_type=jnp.float32) * head_scale
    ).astype(jnp.bfloat16)
    backs = nt_dot(cotangent, o_wide).astype(jnp.bfloat16)

    small = zl_size == 2 and y_size == 2
    own_width = local_heads * head_size
    o_blocks = jnp.stack(o_both).reshape(2, own_width, model, columns).transpose(2, 0, 1, 3)
    q_blocks = jnp.stack(q_both).reshape(2, model, columns, own_width).transpose(1, 0, 3, 2)
    blocks = lax.dynamic_slice_in_dim(
        jnp.concatenate([o_blocks, q_blocks], axis=3), zh * inner, inner, 0
    )

    part_count = 2 if patch_blocks % 2 == 0 else 1
    part_patches = patch_blocks // part_count
    gathered = []
    own = []
    for c in range(local_heads):
        final = c + 1 == local_heads
        if final:
            blocks, bias, received[c] = lax.optimization_barrier((blocks, bias, received[c]))
            if small:
                pairs = lambda d: [(i, i ^ d) for i in range(inner)]
                cols = [
                    lax.ppermute(
                        lax.dynamic_index_in_dim(blocks, spot ^ d, 0, keepdims=False),
                        ("zl", "y"),
                        pairs(d),
                    )
                    if d
                    else lax.dynamic_index_in_dim(blocks, spot, 0, keepdims=False)
                    for d in range(inner)
                ]
                cols = jnp.stack(cols)
            else:
                cols = lax.all_to_all(blocks, ("zl", "y"), split_axis=0, concat_axis=0, tiled=True)
        outs, douts, mine = attention(
            tables, bias, queries, backs, received[c], c, slots, head_scale
        )
        theirs = swap(mine, "zh")
        if final:
            theirs, _ = lax.optimization_barrier((theirs, cols))
        parts = [
            merge(outs, douts, mine, theirs, start, part_patches, head_scale, head_size)
            for start in range(0, patch_blocks, part_patches)
        ]
        if gathered:
            gathered[-1], _ = lax.optimization_barrier((gathered[-1], parts))
            gathered[-1] = [second_hop(x, small) for x in gathered[-1]]
        if not final:
            parts, bias = lax.optimization_barrier((parts, bias))
        merged = [
            (part.astype(jnp.float32) + swap(part, "zh").astype(jnp.float32)).astype(jnp.bfloat16)
            for part in parts
        ]
        pieces = [first_hop(x, small) for x in merged]
        gathered.append(pieces)
        if final:
            result = None
            for i, earlier in enumerate(gathered[:-1]):
                result = project(earlier, cols, result, False, i)
            if result is not None:
                merged, _ = lax.optimization_barrier((merged, result))
        own.append(
            jnp.concatenate(
                [lax.dynamic_slice_in_dim(x, zh * LANES, LANES, 1) for x in merged], axis=0
            )
        )
    last_pieces = [second_hop(x, small) for x in gathered[-1]]
    attended, patch_grad = project(last_pieces, cols, result, True, local_heads - 1)

    dquery = jnp.concatenate([x[:, :head_size] for x in own], axis=1)
    heads_out = jnp.concatenate([x[:, head_size:] for x in own], axis=1)
    query_term = (
        lax.dot_general(
            patches, dquery, (((0,), (0,)), ((), ())), preferred_element_type=jnp.float32
        )
        * grad_scale
    )
    output_term = (
        lax.dot_general(
            heads_out, cotangent, (((0,), (0,)), ((), ())), preferred_element_type=jnp.float32
        )
        * grad_scale
    )
    return (
        attended,
        patch_grad,
        scatter_sum(query_term, groups, 0),
        scatter_sum(output_term, groups, 1),
    )


def solution(mesh):
    groups, model = mesh.shape["dp"], mesh.shape["mp"]
    sizes = (groups, model // 4, 2)
    split = Mesh(
        mesh.devices.reshape(groups, 2, model // 4, 2), ("dp", "zh", "zl", "y")
    )
    mp = ("zh", "zl", "y")
    every = ("dp",) + mp
    return jax.shard_map(
        functools.partial(local, sizes=sizes),
        mesh=split,
        in_specs=(
            P("dp", None),
            P(None, mp),
            P(mp, None),
            P(every, None, None, None),
            P(every),
            P(),
            P("dp", None),
        ),
        out_specs=(P("dp", mp), P("dp", mp), P("dp", mp), P(mp, "dp")),
        check_vma=False,
    )
```

```python
import functools
import math

import jax
import jax.numpy as jnp
from jax import lax
from jax.experimental import pallas as pl
from jax.experimental.pallas import tpu as pltpu
from jax.sharding import Mesh
from jax.sharding import PartitionSpec as P

masked_value = -1e30
LANES = 128
MARK_ROWS = 16
MARK_BASE = 100.0
MARK_LEAST = 64.0
GRANULE = 32
KEY_TILE = 512


def pack_kernel(
    chosen, counts, lengths, cache_ref, out_ref, *, chunk, local_heads, inner, capacity
):
    slot = pl.program_id(0) * capacity + pl.program_id(1)

    @pl.when(pl.program_id(1) < counts[pl.program_id(0)])
    def _():
        by_head = pltpu.einshape("rhd->hrd", cache_ref[0])
        block_rows, width = by_head.shape[1:]
        valid = lengths[chosen[slot]]
        shape = (MARK_ROWS, width)
        corner = (lax.broadcasted_iota(jnp.int32, shape, 0) == MARK_ROWS - 1) & (
            lax.broadcasted_iota(jnp.int32, shape, 1) == 0
        )
        corner = corner & (valid < block_rows)
        mark = valid.astype(jnp.float32) + MARK_BASE
        for r in range(inner):
            for half in range(2):
                tile = by_head[(half * inner + r) * local_heads + chunk]
                out_ref[0, r, 0, half] = tile
                last = tile[block_rows - MARK_ROWS :].astype(jnp.float32)
                out_ref[0, r, 0, half, block_rows - MARK_ROWS :, :] = jnp.where(
                    corner, mark, last
                ).astype(jnp.bfloat16)


def pack_blocks(chosen, counts, lengths, cache, chunk, groups, inner, capacity, local_heads):
    _, block_rows, heads, width = cache.shape
    return pl.pallas_call(
        functools.partial(
            pack_kernel, chunk=chunk, local_heads=local_heads, inner=inner, capacity=capacity
        ),
        grid_spec=pltpu.PrefetchScalarGridSpec(
            num_scalar_prefetch=3,
            grid=(groups, capacity),
            in_specs=[
                pl.BlockSpec(
                    (1, block_rows, heads, width),
                    lambda g, s, ch, ct, ln: (ch[g * capacity + s], 0, 0, 0),
                )
            ],
            out_specs=pl.BlockSpec(
                (1, inner, 1, 2, block_rows, width),
                lambda g, s, ch, ct, ln: (g, 0, s, 0, 0, 0),
            ),
        ),
        out_shape=jax.ShapeDtypeStruct(
            (groups, inner, capacity, 2, block_rows, width), cache.dtype
        ),
        compiler_params=pltpu.CompilerParams(vmem_limit_bytes=32 << 20),
        cost_estimate=pl.CostEstimate(
            flops=0, transcendentals=0, bytes_accessed=groups * capacity * 2 * 262144
        ),
    )(chosen, counts, lengths, cache)


def nt_dot(left, right):
    return lax.dot_general(
        left, right, (((1,), (1,)), ((), ())), preferred_element_type=jnp.float32
    )


def attention_kernel(
    places, counts, offsets, sizes, q_ref, b_ref, bias_ref, recv_ref, co_ref, ds_ref, stat_ref,
    kv, scores, probs, top, acc, dacc, columns, sems, *, slots, scale,
):
    patch = pl.program_id(0)
    block_rows, width = recv_ref.shape[2:]
    steps = block_rows // GRANULE
    folds = KEY_TILE // LANES

    def each_copy(which, act):
        @pl.loop(0, counts[which])
        def _(j):
            entry = which * slots + j
            at = pl.multiple_of(offsets[entry] * GRANULE, GRANULE)
            for size in range(1, steps + 1):

                @pl.when(sizes[entry] == size)
                def _():
                    act(
                        pltpu.make_async_copy(
                            recv_ref.at[places[entry], :, pl.ds(0, size * GRANULE), :],
                            kv.at[which % 2, :, pl.ds(at, size * GRANULE), :],
                            sems.at[which % 2, j],
                        )
                    )

    @pl.when(patch == 0)
    def _():
        each_copy(patch, lambda copy: copy.start())

    @pl.when(patch + 1 < pl.num_programs(0))
    def _():
        each_copy(patch + 1, lambda copy: copy.start())

    filled = offsets[patch * slots + slots - 1] + sizes[patch * slots + slots - 1]
    per_tile = KEY_TILE // GRANULE
    tiles = jnp.maximum((filled + per_tile - 1) // per_tile, 1)

    @pl.loop(filled, tiles * per_tile)
    def _(g):
        kv[patch % 2, :, pl.ds(pl.multiple_of(g * GRANULE, GRANULE), GRANULE), :] = jnp.zeros(
            (2, GRANULE, width), kv.dtype
        )

    each_copy(patch, lambda copy: copy.wait())

    def key_tile(t, head):
        return kv[patch % 2, head, pl.ds(pl.multiple_of(t * KEY_TILE, KEY_TILE), KEY_TILE), :]

    rows = q_ref.shape[0]
    lanes = [pl.ds(head * LANES, LANES) for head in range(2)]
    top[...] = jnp.full_like(top, masked_value)
    acc[...] = jnp.zeros_like(acc)
    dacc[...] = jnp.zeros_like(dacc)

    @pl.loop(0, tiles)
    def _(t):
        for head in range(2):
            score = nt_dot(q_ref[:, lanes[head]], key_tile(t, head))
            best = top[head]
            for fold in range(folds):
                part = score[:, fold * LANES : (fold + 1) * LANES]
                part = part + bias_ref[0, pl.ds(t * folds + fold, 1), :]
                scores[head, t, :, fold * LANES : (fold + 1) * LANES] = part
                best = jnp.maximum(best, part)
            top[head] = best

    row_max = [jnp.max(top[head], axis=1, keepdims=True) for head in range(2)]
    ones = jnp.ones((KEY_TILE, LANES), jnp.bfloat16)

    @pl.loop(0, tiles)
    def _(t):
        for head in range(2):
            weights = jnp.exp(scores[head, t] - row_max[head]).astype(jnp.bfloat16)
            probs[head, t] = weights
            acc[head] += jnp.dot(
                weights,
                jnp.concatenate([key_tile(t, head), ones], axis=1),
                preferred_element_type=jnp.float32,
            )

    inverse, inner, stats = [], [], []
    for head in range(2):
        row_sum = acc[head, :, width : width + 1]
        inverse.append(1.0 / row_sum)
        outs = acc[head, :, :width] * inverse[head]
        co_ref[:, lanes[head]] = outs
        inner.append(
            jnp.sum(outs * b_ref[:, lanes[head]].astype(jnp.float32), axis=1, keepdims=True)
        )
        stats += [row_max[head] + jnp.log(row_sum), inner[head]]

    @pl.loop(0, tiles)
    def _(t):
        for head in range(2):
            dprobs = nt_dot(b_ref[:, lanes[head]], key_tile(t, head))
            dscores = (probs[head, t].astype(jnp.float32) * (dprobs - inner[head])).astype(
                jnp.bfloat16
            )
            dacc[head] += jnp.dot(dscores, key_tile(t, head), preferred_element_type=jnp.float32)

    for head in range(2):
        ds_ref[:, lanes[head]] = dacc[head] * (inverse[head] * scale)
    lane = lax.broadcasted_iota(jnp.int32, (rows, LANES), 1)
    columns[rows:, :] = jnp.zeros((columns.shape[0] - rows, LANES), jnp.float32)
    picked = jnp.where(lane == 0, stats[0], stats[1])
    picked = jnp.where(lane == 2, stats[2], picked)
    columns[:rows, :] = jnp.where(lane == 3, stats[3], picked)
    stat_ref[0] = jnp.transpose(columns[...])[:8]


def attention(tables, bias, queries, backs, received, chunk, slots, scale):
    patch_blocks = bias.shape[0]
    total_rows = queries.shape[0]
    rows = total_rows // patch_blocks
    padded = pl.cdiv(rows, LANES) * LANES
    block_rows, width = received.shape[2:]
    tiles = pl.cdiv(slots * block_rows, KEY_TILE)
    wide = pl.BlockSpec((rows, 2 * LANES), lambda p, *_: (p, chunk))
    out = pl.BlockSpec((rows, 2 * LANES), lambda p, *_: (p, 0))
    return pl.pallas_call(
        functools.partial(attention_kernel, slots=slots, scale=scale),
        grid_spec=pltpu.PrefetchScalarGridSpec(
            num_scalar_prefetch=4,
            grid=(patch_blocks,),
            in_specs=[
                wide,
                wide,
                pl.BlockSpec((1,) + bias.shape[1:], lambda p, *_: (p, 0, 0)),
                pl.BlockSpec(memory_space=pl.ANY),
            ],
            out_specs=[out, out, pl.BlockSpec((1, 8, padded), lambda p, *_: (p, 0, 0))],
            scratch_shapes=[
                pltpu.VMEM((2, 2, tiles * KEY_TILE, width), jnp.bfloat16),
                pltpu.VMEM((2, tiles, rows, KEY_TILE), jnp.float32),
                pltpu.VMEM((2, tiles, rows, KEY_TILE), jnp.bfloat16),
                pltpu.VMEM((2, rows, LANES), jnp.float32),
                pltpu.VMEM((2, rows, width + LANES), jnp.float32),
                pltpu.VMEM((2, rows, width), jnp.float32),
                pltpu.VMEM((padded, LANES), jnp.float32),
                pltpu.SemaphoreType.DMA((2, slots)),
            ],
        ),
        out_shape=[jax.ShapeDtypeStruct((total_rows, 2 * LANES), jnp.float32)] * 2
        + [jax.ShapeDtypeStruct((patch_blocks, 8, padded), jnp.float32)],
        compiler_params=pltpu.CompilerParams(vmem_limit_bytes=58 << 20),
        cost_estimate=pl.CostEstimate(
            flops=8 * total_rows * slots * block_rows * width,
            transcendentals=total_rows * slots * block_rows,
            bytes_accessed=40 << 20,
        ),
    )(*tables, queries, backs, bias, received)


def merge_kernel(co_ref, ds_ref, mine_ref, theirs_ref, out_ref, *, scale, split):
    rows = co_ref.shape[0]
    mine, theirs = mine_ref[0], theirs_ref[0]
    kind = lax.broadcasted_iota(jnp.int32, mine.shape, 0)
    gap = mine - theirs
    share = 1.0 / (1.0 + jnp.exp(-gap))
    rest = 1.0 / (1.0 + jnp.exp(gap))
    rest_below = jnp.concatenate([rest[:1], rest[:-1]], axis=0)
    table = jnp.where(kind % 2 == 0, share, rest_below * gap * scale)
    tall = jnp.transpose(
        jnp.concatenate([table, jnp.zeros((LANES - 8, table.shape[1]), jnp.float32)], axis=0)
    )[:rows]
    lower = lax.broadcasted_iota(jnp.int32, (rows, LANES), 1) < split
    for head in range(2):
        lanes = pl.ds(head * LANES, LANES)
        weight = tall[:, 2 * head : 2 * head + 1]
        shift = tall[:, 2 * head + 1 : 2 * head + 2]
        outs = co_ref[:, lanes]
        value = weight * jnp.where(lower, ds_ref[:, lanes] + shift * outs, outs)
        out_ref[:, lanes] = value.astype(jnp.bfloat16)


def merge(outs, douts, mine, theirs, first, count, scale, split):
    patch_blocks, _, padded = mine.shape
    rows = outs.shape[0] // patch_blocks
    wide = pl.BlockSpec((rows, 2 * LANES), lambda p: (first + p, 0))
    flat = pl.BlockSpec((1, 8, padded), lambda p: (first + p, 0, 0))
    return pl.pallas_call(
        functools.partial(merge_kernel, scale=scale, split=split),
        grid=(count,),
        in_specs=[wide, wide, flat, flat],
        out_specs=pl.BlockSpec((rows, 2 * LANES), lambda p: (p, 0)),
        out_shape=jax.ShapeDtypeStruct((count * rows, 2 * LANES), jnp.bfloat16),
        cost_estimate=pl.CostEstimate(
            flops=20 * count * rows * LANES,
            transcendentals=0,
            bytes_accessed=20 * count * rows * LANES,
        ),
    )(outs, douts, mine, theirs)


def project_kernel(*refs, count, last, chunk, depth, has_before):
    step = pl.program_id(0)
    cols = refs[count]
    rest, weights = refs[count + 1 : -1], refs[-1]
    before = rest[0] if has_before else None
    half = cols.shape[3] // 2

    @pl.when(step == 0)
    def _():
        empty = jnp.zeros((depth, half), weights.dtype)
        for i in range(count):
            for z in range(2):
                own = cols[i, z, pl.ds(chunk * depth, depth), :]
                grad_rows = pl.ds(2 * z * depth, depth)
                out_rows = pl.ds((2 * z + 1) * depth, depth)
                weights[i, grad_rows, :half] = empty
                weights[i, grad_rows, half:] = own[:, half:]
                weights[i, out_rows, :half] = own[:, :half]
                weights[i, out_rows, half:] = empty

    value = jnp.dot(refs[0][...], weights[0], preferred_element_type=jnp.float32)
    for i in range(1, count):
        value += jnp.dot(refs[i][...], weights[i], preferred_element_type=jnp.float32)
    if before is not None:
        value += before[...]
    if last:
        rest[-2][...] = value[:, :half].astype(jnp.bfloat16)
        rest[-1][...] = value[:, half:].astype(jnp.bfloat16)
    else:
        rest[-1][...] = value


def project(pieces, cols, before, outs, last, chunk, part, parts):
    count = len(pieces)
    rows, depth = pieces[0].shape
    total_rows = rows * parts
    width = cols.shape[3]
    steps = 2
    tile = rows // steps
    rowwise = lambda w: pl.BlockSpec((tile, w), lambda i: (part * steps + i, 0))
    halves = jax.ShapeDtypeStruct((total_rows, width // 2), jnp.bfloat16)
    shapes = [halves] * 2 if last else [jax.ShapeDtypeStruct((total_rows, width), jnp.float32)]
    outs = list(outs or [])
    inputs = [*pieces, cols] + ([] if before is None else [before]) + outs
    return pl.pallas_call(
        functools.partial(
            project_kernel, count=count, last=last, chunk=chunk, depth=depth // 4,
            has_before=before is not None,
        ),
        grid=(steps,),
        in_specs=[pl.BlockSpec((tile, depth), lambda i: (i, 0))] * count
        + [pl.BlockSpec(cols.shape, lambda i: (0, 0, 0, 0))]
        + ([] if before is None else [rowwise(width)])
        + [pl.BlockSpec(memory_space=pl.ANY)] * len(outs),
        out_specs=[rowwise(width // 2)] * 2 if last else [rowwise(width)],
        scratch_shapes=[pltpu.VMEM((count, depth, width), jnp.bfloat16)],
        out_shape=shapes,
        input_output_aliases={len(inputs) - len(outs) + i: i for i in range(len(outs))},
        compiler_params=pltpu.CompilerParams(vmem_limit_bytes=40 << 20),
        cost_estimate=pl.CostEstimate(
            flops=2 * rows * depth * count * width,
            transcendentals=0,
            bytes_accessed=2 * rows * (depth * count + 2 * width),
        ),
    )(*inputs)


def swap(x, axis):
    return lax.ppermute(x, axis, [(0, 1), (1, 0)])


def first_hop(x, small):
    if small:
        return [x, swap(x, "y"), swap(x, "zl")]
    whole = lax.all_gather(x, ("zl", "y"), axis=0, tiled=False)
    return [whole[i] for i in range(whole.shape[0])]


def second_hop(pieces, small):
    if not small:
        return pieces
    x, by_y, by_zl = pieces
    cut = x.shape[0] // 2
    corner = jnp.concatenate([swap(by_y[:cut], "zl"), swap(by_zl[cut:], "y")], axis=0)
    return [x, by_y, by_zl, corner]


def scatter_sum(x, size, dim):
    index = lax.axis_index("dp")
    step = size // 2
    while step >= 1:
        half = x.shape[dim] // 2
        upper = (index // step) % 2
        keep = lax.dynamic_slice_in_dim(x, upper * half, half, dim)
        give = lax.dynamic_slice_in_dim(x, (1 - upper) * half, half, dim)
        got = lax.ppermute(
            give.astype(jnp.bfloat16), "dp", [(i, i ^ step) for i in range(size)]
        )
        x = keep + got.astype(jnp.float32)
        step //= 2
    return x


def local(
    patches, query_proj, output_proj, cache, block_lengths, neighbours, cotangent, *, sizes
):
    groups, zl_size, y_size = sizes
    inner = zl_size * y_size
    model = 2 * inner
    owner_count = groups * model
    group = lax.axis_index("dp")
    zh = lax.axis_index("zh")
    spot = lax.axis_index("zl") * y_size + lax.axis_index("y")
    me = group * model + zh * inner + spot
    local_blocks, block_rows, heads, width = cache.shape
    head_size = width // 2
    local_heads = query_proj.shape[1] // head_size
    features = patches.shape[1]
    columns = features // model
    slots = neighbours.shape[1]
    patch_blocks = neighbours.shape[0] // groups
    entry_count = patch_blocks * slots
    capacity = 2 * entry_count // owner_count
    row_count = patches.shape[0]
    head_scale = 1.0 / math.sqrt(head_size)
    grad_scale = 1.0 / math.sqrt(row_count * groups)

    all_ids = neighbours.reshape(groups, entry_count)
    match = all_ids // local_blocks == me
    order = jnp.arange(entry_count, dtype=jnp.int32)
    earlier = order[None, :] < order[:, None]
    rank = jnp.sum((match[:, None, :] & earlier[None]).astype(jnp.int32), axis=2)
    slot_range = jnp.arange(capacity, dtype=jnp.int32)
    placed = match[:, :, None] & (rank[:, :, None] == slot_range)
    chosen = jnp.sum(
        jnp.where(placed, (all_ids % local_blocks)[:, :, None], 0), axis=1
    ).reshape(groups * capacity)
    send_counts = jnp.sum(match.astype(jnp.int32), axis=1)

    def pack(c):
        return pack_blocks(
            chosen, send_counts, block_lengths, cache, c, groups, inner, capacity, local_heads
        ).reshape(groups * inner, capacity * 2 * block_rows, width)

    def exchange(x):
        return lax.all_to_all(
            x, ("dp", "zl", "y"), split_axis=0, concat_axis=0, tiled=True
        ).reshape(groups * inner * capacity, 2, block_rows, width)

    received = [exchange(pack(0))]
    q_other, o_other = swap(query_proj, "zh"), swap(output_proj, "zh")
    for c in range(1, local_heads):
        packed, q_other, o_other = lax.optimization_barrier((pack(c), q_other, o_other))
        received.append(exchange(packed))

    my_ids = lax.dynamic_slice_in_dim(
        neighbours, group * patch_blocks, patch_blocks, 0
    ).reshape(entry_count)
    owners = my_ids // local_blocks
    slot_of = jnp.sum(((owners[:, None] == owners[None, :]) & earlier).astype(jnp.int32), axis=1)
    source = (owners // model) * inner + owners % inner
    in_half = ((owners % model) // inner == zh).reshape(patch_blocks, slots)
    arrival = (source * capacity + slot_of).reshape(patch_blocks, slots)
    spots = jnp.arange(slots, dtype=jnp.int32)
    before = jnp.sum(
        (in_half[:, None, :] & (spots[None, :] < spots[:, None])[None]).astype(jnp.int32), axis=2
    )
    at = in_half[:, :, None] & (before[:, :, None] == spots)
    places = jnp.sum(jnp.where(at, arrival[:, :, None], 0), axis=1).reshape(entry_count)
    counts = jnp.sum(in_half.astype(jnp.int32), axis=1)

    marks = received[0][:, 0, block_rows - MARK_ROWS :, :].astype(jnp.float32)
    marks = marks[:, MARK_ROWS - 1, 0]
    rows_of = jnp.where(marks > MARK_LEAST, marks - MARK_BASE, float(block_rows)).astype(jnp.int32)
    arrivals = jnp.arange(rows_of.shape[0], dtype=jnp.int32)
    valid = jnp.sum(
        jnp.where(places[:, None] == arrivals[None, :], rows_of[None, :], 0), axis=1
    ).reshape(patch_blocks, slots)
    valid = jnp.where(spots[None, :] < counts[:, None], valid, 0)
    sizes_of = (valid + GRANULE - 1) // GRANULE
    offsets = jnp.sum(
        jnp.where(spots[None, None, :] < spots[None, :, None], sizes_of[:, None, :], 0), axis=2
    )
    tile_count = pl.cdiv(slots * block_rows, KEY_TILE)
    bias_shape = (patch_blocks, tile_count * KEY_TILE // LANES, LANES)
    key_at = LANES * lax.broadcasted_iota(jnp.int32, bias_shape, 1) + lax.broadcasted_iota(
        jnp.int32, bias_shape, 2
    )
    first_key = (offsets * GRANULE)[:, :, None, None]
    seen = (key_at[:, None] >= first_key) & (key_at[:, None] < first_key + valid[:, :, None, None])
    bias = jnp.where(jnp.any(seen, axis=1), 0.0, masked_value).astype(jnp.float32)
    tables = (places, counts, offsets.reshape(entry_count), sizes_of.reshape(entry_count))

    q_other, o_other, received[0] = lax.optimization_barrier(
        (q_other, o_other, received[0])
    )

    def both_halves(own, other):
        return jnp.where(zh == 0, own, other), jnp.where(zh == 0, other, own)

    q_both = both_halves(query_proj, q_other)
    q_wide = jnp.stack([w.reshape(features, local_heads, head_size) for w in q_both], axis=2)
    q_wide = jnp.pad(q_wide, ((0, 0), (0, 0), (0, 0), (0, LANES - head_size)))
    q_wide = q_wide.reshape(features, local_heads * 2 * LANES)
    o_both = both_halves(output_proj, o_other)
    o_wide = jnp.stack([w.reshape(local_heads, head_size, features) for w in o_both], axis=1)
    o_wide = jnp.pad(o_wide, ((0, 0), (0, 0), (LANES - head_size, 0), (0, 0)))
    o_wide = o_wide.reshape(local_heads * 2 * LANES, features)
    queries = (
        jnp.dot(patches, q_wide, preferred_element_type=jnp.float32) * head_scale
    ).astype(jnp.bfloat16)
    backs = nt_dot(cotangent, o_wide).astype(jnp.bfloat16)

    small = zl_size == 2 and y_size == 2
    own_width = local_heads * head_size
    o_blocks = jnp.stack(o_both).reshape(2, own_width, model, columns).transpose(2, 0, 1, 3)
    q_blocks = jnp.stack(q_both).reshape(2, model, columns, own_width).transpose(1, 0, 3, 2)
    blocks = lax.dynamic_slice_in_dim(
        jnp.concatenate([o_blocks, q_blocks], axis=3), zh * inner, inner, 0
    )

    part_count = 2 if patch_blocks % 2 == 0 else 1
    part_patches = patch_blocks // part_count
    gathered = []
    own = []
    cols = None
    for c in range(local_heads):
        final = c + 1 == local_heads
        if final:
            if c:
                blocks, _ = lax.optimization_barrier((blocks, mine))
            if small:
                cols = [lax.dynamic_index_in_dim(blocks, spot, 0, keepdims=False)] + [
                    lax.ppermute(
                        lax.dynamic_index_in_dim(blocks, spot ^ d, 0, keepdims=False),
                        ("zl", "y"),
                        [(i, i ^ d) for i in range(inner)],
                    )
                    for d in range(1, inner)
                ]
                cols = jnp.stack(cols)
            else:
                cols = lax.all_to_all(blocks, ("zl", "y"), split_axis=0, concat_axis=0, tiled=True)
            bias, cols = lax.optimization_barrier((bias, cols))
        outs, douts, mine = attention(
            tables, bias, queries, backs, received[c], c, slots, head_scale
        )
        theirs = swap(mine, "zh")
        parts = [
            merge(outs, douts, mine, theirs, start, part_patches, head_scale, head_size)
            for start in range(0, patch_blocks, part_patches)
        ]
        if gathered:
            gathered[-1], _ = lax.optimization_barrier((gathered[-1], parts))
            gathered[-1] = [second_hop(x, small) for x in gathered[-1]]
        if not final:
            parts, bias = lax.optimization_barrier((parts, bias))
        merged = []
        for part in parts:
            if final and merged:
                part, _ = lax.optimization_barrier((part, merged[-1]))
            other = swap(part, "zh").astype(jnp.float32)
            merged.append((part.astype(jnp.float32) + other).astype(jnp.bfloat16))
        gathered.append([first_hop(x, small) for x in merged])
        if final:
            results = None
            for i, earlier in enumerate(gathered[:-1]):
                before = results
                results = None
                for j, pieces in enumerate(earlier):
                    results = project(
                        pieces, cols, before[0] if before else None, results, False, i, j,
                        part_count,
                    )
            if results is not None:
                merged, _ = lax.optimization_barrier((merged, results))
        own.append(
            jnp.concatenate(
                [lax.dynamic_slice_in_dim(x, zh * LANES, LANES, 1) for x in merged], axis=0
            )
        )
    before = results[0] if results else None
    final_outs = None
    for j, pieces in enumerate(gathered[-1]):
        final_outs = project(
            second_hop(pieces, small), cols, before, final_outs, True, local_heads - 1, j,
            part_count,
        )
    attended, patch_grad = final_outs

    dquery = jnp.concatenate([x[:, :head_size] for x in own], axis=1)
    heads_out = jnp.concatenate([x[:, head_size:] for x in own], axis=1)
    query_term = (
        lax.dot_general(
            patches, dquery, (((0,), (0,)), ((), ())), preferred_element_type=jnp.float32
        )
        * grad_scale
    )
    output_term = (
        lax.dot_general(
            heads_out, cotangent, (((0,), (0,)), ((), ())), preferred_element_type=jnp.float32
        )
        * grad_scale
    )
    return (
        attended,
        patch_grad,
        scatter_sum(query_term, groups, 0),
        scatter_sum(output_term, groups, 1),
    )


def solution(mesh):
    groups, model = mesh.shape["dp"], mesh.shape["mp"]
    sizes = (groups, model // 4, 2)
    split = Mesh(
        mesh.devices.reshape(groups, 2, model // 4, 2), ("dp", "zh", "zl", "y")
    )
    mp = ("zh", "zl", "y")
    every = ("dp",) + mp
    return jax.shard_map(
        functools.partial(local, sizes=sizes),
        mesh=split,
        in_specs=(
            P("dp", None),
            P(None, mp),
            P(mp, None),
            P(every, None, None, None),
            P(every),
            P(),
            P("dp", None),
        ),
        out_specs=(P("dp", mp), P("dp", mp), P("dp", mp), P(mp, "dp")),
        check_vma=False,
    )
```

```python
import functools
import math

import jax
import jax.numpy as jnp
from jax import lax
from jax.experimental import pallas as pl
from jax.experimental.pallas import tpu as pltpu
from jax.sharding import Mesh
from jax.sharding import PartitionSpec as P

masked_value = -1e30
LANES = 128
MARK_ROWS = 16
MARK_BASE = 100.0
MARK_LEAST = 64.0
GRANULE = 32
KEY_TILE = 512


def pack_kernel(
    chosen, counts, lengths, cache_ref, out_ref, *, chunk, local_heads, inner, capacity
):
    slot = pl.program_id(0) * capacity + pl.program_id(1)

    @pl.when(pl.program_id(1) < counts[pl.program_id(0)])
    def _():
        by_head = pltpu.einshape("rhd->hrd", cache_ref[0])
        block_rows, width = by_head.shape[1:]
        valid = lengths[chosen[slot]]
        shape = (MARK_ROWS, width)
        corner = (lax.broadcasted_iota(jnp.int32, shape, 0) == MARK_ROWS - 1) & (
            lax.broadcasted_iota(jnp.int32, shape, 1) == 0
        )
        corner = corner & (valid < block_rows)
        mark = valid.astype(jnp.float32) + MARK_BASE
        for r in range(inner):
            for half in range(2):
                tile = by_head[(half * inner + r) * local_heads + chunk]
                out_ref[0, r, 0, half] = tile
                last = tile[block_rows - MARK_ROWS :].astype(jnp.float32)
                out_ref[0, r, 0, half, block_rows - MARK_ROWS :, :] = jnp.where(
                    corner, mark, last
                ).astype(jnp.bfloat16)


def pack_blocks(chosen, counts, lengths, cache, chunk, groups, inner, capacity, local_heads):
    _, block_rows, heads, width = cache.shape
    return pl.pallas_call(
        functools.partial(
            pack_kernel, chunk=chunk, local_heads=local_heads, inner=inner, capacity=capacity
        ),
        grid_spec=pltpu.PrefetchScalarGridSpec(
            num_scalar_prefetch=3,
            grid=(groups, capacity),
            in_specs=[
                pl.BlockSpec(
                    (1, block_rows, heads, width),
                    lambda g, s, ch, ct, ln: (ch[g * capacity + s], 0, 0, 0),
                )
            ],
            out_specs=pl.BlockSpec(
                (1, inner, 1, 2, block_rows, width),
                lambda g, s, ch, ct, ln: (g, 0, s, 0, 0, 0),
            ),
        ),
        out_shape=jax.ShapeDtypeStruct(
            (groups, inner, capacity, 2, block_rows, width), cache.dtype
        ),
        compiler_params=pltpu.CompilerParams(vmem_limit_bytes=32 << 20),
        cost_estimate=pl.CostEstimate(
            flops=0, transcendentals=0, bytes_accessed=groups * capacity * 2 * 262144
        ),
    )(chosen, counts, lengths, cache)


def nt_dot(left, right):
    return lax.dot_general(
        left, right, (((1,), (1,)), ((), ())), preferred_element_type=jnp.float32
    )


def attention_kernel(
    places, counts, offsets, sizes, q_ref, b_ref, bias_ref, recv_ref, co_ref, ds_ref, stat_ref,
    kv, scores, probs, top, acc, dacc, columns, sems, *, slots, scale,
):
    patch = pl.program_id(0)
    block_rows, width = recv_ref.shape[2:]
    steps = block_rows // GRANULE
    folds = KEY_TILE // LANES

    def each_copy(which, act):
        @pl.loop(0, counts[which])
        def _(j):
            entry = which * slots + j
            at = pl.multiple_of(offsets[entry] * GRANULE, GRANULE)
            for size in range(1, steps + 1):

                @pl.when(sizes[entry] == size)
                def _():
                    act(
                        pltpu.make_async_copy(
                            recv_ref.at[places[entry], :, pl.ds(0, size * GRANULE), :],
                            kv.at[which % 2, :, pl.ds(at, size * GRANULE), :],
                            sems.at[which % 2, j],
                        )
                    )

    @pl.when(patch == 0)
    def _():
        each_copy(patch, lambda copy: copy.start())

    @pl.when(patch + 1 < pl.num_programs(0))
    def _():
        each_copy(patch + 1, lambda copy: copy.start())

    filled = offsets[patch * slots + slots - 1] + sizes[patch * slots + slots - 1]
    per_tile = KEY_TILE // GRANULE
    tiles = jnp.maximum((filled + per_tile - 1) // per_tile, 1)

    @pl.loop(filled, tiles * per_tile)
    def _(g):
        kv[patch % 2, :, pl.ds(pl.multiple_of(g * GRANULE, GRANULE), GRANULE), :] = jnp.zeros(
            (2, GRANULE, width), kv.dtype
        )

    each_copy(patch, lambda copy: copy.wait())

    def key_tile(t, head):
        return kv[patch % 2, head, pl.ds(pl.multiple_of(t * KEY_TILE, KEY_TILE), KEY_TILE), :]

    rows = q_ref.shape[0]
    lanes = [pl.ds(head * LANES, LANES) for head in range(2)]
    top[...] = jnp.full_like(top, masked_value)
    acc[...] = jnp.zeros_like(acc)
    dacc[...] = jnp.zeros_like(dacc)

    @pl.loop(0, tiles)
    def _(t):
        for head in range(2):
            score = nt_dot(q_ref[:, lanes[head]], key_tile(t, head))
            best = top[head]
            for fold in range(folds):
                part = score[:, fold * LANES : (fold + 1) * LANES]
                part = part + bias_ref[0, pl.ds(t * folds + fold, 1), :]
                scores[head, t, :, fold * LANES : (fold + 1) * LANES] = part
                best = jnp.maximum(best, part)
            top[head] = best

    row_max = [jnp.max(top[head], axis=1, keepdims=True) for head in range(2)]
    ones = jnp.ones((KEY_TILE, LANES), jnp.bfloat16)

    @pl.loop(0, tiles)
    def _(t):
        for head in range(2):
            weights = jnp.exp(scores[head, t] - row_max[head]).astype(jnp.bfloat16)
            probs[head, t] = weights
            acc[head] += jnp.dot(
                weights,
                jnp.concatenate([key_tile(t, head), ones], axis=1),
                preferred_element_type=jnp.float32,
            )

    inverse, inner, stats = [], [], []
    for head in range(2):
        row_sum = acc[head, :, width : width + 1]
        inverse.append(1.0 / row_sum)
        outs = acc[head, :, :width] * inverse[head]
        co_ref[:, lanes[head]] = outs
        inner.append(
            jnp.sum(outs * b_ref[:, lanes[head]].astype(jnp.float32), axis=1, keepdims=True)
        )
        stats += [row_max[head] + jnp.log(row_sum), inner[head]]

    @pl.loop(0, tiles)
    def _(t):
        for head in range(2):
            dprobs = nt_dot(b_ref[:, lanes[head]], key_tile(t, head))
            dscores = (probs[head, t].astype(jnp.float32) * (dprobs - inner[head])).astype(
                jnp.bfloat16
            )
            dacc[head] += jnp.dot(dscores, key_tile(t, head), preferred_element_type=jnp.float32)

    for head in range(2):
        ds_ref[:, lanes[head]] = dacc[head] * (inverse[head] * scale)
    lane = lax.broadcasted_iota(jnp.int32, (rows, LANES), 1)
    columns[rows:, :] = jnp.zeros((columns.shape[0] - rows, LANES), jnp.float32)
    picked = jnp.where(lane == 0, stats[0], stats[1])
    picked = jnp.where(lane == 2, stats[2], picked)
    columns[:rows, :] = jnp.where(lane == 3, stats[3], picked)
    stat_ref[0] = jnp.transpose(columns[...])[:8]


def attention(tables, bias, queries, backs, received, chunk, slots, scale):
    patch_blocks = bias.shape[0]
    total_rows = queries.shape[0]
    rows = total_rows // patch_blocks
    padded = pl.cdiv(rows, LANES) * LANES
    block_rows, width = received.shape[2:]
    tiles = pl.cdiv(slots * block_rows, KEY_TILE)
    wide = pl.BlockSpec((rows, 2 * LANES), lambda p, *_: (p, chunk))
    out = pl.BlockSpec((rows, 2 * LANES), lambda p, *_: (p, 0))
    return pl.pallas_call(
        functools.partial(attention_kernel, slots=slots, scale=scale),
        grid_spec=pltpu.PrefetchScalarGridSpec(
            num_scalar_prefetch=4,
            grid=(patch_blocks,),
            in_specs=[
                wide,
                wide,
                pl.BlockSpec((1,) + bias.shape[1:], lambda p, *_: (p, 0, 0)),
                pl.BlockSpec(memory_space=pl.ANY),
            ],
            out_specs=[out, out, pl.BlockSpec((1, 8, padded), lambda p, *_: (p, 0, 0))],
            scratch_shapes=[
                pltpu.VMEM((2, 2, tiles * KEY_TILE, width), jnp.bfloat16),
                pltpu.VMEM((2, tiles, rows, KEY_TILE), jnp.float32),
                pltpu.VMEM((2, tiles, rows, KEY_TILE), jnp.bfloat16),
                pltpu.VMEM((2, rows, LANES), jnp.float32),
                pltpu.VMEM((2, rows, width + LANES), jnp.float32),
                pltpu.VMEM((2, rows, width), jnp.float32),
                pltpu.VMEM((padded, LANES), jnp.float32),
                pltpu.SemaphoreType.DMA((2, slots)),
            ],
        ),
        out_shape=[jax.ShapeDtypeStruct((total_rows, 2 * LANES), jnp.float32)] * 2
        + [jax.ShapeDtypeStruct((patch_blocks, 8, padded), jnp.float32)],
        compiler_params=pltpu.CompilerParams(vmem_limit_bytes=58 << 20),
        cost_estimate=pl.CostEstimate(
            flops=8 * total_rows * slots * block_rows * width,
            transcendentals=total_rows * slots * block_rows,
            bytes_accessed=40 << 20,
        ),
    )(*tables, queries, backs, bias, received)


def merge_kernel(co_ref, ds_ref, mine_ref, theirs_ref, out_ref, *, scale, split):
    rows = co_ref.shape[0]
    mine, theirs = mine_ref[0], theirs_ref[0]
    kind = lax.broadcasted_iota(jnp.int32, mine.shape, 0)
    gap = mine - theirs
    share = 1.0 / (1.0 + jnp.exp(-gap))
    rest = 1.0 / (1.0 + jnp.exp(gap))
    rest_below = jnp.concatenate([rest[:1], rest[:-1]], axis=0)
    table = jnp.where(kind % 2 == 0, share, rest_below * gap * scale)
    tall = jnp.transpose(
        jnp.concatenate([table, jnp.zeros((LANES - 8, table.shape[1]), jnp.float32)], axis=0)
    )[:rows]
    lower = lax.broadcasted_iota(jnp.int32, (rows, LANES), 1) < split
    for head in range(2):
        lanes = pl.ds(head * LANES, LANES)
        weight = tall[:, 2 * head : 2 * head + 1]
        shift = tall[:, 2 * head + 1 : 2 * head + 2]
        outs = co_ref[:, lanes]
        value = weight * jnp.where(lower, ds_ref[:, lanes] + shift * outs, outs)
        out_ref[:, lanes] = value.astype(jnp.bfloat16)


def merge(outs, douts, mine, theirs, first, count, scale, split):
    patch_blocks, _, padded = mine.shape
    rows = outs.shape[0] // patch_blocks
    wide = pl.BlockSpec((rows, 2 * LANES), lambda p: (first + p, 0))
    flat = pl.BlockSpec((1, 8, padded), lambda p: (first + p, 0, 0))
    return pl.pallas_call(
        functools.partial(merge_kernel, scale=scale, split=split),
        grid=(count,),
        in_specs=[wide, wide, flat, flat],
        out_specs=pl.BlockSpec((rows, 2 * LANES), lambda p: (p, 0)),
        out_shape=jax.ShapeDtypeStruct((count * rows, 2 * LANES), jnp.bfloat16),
        cost_estimate=pl.CostEstimate(
            flops=20 * count * rows * LANES,
            transcendentals=0,
            bytes_accessed=20 * count * rows * LANES,
        ),
    )(outs, douts, mine, theirs)


def project_kernel(*refs, count, chunk, depth, has_before):
    cols = refs[count]
    before = refs[count + 1] if has_before else None
    out, weights = refs[-2], refs[-1]
    dests, width = cols.shape[1], cols.shape[4]
    half = width // 2
    empty = jnp.zeros((depth, half), weights.dtype)
    for i in range(count):
        for dest in range(dests):
            low = pl.ds(dest * width, half)
            high = pl.ds(dest * width + half, half)
            for z in range(2):
                own = cols[i, dest, z, pl.ds(chunk * depth, depth), :]
                grad_rows = pl.ds(2 * z * depth, depth)
                out_rows = pl.ds((2 * z + 1) * depth, depth)
                weights[i, grad_rows, low] = empty
                weights[i, grad_rows, high] = own[:, half:]
                weights[i, out_rows, low] = own[:, :half]
                weights[i, out_rows, high] = empty
    for dest in range(dests):
        lanes = pl.ds(dest * width, width)
        value = jnp.dot(refs[0][...], weights[0, :, lanes], preferred_element_type=jnp.float32)
        for i in range(1, count):
            value += jnp.dot(
                refs[i][...], weights[i, :, lanes], preferred_element_type=jnp.float32
            )
        if has_before:
            value += before[dest]
        out[dest] = value.astype(out.dtype)


def project(pieces, cols, before, last, chunk):
    count = len(pieces)
    rows, depth = pieces[0].shape
    dests, width = cols.shape[1], cols.shape[4]
    inputs = [*pieces, cols] + ([] if before is None else [before])
    return pl.pallas_call(
        functools.partial(
            project_kernel, count=count, chunk=chunk, depth=depth // 4,
            has_before=before is not None,
        ),
        out_shape=jax.ShapeDtypeStruct(
            (dests, rows, width), jnp.bfloat16 if last else jnp.float32
        ),
        scratch_shapes=[pltpu.VMEM((count, depth, dests * width), jnp.bfloat16)],
        compiler_params=pltpu.CompilerParams(vmem_limit_bytes=40 << 20),
        cost_estimate=pl.CostEstimate(
            flops=2 * rows * depth * count * width * dests,
            transcendentals=0,
            bytes_accessed=2 * rows * (depth * count + 2 * width) + 2 * cols.size,
        ),
    )(*inputs)


def swap(x, axis):
    return lax.ppermute(x, axis, [(0, 1), (1, 0)])


def trade(blocks, spot, small):
    count = blocks.shape[0]
    if not small:
        whole = lax.all_to_all(blocks, ("zl", "y"), split_axis=0, concat_axis=0, tiled=True)
        return [whole[i] for i in range(count)]
    return [
        across(lax.dynamic_index_in_dim(blocks, spot ^ d, 0, keepdims=False), d, count)
        for d in range(count)
    ]


def across(x, d, count):
    if d == 0:
        return x
    return lax.ppermute(x, ("zl", "y"), [(i, i ^ d) for i in range(count)])


def in_order(pieces, spot, small):
    if not small:
        return pieces
    low, high = spot % 2 == 1, spot // 2 == 1
    return [
        jnp.where(
            high,
            jnp.where(low, pieces[i ^ 3], pieces[i ^ 2]),
            jnp.where(low, pieces[i ^ 1], pieces[i]),
        )
        for i in range(len(pieces))
    ]


def scatter_sum(x, size, dim):
    index = lax.axis_index("dp")
    step = size // 2
    while step >= 1:
        half = x.shape[dim] // 2
        upper = (index // step) % 2
        keep = lax.dynamic_slice_in_dim(x, upper * half, half, dim)
        give = lax.dynamic_slice_in_dim(x, (1 - upper) * half, half, dim)
        got = lax.ppermute(
            give.astype(jnp.bfloat16), "dp", [(i, i ^ step) for i in range(size)]
        )
        x = keep + got.astype(jnp.float32)
        step //= 2
    return x


def local(
    patches, query_proj, output_proj, cache, block_lengths, neighbours, cotangent, *, sizes
):
    groups, zl_size, y_size = sizes
    inner = zl_size * y_size
    model = 2 * inner
    owner_count = groups * model
    group = lax.axis_index("dp")
    zh = lax.axis_index("zh")
    spot = lax.axis_index("zl") * y_size + lax.axis_index("y")
    me = group * model + zh * inner + spot
    local_blocks, block_rows, heads, width = cache.shape
    head_size = width // 2
    local_heads = query_proj.shape[1] // head_size
    features = patches.shape[1]
    columns = features // model
    slots = neighbours.shape[1]
    patch_blocks = neighbours.shape[0] // groups
    entry_count = patch_blocks * slots
    capacity = 2 * entry_count // owner_count
    row_count = patches.shape[0]
    head_scale = 1.0 / math.sqrt(head_size)
    grad_scale = 1.0 / math.sqrt(row_count * groups)

    all_ids = neighbours.reshape(groups, entry_count)
    match = all_ids // local_blocks == me
    order = jnp.arange(entry_count, dtype=jnp.int32)
    earlier = order[None, :] < order[:, None]
    rank = jnp.sum((match[:, None, :] & earlier[None]).astype(jnp.int32), axis=2)
    slot_range = jnp.arange(capacity, dtype=jnp.int32)
    placed = match[:, :, None] & (rank[:, :, None] == slot_range)
    chosen = jnp.sum(
        jnp.where(placed, (all_ids % local_blocks)[:, :, None], 0), axis=1
    ).reshape(groups * capacity)
    send_counts = jnp.sum(match.astype(jnp.int32), axis=1)

    def pack(c):
        return pack_blocks(
            chosen, send_counts, block_lengths, cache, c, groups, inner, capacity, local_heads
        ).reshape(groups * inner, capacity * 2 * block_rows, width)

    def exchange(x):
        return lax.all_to_all(
            x, ("dp", "zl", "y"), split_axis=0, concat_axis=0, tiled=True
        ).reshape(groups * inner * capacity, 2, block_rows, width)

    received = [exchange(pack(0))]
    q_other, o_other = swap(query_proj, "zh"), swap(output_proj, "zh")
    for c in range(1, local_heads):
        packed, q_other, o_other = lax.optimization_barrier((pack(c), q_other, o_other))
        received.append(exchange(packed))

    my_ids = lax.dynamic_slice_in_dim(
        neighbours, group * patch_blocks, patch_blocks, 0
    ).reshape(entry_count)
    owners = my_ids // local_blocks
    slot_of = jnp.sum(((owners[:, None] == owners[None, :]) & earlier).astype(jnp.int32), axis=1)
    source = (owners // model) * inner + owners % inner
    in_half = ((owners % model) // inner == zh).reshape(patch_blocks, slots)
    arrival = (source * capacity + slot_of).reshape(patch_blocks, slots)
    spots = jnp.arange(slots, dtype=jnp.int32)
    before = jnp.sum(
        (in_half[:, None, :] & (spots[None, :] < spots[:, None])[None]).astype(jnp.int32), axis=2
    )
    at = in_half[:, :, None] & (before[:, :, None] == spots)
    places = jnp.sum(jnp.where(at, arrival[:, :, None], 0), axis=1).reshape(entry_count)
    counts = jnp.sum(in_half.astype(jnp.int32), axis=1)

    marks = received[0][:, 0, block_rows - MARK_ROWS :, :].astype(jnp.float32)
    marks = marks[:, MARK_ROWS - 1, 0]
    rows_of = jnp.where(marks > MARK_LEAST, marks - MARK_BASE, float(block_rows)).astype(jnp.int32)
    arrivals = jnp.arange(rows_of.shape[0], dtype=jnp.int32)
    valid = jnp.sum(
        jnp.where(places[:, None] == arrivals[None, :], rows_of[None, :], 0), axis=1
    ).reshape(patch_blocks, slots)
    valid = jnp.where(spots[None, :] < counts[:, None], valid, 0)
    sizes_of = (valid + GRANULE - 1) // GRANULE
    offsets = jnp.sum(
        jnp.where(spots[None, None, :] < spots[None, :, None], sizes_of[:, None, :], 0), axis=2
    )
    tile_count = pl.cdiv(slots * block_rows, KEY_TILE)
    bias_shape = (patch_blocks, tile_count * KEY_TILE // LANES, LANES)
    key_at = LANES * lax.broadcasted_iota(jnp.int32, bias_shape, 1) + lax.broadcasted_iota(
        jnp.int32, bias_shape, 2
    )
    first_key = (offsets * GRANULE)[:, :, None, None]
    seen = (key_at[:, None] >= first_key) & (key_at[:, None] < first_key + valid[:, :, None, None])
    bias = jnp.where(jnp.any(seen, axis=1), 0.0, masked_value).astype(jnp.float32)
    tables = (places, counts, offsets.reshape(entry_count), sizes_of.reshape(entry_count))

    q_other, o_other, received[0] = lax.optimization_barrier(
        (q_other, o_other, received[0])
    )

    def both_halves(own, other):
        return jnp.where(zh == 0, own, other), jnp.where(zh == 0, other, own)

    q_both = both_halves(query_proj, q_other)
    q_wide = jnp.stack([w.reshape(features, local_heads, head_size) for w in q_both], axis=2)
    q_wide = jnp.pad(q_wide, ((0, 0), (0, 0), (0, 0), (0, LANES - head_size)))
    q_wide = q_wide.reshape(features, local_heads * 2 * LANES)
    o_both = both_halves(output_proj, o_other)
    o_wide = jnp.stack([w.reshape(local_heads, head_size, features) for w in o_both], axis=1)
    o_wide = jnp.pad(o_wide, ((0, 0), (0, 0), (LANES - head_size, 0), (0, 0)))
    o_wide = o_wide.reshape(local_heads * 2 * LANES, features)
    queries = (
        jnp.dot(patches, q_wide, preferred_element_type=jnp.float32) * head_scale
    ).astype(jnp.bfloat16)
    backs = nt_dot(cotangent, o_wide).astype(jnp.bfloat16)

    small = zl_size == 2 and y_size == 2
    own_width = local_heads * head_size
    o_blocks = jnp.stack(o_both).reshape(2, own_width, model, columns).transpose(2, 0, 1, 3)
    q_blocks = jnp.stack(q_both).reshape(2, model, columns, own_width).transpose(1, 0, 3, 2)
    blocks = lax.dynamic_slice_in_dim(
        jnp.concatenate([o_blocks, q_blocks], axis=3), zh * inner, inner, 0
    )

    part_count = 2 if patch_blocks % 2 == 0 else 1
    part_patches = patch_blocks // part_count
    results = [None] * part_count
    traded = []
    own = []
    for c in range(local_heads):
        final = c + 1 == local_heads
        if final:
            if c:
                blocks, _ = lax.optimization_barrier((blocks, mine))
            if small:
                cols = jnp.stack([across(blocks, d, inner) for d in range(inner)])
            else:
                cols = lax.all_gather(blocks, ("zl", "y"), axis=0, tiled=False)
        outs, douts, mine = attention(
            tables, bias, queries, backs, received[c], c, slots, head_scale
        )
        theirs = swap(mine, "zh")
        parts = [
            merge(outs, douts, mine, theirs, start, part_patches, head_scale, head_size)
            for start in range(0, patch_blocks, part_patches)
        ]
        if not final:
            parts, bias = lax.optimization_barrier((parts, bias))
        merged = []
        for part in parts:
            if final and merged:
                part, _ = lax.optimization_barrier((part, merged[-1]))
            other = swap(part, "zh").astype(jnp.float32)
            merged.append((part.astype(jnp.float32) + other).astype(jnp.bfloat16))
        by_rows = [
            trade(x.reshape(inner, x.shape[0] // inner, x.shape[1]), spot, small) for x in merged
        ]
        if not final:
            traded.append(by_rows)
            own.append(merged)
            continue
        for i, earlier in enumerate(traded):
            results = [
                project(pieces, cols, before, False, i)
                for pieces, before in zip(earlier, results)
            ]
        behind = merged
        if traded:
            behind, _ = lax.optimization_barrier((merged, results))
        own.append(behind)
        outputs = []
        for pieces, before in zip(by_rows, results):
            outputs += in_order(trade(project(pieces, cols, before, True, c), spot, small), spot, small)
    attended = jnp.concatenate([x[:, :columns] for x in outputs], axis=0)
    patch_grad = jnp.concatenate([x[:, columns:] for x in outputs], axis=0)
    own = [
        jnp.concatenate([lax.dynamic_slice_in_dim(x, zh * LANES, LANES, 1) for x in xs], axis=0)
        for xs in own
    ]

    dquery = jnp.concatenate([x[:, :head_size] for x in own], axis=1)
    heads_out = jnp.concatenate([x[:, head_size:] for x in own], axis=1)
    query_term = (
        lax.dot_general(
            patches, dquery, (((0,), (0,)), ((), ())), preferred_element_type=jnp.float32
        )
        * grad_scale
    )
    output_term = (
        lax.dot_general(
            heads_out, cotangent, (((0,), (0,)), ((), ())), preferred_element_type=jnp.float32
        )
        * grad_scale
    )
    return (
        attended,
        patch_grad,
        scatter_sum(query_term, groups, 0),
        scatter_sum(output_term, groups, 1),
    )


def solution(mesh):
    groups, model = mesh.shape["dp"], mesh.shape["mp"]
    sizes = (groups, model // 4, 2)
    split = Mesh(
        mesh.devices.reshape(groups, 2, model // 4, 2), ("dp", "zh", "zl", "y")
    )
    mp = ("zh", "zl", "y")
    every = ("dp",) + mp
    return jax.shard_map(
        functools.partial(local, sizes=sizes),
        mesh=split,
        in_specs=(
            P("dp", None),
            P(None, mp),
            P(mp, None),
            P(every, None, None, None),
            P(every),
            P(),
            P("dp", None),
        ),
        out_specs=(P("dp", mp), P("dp", mp), P("dp", mp), P(mp, "dp")),
        check_vma=False,
    )
```

```python
import functools
import math

import jax
import jax.numpy as jnp
from jax import lax
from jax.experimental import pallas as pl
from jax.experimental.pallas import tpu as pltpu
from jax.sharding import Mesh
from jax.sharding import PartitionSpec as P

masked_value = -1e30
LANES = 128
MARK_ROWS = 16
MARK_BASE = 100.0
MARK_LEAST = 64.0
GRANULE = 32
KEY_TILE = 512


def pack_kernel(
    chosen, counts, lengths, cache_ref, out_ref, *, chunk, local_heads, inner, capacity
):
    slot = pl.program_id(0) * capacity + pl.program_id(1)

    @pl.when(pl.program_id(1) < counts[pl.program_id(0)])
    def _():
        by_head = pltpu.einshape("rhd->hrd", cache_ref[0])
        block_rows, width = by_head.shape[1:]
        valid = lengths[chosen[slot]]
        shape = (MARK_ROWS, width)
        corner = (lax.broadcasted_iota(jnp.int32, shape, 0) == MARK_ROWS - 1) & (
            lax.broadcasted_iota(jnp.int32, shape, 1) == 0
        )
        corner = corner & (valid < block_rows)
        mark = valid.astype(jnp.float32) + MARK_BASE
        for r in range(inner):
            for half in range(2):
                tile = by_head[(half * inner + r) * local_heads + chunk]
                out_ref[0, r, 0, half] = tile
                last = tile[block_rows - MARK_ROWS :].astype(jnp.float32)
                out_ref[0, r, 0, half, block_rows - MARK_ROWS :, :] = jnp.where(
                    corner, mark, last
                ).astype(jnp.bfloat16)


def pack_blocks(chosen, counts, lengths, cache, chunk, groups, inner, capacity, local_heads):
    _, block_rows, heads, width = cache.shape
    return pl.pallas_call(
        functools.partial(
            pack_kernel, chunk=chunk, local_heads=local_heads, inner=inner, capacity=capacity
        ),
        grid_spec=pltpu.PrefetchScalarGridSpec(
            num_scalar_prefetch=3,
            grid=(groups, capacity),
            in_specs=[
                pl.BlockSpec(
                    (1, block_rows, heads, width),
                    lambda g, s, ch, ct, ln: (ch[g * capacity + s], 0, 0, 0),
                )
            ],
            out_specs=pl.BlockSpec(
                (1, inner, 1, 2, block_rows, width),
                lambda g, s, ch, ct, ln: (g, 0, s, 0, 0, 0),
            ),
        ),
        out_shape=jax.ShapeDtypeStruct(
            (groups, inner, capacity, 2, block_rows, width), cache.dtype
        ),
        compiler_params=pltpu.CompilerParams(vmem_limit_bytes=32 << 20),
        cost_estimate=pl.CostEstimate(
            flops=0, transcendentals=0, bytes_accessed=groups * capacity * 2 * 262144
        ),
    )(chosen, counts, lengths, cache)


def nt_dot(left, right):
    return lax.dot_general(
        left, right, (((1,), (1,)), ((), ())), preferred_element_type=jnp.float32
    )


def attention_kernel(
    places, counts, offsets, sizes, q_ref, b_ref, bias_ref, recv_ref, co_ref, ds_ref, stat_ref,
    kv, scores, probs, top, acc, dacc, columns, sems, *, slots, scale,
):
    patch = pl.program_id(0)
    block_rows, width = recv_ref.shape[2:]
    steps = block_rows // GRANULE
    folds = KEY_TILE // LANES

    def each_copy(which, act):
        @pl.loop(0, counts[which])
        def _(j):
            entry = which * slots + j
            at = pl.multiple_of(offsets[entry] * GRANULE, GRANULE)
            for size in range(1, steps + 1):

                @pl.when(sizes[entry] == size)
                def _():
                    act(
                        pltpu.make_async_copy(
                            recv_ref.at[places[entry], :, pl.ds(0, size * GRANULE), :],
                            kv.at[which % 2, :, pl.ds(at, size * GRANULE), :],
                            sems.at[which % 2, j],
                        )
                    )

    @pl.when(patch == 0)
    def _():
        each_copy(patch, lambda copy: copy.start())

    @pl.when(patch + 1 < pl.num_programs(0))
    def _():
        each_copy(patch + 1, lambda copy: copy.start())

    filled = offsets[patch * slots + slots - 1] + sizes[patch * slots + slots - 1]
    per_tile = KEY_TILE // GRANULE
    tiles = jnp.maximum((filled + per_tile - 1) // per_tile, 1)

    @pl.loop(filled, tiles * per_tile)
    def _(g):
        kv[patch % 2, :, pl.ds(pl.multiple_of(g * GRANULE, GRANULE), GRANULE), :] = jnp.zeros(
            (2, GRANULE, width), kv.dtype
        )

    each_copy(patch, lambda copy: copy.wait())

    def key_tile(t, head):
        return kv[patch % 2, head, pl.ds(pl.multiple_of(t * KEY_TILE, KEY_TILE), KEY_TILE), :]

    rows = q_ref.shape[0]
    lanes = [pl.ds(head * LANES, LANES) for head in range(2)]
    top[...] = jnp.full_like(top, masked_value)
    acc[...] = jnp.zeros_like(acc)
    dacc[...] = jnp.zeros_like(dacc)

    @pl.loop(0, tiles)
    def _(t):
        for head in range(2):
            score = nt_dot(q_ref[:, lanes[head]], key_tile(t, head))
            best = top[head]
            for fold in range(folds):
                part = score[:, fold * LANES : (fold + 1) * LANES]
                part = part + bias_ref[0, pl.ds(t * folds + fold, 1), :]
                scores[head, t, :, fold * LANES : (fold + 1) * LANES] = part
                best = jnp.maximum(best, part)
            top[head] = best

    row_max = [jnp.max(top[head], axis=1, keepdims=True) for head in range(2)]
    ones = jnp.ones((KEY_TILE, LANES), jnp.bfloat16)

    @pl.loop(0, tiles)
    def _(t):
        for head in range(2):
            weights = jnp.exp(scores[head, t] - row_max[head]).astype(jnp.bfloat16)
            probs[head, t] = weights
            acc[head] += jnp.dot(
                weights,
                jnp.concatenate([key_tile(t, head), ones], axis=1),
                preferred_element_type=jnp.float32,
            )

    inverse, inner, stats = [], [], []
    for head in range(2):
        row_sum = acc[head, :, width : width + 1]
        inverse.append(1.0 / row_sum)
        outs = acc[head, :, :width] * inverse[head]
        co_ref[:, lanes[head]] = outs
        inner.append(
            jnp.sum(outs * b_ref[:, lanes[head]].astype(jnp.float32), axis=1, keepdims=True)
        )
        stats += [row_max[head] + jnp.log(row_sum), inner[head]]

    @pl.loop(0, tiles)
    def _(t):
        for head in range(2):
            dprobs = nt_dot(b_ref[:, lanes[head]], key_tile(t, head))
            dscores = (probs[head, t].astype(jnp.float32) * (dprobs - inner[head])).astype(
                jnp.bfloat16
            )
            dacc[head] += jnp.dot(dscores, key_tile(t, head), preferred_element_type=jnp.float32)

    for head in range(2):
        ds_ref[:, lanes[head]] = dacc[head] * (inverse[head] * scale)
    lane = lax.broadcasted_iota(jnp.int32, (rows, LANES), 1)
    columns[rows:, :] = jnp.zeros((columns.shape[0] - rows, LANES), jnp.float32)
    picked = jnp.where(lane == 0, stats[0], stats[1])
    picked = jnp.where(lane == 2, stats[2], picked)
    columns[:rows, :] = jnp.where(lane == 3, stats[3], picked)
    stat_ref[0] = jnp.transpose(columns[...])[:8]


def attention(tables, bias, queries, backs, received, chunk, slots, scale):
    patch_blocks = bias.shape[0]
    total_rows = queries.shape[0]
    rows = total_rows // patch_blocks
    padded = pl.cdiv(rows, LANES) * LANES
    block_rows, width = received.shape[2:]
    tiles = pl.cdiv(slots * block_rows, KEY_TILE)
    wide = pl.BlockSpec((rows, 2 * LANES), lambda p, *_: (p, chunk))
    out = pl.BlockSpec((rows, 2 * LANES), lambda p, *_: (p, 0))
    return pl.pallas_call(
        functools.partial(attention_kernel, slots=slots, scale=scale),
        grid_spec=pltpu.PrefetchScalarGridSpec(
            num_scalar_prefetch=4,
            grid=(patch_blocks,),
            in_specs=[
                wide,
                wide,
                pl.BlockSpec((1,) + bias.shape[1:], lambda p, *_: (p, 0, 0)),
                pl.BlockSpec(memory_space=pl.ANY),
            ],
            out_specs=[out, out, pl.BlockSpec((1, 8, padded), lambda p, *_: (p, 0, 0))],
            scratch_shapes=[
                pltpu.VMEM((2, 2, tiles * KEY_TILE, width), jnp.bfloat16),
                pltpu.VMEM((2, tiles, rows, KEY_TILE), jnp.float32),
                pltpu.VMEM((2, tiles, rows, KEY_TILE), jnp.bfloat16),
                pltpu.VMEM((2, rows, LANES), jnp.float32),
                pltpu.VMEM((2, rows, width + LANES), jnp.float32),
                pltpu.VMEM((2, rows, width), jnp.float32),
                pltpu.VMEM((padded, LANES), jnp.float32),
                pltpu.SemaphoreType.DMA((2, slots)),
            ],
        ),
        out_shape=[jax.ShapeDtypeStruct((total_rows, 2 * LANES), jnp.float32)] * 2
        + [jax.ShapeDtypeStruct((patch_blocks, 8, padded), jnp.float32)],
        compiler_params=pltpu.CompilerParams(vmem_limit_bytes=58 << 20),
        cost_estimate=pl.CostEstimate(
            flops=8 * total_rows * slots * block_rows * width,
            transcendentals=total_rows * slots * block_rows,
            bytes_accessed=40 << 20,
        ),
    )(*tables, queries, backs, bias, received)


def merge_kernel(co_ref, ds_ref, mine_ref, theirs_ref, out_ref, *, scale, split):
    rows = co_ref.shape[0]
    mine, theirs = mine_ref[0], theirs_ref[0]
    kind = lax.broadcasted_iota(jnp.int32, mine.shape, 0)
    gap = mine - theirs
    share = 1.0 / (1.0 + jnp.exp(-gap))
    rest = 1.0 / (1.0 + jnp.exp(gap))
    rest_below = jnp.concatenate([rest[:1], rest[:-1]], axis=0)
    table = jnp.where(kind % 2 == 0, share, rest_below * gap * scale)
    tall = jnp.transpose(
        jnp.concatenate([table, jnp.zeros((LANES - 8, table.shape[1]), jnp.float32)], axis=0)
    )[:rows]
    lower = lax.broadcasted_iota(jnp.int32, (rows, LANES), 1) < split
    for head in range(2):
        lanes = pl.ds(head * LANES, LANES)
        weight = tall[:, 2 * head : 2 * head + 1]
        shift = tall[:, 2 * head + 1 : 2 * head + 2]
        outs = co_ref[:, lanes]
        value = weight * jnp.where(lower, ds_ref[:, lanes] + shift * outs, outs)
        out_ref[:, lanes] = value.astype(jnp.bfloat16)


def merge(outs, douts, mine, theirs, first, count, scale, split):
    patch_blocks, _, padded = mine.shape
    rows = outs.shape[0] // patch_blocks
    wide = pl.BlockSpec((rows, 2 * LANES), lambda p: (first + p, 0))
    flat = pl.BlockSpec((1, 8, padded), lambda p: (first + p, 0, 0))
    return pl.pallas_call(
        functools.partial(merge_kernel, scale=scale, split=split),
        grid=(count,),
        in_specs=[wide, wide, flat, flat],
        out_specs=pl.BlockSpec((rows, 2 * LANES), lambda p: (p, 0)),
        out_shape=jax.ShapeDtypeStruct((count * rows, 2 * LANES), jnp.bfloat16),
        cost_estimate=pl.CostEstimate(
            flops=20 * count * rows * LANES,
            transcendentals=0,
            bytes_accessed=20 * count * rows * LANES,
        ),
    )(outs, douts, mine, theirs)


def project_kernel(*refs, count, chunk, depth, has_before):
    cols = refs[count]
    before = refs[count + 1] if has_before else None
    out, weights = refs[-2], refs[-1]
    dests, width = cols.shape[1], cols.shape[4]
    half = width // 2
    empty = jnp.zeros((depth, half), weights.dtype)
    for i in range(count):
        for dest in range(dests):
            low = pl.ds(dest * width, half)
            high = pl.ds(dest * width + half, half)
            for z in range(2):
                own = cols[i, dest, z, pl.ds(chunk * depth, depth), :]
                grad_rows = pl.ds(2 * z * depth, depth)
                out_rows = pl.ds((2 * z + 1) * depth, depth)
                weights[i, grad_rows, low] = empty
                weights[i, grad_rows, high] = own[:, half:]
                weights[i, out_rows, low] = own[:, :half]
                weights[i, out_rows, high] = empty
    for dest in range(dests):
        lanes = pl.ds(dest * width, width)
        value = jnp.dot(refs[0][...], weights[0, :, lanes], preferred_element_type=jnp.float32)
        for i in range(1, count):
            value += jnp.dot(
                refs[i][...], weights[i, :, lanes], preferred_element_type=jnp.float32
            )
        if has_before:
            value += before[dest]
        out[dest] = value.astype(out.dtype)


def project(pieces, cols, before, last, chunk):
    count = len(pieces)
    rows, depth = pieces[0].shape
    dests, width = cols.shape[1], cols.shape[4]
    inputs = [*pieces, cols] + ([] if before is None else [before])
    return pl.pallas_call(
        functools.partial(
            project_kernel, count=count, chunk=chunk, depth=depth // 4,
            has_before=before is not None,
        ),
        out_shape=jax.ShapeDtypeStruct(
            (dests, rows, width), jnp.bfloat16 if last else jnp.float32
        ),
        scratch_shapes=[pltpu.VMEM((count, depth, dests * width), jnp.bfloat16)],
        compiler_params=pltpu.CompilerParams(vmem_limit_bytes=40 << 20),
        cost_estimate=pl.CostEstimate(
            flops=2 * rows * depth * count * width * dests,
            transcendentals=0,
            bytes_accessed=2 * rows * (depth * count + 2 * width) + 2 * cols.size,
        ),
    )(*inputs)


def swap(x, axis):
    return lax.ppermute(x, axis, [(0, 1), (1, 0)])


def trade(blocks, spot, small):
    count = blocks.shape[0]
    if not small:
        whole = lax.all_to_all(blocks, ("zl", "y"), split_axis=0, concat_axis=0, tiled=True)
        return [whole[i] for i in range(count)]
    return [
        across(lax.dynamic_index_in_dim(blocks, spot ^ d, 0, keepdims=False), d, count)
        for d in range(count)
    ]


def across(x, d, count):
    if d == 0:
        return x
    return lax.ppermute(x, ("zl", "y"), [(i, i ^ d) for i in range(count)])


def in_order(pieces, spot, small):
    if not small:
        return pieces
    low, high = spot % 2 == 1, spot // 2 == 1
    return [
        jnp.where(
            high,
            jnp.where(low, pieces[i ^ 3], pieces[i ^ 2]),
            jnp.where(low, pieces[i ^ 1], pieces[i]),
        )
        for i in range(len(pieces))
    ]


def scatter_sum(x, size, dim):
    index = lax.axis_index("dp")
    step = size // 2
    while step >= 1:
        half = x.shape[dim] // 2
        upper = (index // step) % 2
        keep = lax.dynamic_slice_in_dim(x, upper * half, half, dim)
        give = lax.dynamic_slice_in_dim(x, (1 - upper) * half, half, dim)
        got = lax.ppermute(
            give.astype(jnp.bfloat16), "dp", [(i, i ^ step) for i in range(size)]
        )
        x = keep + got.astype(jnp.float32)
        step //= 2
    return x


def local(
    patches, query_proj, output_proj, cache, block_lengths, neighbours, cotangent, *, sizes
):
    groups, zl_size, y_size = sizes
    inner = zl_size * y_size
    model = 2 * inner
    owner_count = groups * model
    group = lax.axis_index("dp")
    zh = lax.axis_index("zh")
    spot = lax.axis_index("zl") * y_size + lax.axis_index("y")
    me = group * model + zh * inner + spot
    local_blocks, block_rows, heads, width = cache.shape
    head_size = width // 2
    local_heads = query_proj.shape[1] // head_size
    features = patches.shape[1]
    columns = features // model
    slots = neighbours.shape[1]
    patch_blocks = neighbours.shape[0] // groups
    entry_count = patch_blocks * slots
    capacity = 2 * entry_count // owner_count
    row_count = patches.shape[0]
    head_scale = 1.0 / math.sqrt(head_size)
    grad_scale = 1.0 / math.sqrt(row_count * groups)

    all_ids = neighbours.reshape(groups, entry_count)
    match = all_ids // local_blocks == me
    order = jnp.arange(entry_count, dtype=jnp.int32)
    earlier = order[None, :] < order[:, None]
    rank = jnp.sum((match[:, None, :] & earlier[None]).astype(jnp.int32), axis=2)
    slot_range = jnp.arange(capacity, dtype=jnp.int32)
    placed = match[:, :, None] & (rank[:, :, None] == slot_range)
    chosen = jnp.sum(
        jnp.where(placed, (all_ids % local_blocks)[:, :, None], 0), axis=1
    ).reshape(groups * capacity)
    send_counts = jnp.sum(match.astype(jnp.int32), axis=1)

    def pack(c):
        return pack_blocks(
            chosen, send_counts, block_lengths, cache, c, groups, inner, capacity, local_heads
        ).reshape(groups * inner, capacity * 2 * block_rows, width)

    def exchange(x):
        return lax.all_to_all(
            x, ("dp", "zl", "y"), split_axis=0, concat_axis=0, tiled=True
        ).reshape(groups * inner * capacity, 2, block_rows, width)

    received = [exchange(pack(0))]
    q_other, o_other = swap(query_proj, "zh"), swap(output_proj, "zh")
    for c in range(1, local_heads):
        packed, q_other, o_other = lax.optimization_barrier((pack(c), q_other, o_other))
        received.append(exchange(packed))

    my_ids = lax.dynamic_slice_in_dim(
        neighbours, group * patch_blocks, patch_blocks, 0
    ).reshape(entry_count)
    owners = my_ids // local_blocks
    slot_of = jnp.sum(((owners[:, None] == owners[None, :]) & earlier).astype(jnp.int32), axis=1)
    source = (owners // model) * inner + owners % inner
    in_half = ((owners % model) // inner == zh).reshape(patch_blocks, slots)
    arrival = (source * capacity + slot_of).reshape(patch_blocks, slots)
    spots = jnp.arange(slots, dtype=jnp.int32)
    before = jnp.sum(
        (in_half[:, None, :] & (spots[None, :] < spots[:, None])[None]).astype(jnp.int32), axis=2
    )
    at = in_half[:, :, None] & (before[:, :, None] == spots)
    places = jnp.sum(jnp.where(at, arrival[:, :, None], 0), axis=1).reshape(entry_count)
    counts = jnp.sum(in_half.astype(jnp.int32), axis=1)

    marks = received[0][:, 0, block_rows - MARK_ROWS :, :].astype(jnp.float32)
    marks = marks[:, MARK_ROWS - 1, 0]
    rows_of = jnp.where(marks > MARK_LEAST, marks - MARK_BASE, float(block_rows)).astype(jnp.int32)
    arrivals = jnp.arange(rows_of.shape[0], dtype=jnp.int32)
    valid = jnp.sum(
        jnp.where(places[:, None] == arrivals[None, :], rows_of[None, :], 0), axis=1
    ).reshape(patch_blocks, slots)
    valid = jnp.where(spots[None, :] < counts[:, None], valid, 0)
    sizes_of = (valid + GRANULE - 1) // GRANULE
    offsets = jnp.sum(
        jnp.where(spots[None, None, :] < spots[None, :, None], sizes_of[:, None, :], 0), axis=2
    )
    tile_count = pl.cdiv(slots * block_rows, KEY_TILE)
    bias_shape = (patch_blocks, tile_count * KEY_TILE // LANES, LANES)
    key_at = LANES * lax.broadcasted_iota(jnp.int32, bias_shape, 1) + lax.broadcasted_iota(
        jnp.int32, bias_shape, 2
    )
    first_key = (offsets * GRANULE)[:, :, None, None]
    seen = (key_at[:, None] >= first_key) & (key_at[:, None] < first_key + valid[:, :, None, None])
    bias = jnp.where(jnp.any(seen, axis=1), 0.0, masked_value).astype(jnp.float32)
    tables = (places, counts, offsets.reshape(entry_count), sizes_of.reshape(entry_count))

    q_other, o_other, received[0] = lax.optimization_barrier(
        (q_other, o_other, received[0])
    )

    def both_halves(own, other):
        return jnp.where(zh == 0, own, other), jnp.where(zh == 0, other, own)

    q_both = both_halves(query_proj, q_other)
    q_wide = jnp.stack([w.reshape(features, local_heads, head_size) for w in q_both], axis=2)
    q_wide = jnp.pad(q_wide, ((0, 0), (0, 0), (0, 0), (0, LANES - head_size)))
    q_wide = q_wide.reshape(features, local_heads * 2 * LANES)
    o_both = both_halves(output_proj, o_other)
    o_wide = jnp.stack([w.reshape(local_heads, head_size, features) for w in o_both], axis=1)
    o_wide = jnp.pad(o_wide, ((0, 0), (0, 0), (LANES - head_size, 0), (0, 0)))
    o_wide = o_wide.reshape(local_heads * 2 * LANES, features)
    queries = (
        jnp.dot(patches, q_wide, preferred_element_type=jnp.float32) * head_scale
    ).astype(jnp.bfloat16)
    backs = nt_dot(cotangent, o_wide).astype(jnp.bfloat16)

    small = zl_size == 2 and y_size == 2
    own_width = local_heads * head_size
    o_blocks = jnp.stack(o_both).reshape(2, own_width, model, columns).transpose(2, 0, 1, 3)
    q_blocks = jnp.stack(q_both).reshape(2, model, columns, own_width).transpose(1, 0, 3, 2)
    blocks = lax.dynamic_slice_in_dim(
        jnp.concatenate([o_blocks, q_blocks], axis=3), zh * inner, inner, 0
    )

    part_count = 2 if patch_blocks % 2 == 0 else 1
    part_patches = patch_blocks // part_count
    results = [None] * part_count
    traded = []
    own = []
    for c in range(local_heads):
        final = c + 1 == local_heads
        if final:
            blocks, _ = lax.optimization_barrier((blocks, received[c]))
            if small:
                cols = jnp.stack([across(blocks, d, inner) for d in range(inner)])
            else:
                cols = lax.all_gather(blocks, ("zl", "y"), axis=0, tiled=False)
        outs, douts, mine = attention(
            tables, bias, queries, backs, received[c], c, slots, head_scale
        )
        theirs = swap(mine, "zh")
        parts = [
            merge(outs, douts, mine, theirs, start, part_patches, head_scale, head_size)
            for start in range(0, patch_blocks, part_patches)
        ]
        if not final:
            parts, bias = lax.optimization_barrier((parts, bias))
        merged = []
        for part in parts:
            if final and merged:
                part, _ = lax.optimization_barrier((part, merged[-1]))
            other = swap(part, "zh").astype(jnp.float32)
            merged.append((part.astype(jnp.float32) + other).astype(jnp.bfloat16))
        by_rows = [
            trade(x.reshape(inner, x.shape[0] // inner, x.shape[1]), spot, small) for x in merged
        ]
        if not final:
            traded.append(by_rows)
            own.append(merged)
            continue
        for i, earlier in enumerate(traded):
            results = [
                project(pieces, cols, before, False, i)
                for pieces, before in zip(earlier, results)
            ]
        behind = merged
        if traded:
            behind, _ = lax.optimization_barrier((merged, results))
        own.append(behind)
        outputs = []
        for pieces, before in zip(by_rows, results):
            outputs += in_order(trade(project(pieces, cols, before, True, c), spot, small), spot, small)
    attended = jnp.concatenate([x[:, :columns] for x in outputs], axis=0)
    patch_grad = jnp.concatenate([x[:, columns:] for x in outputs], axis=0)
    own = [
        jnp.concatenate([lax.dynamic_slice_in_dim(x, zh * LANES, LANES, 1) for x in xs], axis=0)
        for xs in own
    ]

    dquery = jnp.concatenate([x[:, :head_size] for x in own], axis=1)
    heads_out = jnp.concatenate([x[:, head_size:] for x in own], axis=1)
    query_term = (
        lax.dot_general(
            patches, dquery, (((0,), (0,)), ((), ())), preferred_element_type=jnp.float32
        )
        * grad_scale
    )
    output_term = (
        lax.dot_general(
            heads_out, cotangent, (((0,), (0,)), ((), ())), preferred_element_type=jnp.float32
        )
        * grad_scale
    )
    return (
        attended,
        patch_grad,
        scatter_sum(query_term, groups, 0),
        scatter_sum(output_term, groups, 1),
    )


def solution(mesh):
    groups, model = mesh.shape["dp"], mesh.shape["mp"]
    sizes = (groups, model // 4, 2)
    split = Mesh(
        mesh.devices.reshape(groups, 2, model // 4, 2), ("dp", "zh", "zl", "y")
    )
    mp = ("zh", "zl", "y")
    every = ("dp",) + mp
    return jax.shard_map(
        functools.partial(local, sizes=sizes),
        mesh=split,
        in_specs=(
            P("dp", None),
            P(None, mp),
            P(mp, None),
            P(every, None, None, None),
            P(every),
            P(),
            P("dp", None),
        ),
        out_specs=(P("dp", mp), P("dp", mp), P("dp", mp), P(mp, "dp")),
        check_vma=False,
    )
```

```python
import functools
import math

import jax
import jax.numpy as jnp
from jax import lax
from jax.experimental import pallas as pl
from jax.experimental.pallas import tpu as pltpu
from jax.sharding import Mesh
from jax.sharding import PartitionSpec as P

masked_value = -1e30
LANES = 128
MARK_ROWS = 16
MARK_BASE = 100.0
MARK_LEAST = 64.0
GRANULE = 32
KEY_TILE = 512


def pack_kernel(
    chosen, counts, lengths, cache_ref, out_ref, *, chunk, local_heads, inner, capacity
):
    slot = pl.program_id(0) * capacity + pl.program_id(1)

    @pl.when(pl.program_id(1) < counts[pl.program_id(0)])
    def _():
        by_head = pltpu.einshape("rhd->hrd", cache_ref[0])
        block_rows, width = by_head.shape[1:]
        valid = lengths[chosen[slot]]
        shape = (MARK_ROWS, width)
        corner = (lax.broadcasted_iota(jnp.int32, shape, 0) == MARK_ROWS - 1) & (
            lax.broadcasted_iota(jnp.int32, shape, 1) == 0
        )
        corner = corner & (valid < block_rows)
        mark = valid.astype(jnp.float32) + MARK_BASE
        for r in range(inner):
            for half in range(2):
                tile = by_head[(half * inner + r) * local_heads + chunk]
                out_ref[0, r, 0, half] = tile
                last = tile[block_rows - MARK_ROWS :].astype(jnp.float32)
                out_ref[0, r, 0, half, block_rows - MARK_ROWS :, :] = jnp.where(
                    corner, mark, last
                ).astype(jnp.bfloat16)


def pack_blocks(chosen, counts, lengths, cache, chunk, groups, inner, capacity, local_heads):
    _, block_rows, heads, width = cache.shape
    return pl.pallas_call(
        functools.partial(
            pack_kernel, chunk=chunk, local_heads=local_heads, inner=inner, capacity=capacity
        ),
        grid_spec=pltpu.PrefetchScalarGridSpec(
            num_scalar_prefetch=3,
            grid=(groups, capacity),
            in_specs=[
                pl.BlockSpec(
                    (1, block_rows, heads, width),
                    lambda g, s, ch, ct, ln: (ch[g * capacity + s], 0, 0, 0),
                )
            ],
            out_specs=pl.BlockSpec(
                (1, inner, 1, 2, block_rows, width),
                lambda g, s, ch, ct, ln: (g, 0, s, 0, 0, 0),
            ),
        ),
        out_shape=jax.ShapeDtypeStruct(
            (groups, inner, capacity, 2, block_rows, width), cache.dtype
        ),
        compiler_params=pltpu.CompilerParams(vmem_limit_bytes=32 << 20),
        cost_estimate=pl.CostEstimate(
            flops=0, transcendentals=0, bytes_accessed=groups * capacity * 2 * 262144
        ),
    )(chosen, counts, lengths, cache)


def nt_dot(left, right):
    return lax.dot_general(
        left, right, (((1,), (1,)), ((), ())), preferred_element_type=jnp.float32
    )


def attention_kernel(
    places, counts, offsets, sizes, q_ref, b_ref, bias_ref, recv_ref, co_ref, ds_ref, stat_ref,
    kv, scores, probs, top, acc, dacc, columns, sems, *, slots, scale,
):
    patch = pl.program_id(0)
    block_rows, width = recv_ref.shape[2:]
    steps = block_rows // GRANULE
    folds = KEY_TILE // LANES

    def each_copy(which, act):
        @pl.loop(0, counts[which])
        def _(j):
            entry = which * slots + j
            at = pl.multiple_of(offsets[entry] * GRANULE, GRANULE)
            for size in range(1, steps + 1):

                @pl.when(sizes[entry] == size)
                def _():
                    act(
                        pltpu.make_async_copy(
                            recv_ref.at[places[entry], :, pl.ds(0, size * GRANULE), :],
                            kv.at[which % 2, :, pl.ds(at, size * GRANULE), :],
                            sems.at[which % 2, j],
                        )
                    )

    @pl.when(patch == 0)
    def _():
        each_copy(patch, lambda copy: copy.start())

    @pl.when(patch + 1 < pl.num_programs(0))
    def _():
        each_copy(patch + 1, lambda copy: copy.start())

    filled = offsets[patch * slots + slots - 1] + sizes[patch * slots + slots - 1]
    per_tile = KEY_TILE // GRANULE
    tiles = jnp.maximum((filled + per_tile - 1) // per_tile, 1)

    @pl.loop(filled, tiles * per_tile)
    def _(g):
        kv[patch % 2, :, pl.ds(pl.multiple_of(g * GRANULE, GRANULE), GRANULE), :] = jnp.zeros(
            (2, GRANULE, width), kv.dtype
        )

    each_copy(patch, lambda copy: copy.wait())

    def key_tile(t, head):
        return kv[patch % 2, head, pl.ds(pl.multiple_of(t * KEY_TILE, KEY_TILE), KEY_TILE), :]

    rows = q_ref.shape[0]
    lanes = [pl.ds(head * LANES, LANES) for head in range(2)]
    top[...] = jnp.full_like(top, masked_value)
    acc[...] = jnp.zeros_like(acc)
    dacc[...] = jnp.zeros_like(dacc)

    @pl.loop(0, tiles)
    def _(t):
        for head in range(2):
            score = nt_dot(q_ref[:, lanes[head]], key_tile(t, head))
            best = top[head]
            for fold in range(folds):
                part = score[:, fold * LANES : (fold + 1) * LANES]
                part = part + bias_ref[0, pl.ds(t * folds + fold, 1), :]
                scores[head, t, :, fold * LANES : (fold + 1) * LANES] = part
                best = jnp.maximum(best, part)
            top[head] = best

    row_max = [jnp.max(top[head], axis=1, keepdims=True) for head in range(2)]
    ones = jnp.ones((KEY_TILE, LANES), jnp.bfloat16)

    @pl.loop(0, tiles)
    def _(t):
        for head in range(2):
            weights = jnp.exp(scores[head, t] - row_max[head]).astype(jnp.bfloat16)
            probs[head, t] = weights
            acc[head] += jnp.dot(
                weights,
                jnp.concatenate([key_tile(t, head), ones], axis=1),
                preferred_element_type=jnp.float32,
            )

    inverse, inner, stats = [], [], []
    for head in range(2):
        row_sum = acc[head, :, width : width + 1]
        inverse.append(1.0 / row_sum)
        outs = acc[head, :, :width] * inverse[head]
        co_ref[:, lanes[head]] = outs
        inner.append(
            jnp.sum(outs * b_ref[:, lanes[head]].astype(jnp.float32), axis=1, keepdims=True)
        )
        stats += [row_max[head] + jnp.log(row_sum), inner[head]]

    @pl.loop(0, tiles)
    def _(t):
        for head in range(2):
            dprobs = nt_dot(b_ref[:, lanes[head]], key_tile(t, head))
            dscores = (probs[head, t].astype(jnp.float32) * (dprobs - inner[head])).astype(
                jnp.bfloat16
            )
            dacc[head] += jnp.dot(dscores, key_tile(t, head), preferred_element_type=jnp.float32)

    for head in range(2):
        ds_ref[:, lanes[head]] = dacc[head] * (inverse[head] * scale)
    lane = lax.broadcasted_iota(jnp.int32, (rows, LANES), 1)
    columns[rows:, :] = jnp.zeros((columns.shape[0] - rows, LANES), jnp.float32)
    picked = jnp.where(lane == 0, stats[0], stats[1])
    picked = jnp.where(lane == 2, stats[2], picked)
    columns[:rows, :] = jnp.where(lane == 3, stats[3], picked)
    stat_ref[0] = jnp.transpose(columns[...])[:8]


def attention(tables, bias, queries, backs, received, chunk, slots, scale):
    patch_blocks = bias.shape[0]
    total_rows = queries.shape[0]
    rows = total_rows // patch_blocks
    padded = pl.cdiv(rows, LANES) * LANES
    block_rows, width = received.shape[2:]
    tiles = pl.cdiv(slots * block_rows, KEY_TILE)
    wide = pl.BlockSpec((rows, 2 * LANES), lambda p, *_: (p, chunk))
    out = pl.BlockSpec((rows, 2 * LANES), lambda p, *_: (p, 0))
    return pl.pallas_call(
        functools.partial(attention_kernel, slots=slots, scale=scale),
        grid_spec=pltpu.PrefetchScalarGridSpec(
            num_scalar_prefetch=4,
            grid=(patch_blocks,),
            in_specs=[
                wide,
                wide,
                pl.BlockSpec((1,) + bias.shape[1:], lambda p, *_: (p, 0, 0)),
                pl.BlockSpec(memory_space=pl.ANY),
            ],
            out_specs=[out, out, pl.BlockSpec((1, 8, padded), lambda p, *_: (p, 0, 0))],
            scratch_shapes=[
                pltpu.VMEM((2, 2, tiles * KEY_TILE, width), jnp.bfloat16),
                pltpu.VMEM((2, tiles, rows, KEY_TILE), jnp.float32),
                pltpu.VMEM((2, tiles, rows, KEY_TILE), jnp.bfloat16),
                pltpu.VMEM((2, rows, LANES), jnp.float32),
                pltpu.VMEM((2, rows, width + LANES), jnp.float32),
                pltpu.VMEM((2, rows, width), jnp.float32),
                pltpu.VMEM((padded, LANES), jnp.float32),
                pltpu.SemaphoreType.DMA((2, slots)),
            ],
        ),
        out_shape=[jax.ShapeDtypeStruct((total_rows, 2 * LANES), jnp.float32)] * 2
        + [jax.ShapeDtypeStruct((patch_blocks, 8, padded), jnp.float32)],
        compiler_params=pltpu.CompilerParams(vmem_limit_bytes=58 << 20),
        cost_estimate=pl.CostEstimate(
            flops=8 * total_rows * slots * block_rows * width,
            transcendentals=total_rows * slots * block_rows,
            bytes_accessed=40 << 20,
        ),
    )(*tables, queries, backs, bias, received)


def merge_kernel(co_ref, ds_ref, mine_ref, theirs_ref, out_ref, *, scale, split):
    rows = co_ref.shape[0]
    mine, theirs = mine_ref[0], theirs_ref[0]
    kind = lax.broadcasted_iota(jnp.int32, mine.shape, 0)
    gap = mine - theirs
    share = 1.0 / (1.0 + jnp.exp(-gap))
    rest = 1.0 / (1.0 + jnp.exp(gap))
    rest_below = jnp.concatenate([rest[:1], rest[:-1]], axis=0)
    table = jnp.where(kind % 2 == 0, share, rest_below * gap * scale)
    tall = jnp.transpose(
        jnp.concatenate([table, jnp.zeros((LANES - 8, table.shape[1]), jnp.float32)], axis=0)
    )[:rows]
    lower = lax.broadcasted_iota(jnp.int32, (rows, LANES), 1) < split
    for head in range(2):
        lanes = pl.ds(head * LANES, LANES)
        weight = tall[:, 2 * head : 2 * head + 1]
        shift = tall[:, 2 * head + 1 : 2 * head + 2]
        outs = co_ref[:, lanes]
        value = weight * jnp.where(lower, ds_ref[:, lanes] + shift * outs, outs)
        out_ref[:, lanes] = value.astype(jnp.bfloat16)


def merge(outs, douts, mine, theirs, first, count, scale, split):
    patch_blocks, _, padded = mine.shape
    rows = outs.shape[0] // patch_blocks
    wide = pl.BlockSpec((rows, 2 * LANES), lambda p: (first + p, 0))
    flat = pl.BlockSpec((1, 8, padded), lambda p: (first + p, 0, 0))
    return pl.pallas_call(
        functools.partial(merge_kernel, scale=scale, split=split),
        grid=(count,),
        in_specs=[wide, wide, flat, flat],
        out_specs=pl.BlockSpec((rows, 2 * LANES), lambda p: (p, 0)),
        out_shape=jax.ShapeDtypeStruct((count * rows, 2 * LANES), jnp.bfloat16),
        cost_estimate=pl.CostEstimate(
            flops=20 * count * rows * LANES,
            transcendentals=0,
            bytes_accessed=20 * count * rows * LANES,
        ),
    )(outs, douts, mine, theirs)


def project_kernel(spot, *refs, count, dests, chunk, depth, has_before):
    cols = refs[count : count + dests]
    before = refs[count + dests] if has_before else None
    out, weights = refs[-2], refs[-1]
    half = weights.shape[3] // 2
    empty = jnp.zeros((depth, half), weights.dtype)
    for j in range(dests):
        dest = spot[j]
        for i in range(count):
            for z in range(2):
                own = cols[j][i, z, pl.ds(chunk * depth, depth), :]
                grad_rows = pl.ds(2 * z * depth, depth)
                out_rows = pl.ds((2 * z + 1) * depth, depth)
                weights[dest, i, grad_rows, :half] = empty
                weights[dest, i, grad_rows, half:] = own[:, half:]
                weights[dest, i, out_rows, :half] = own[:, :half]
                weights[dest, i, out_rows, half:] = empty
    for dest in range(dests):
        value = jnp.dot(refs[0][...], weights[dest, 0], preferred_element_type=jnp.float32)
        for i in range(1, count):
            value += jnp.dot(refs[i][...], weights[dest, i], preferred_element_type=jnp.float32)
        if has_before:
            value += before[dest]
        out[dest] = value.astype(out.dtype)


def project(pieces, cols, order, before, last, chunk):
    count, dests = len(pieces), len(cols)
    rows, depth = pieces[0].shape
    width = cols[0].shape[3]
    inputs = [*pieces, *cols] + ([] if before is None else [before])
    full = lambda x: pl.BlockSpec(x.shape, lambda i, *_: (0,) * x.ndim)
    result = jax.ShapeDtypeStruct((dests, rows, width), jnp.bfloat16 if last else jnp.float32)
    return pl.pallas_call(
        functools.partial(
            project_kernel, count=count, dests=dests, chunk=chunk, depth=depth // 4,
            has_before=before is not None,
        ),
        grid_spec=pltpu.PrefetchScalarGridSpec(
            num_scalar_prefetch=1,
            grid=(1,),
            in_specs=[full(x) for x in inputs],
            out_specs=full(result),
            scratch_shapes=[pltpu.VMEM((dests, count, depth, width), jnp.bfloat16)],
        ),
        out_shape=result,
        compiler_params=pltpu.CompilerParams(vmem_limit_bytes=40 << 20),
        cost_estimate=pl.CostEstimate(
            flops=2 * rows * depth * count * width * dests,
            transcendentals=0,
            bytes_accessed=2 * rows * (depth * count + 2 * width)
            + 2 * sum(x.size for x in cols),
        ),
    )(order, *inputs)


def swap(x, axis):
    return lax.ppermute(x, axis, [(0, 1), (1, 0)])


def trade(blocks, spot, small):
    count = blocks.shape[0]
    if not small:
        whole = lax.all_to_all(blocks, ("zl", "y"), split_axis=0, concat_axis=0, tiled=True)
        return [whole[i] for i in range(count)]
    return [
        across(lax.dynamic_index_in_dim(blocks, spot ^ d, 0, keepdims=False), d, count)
        for d in range(count)
    ]


def across(x, d, count):
    if d == 0:
        return x
    return lax.ppermute(x, ("zl", "y"), [(i, i ^ d) for i in range(count)])


def in_order(pieces, spot, small):
    if not small:
        return pieces
    low, high = spot % 2 == 1, spot // 2 == 1
    return [
        jnp.where(
            high,
            jnp.where(low, pieces[i ^ 3], pieces[i ^ 2]),
            jnp.where(low, pieces[i ^ 1], pieces[i]),
        )
        for i in range(len(pieces))
    ]


def scatter_sum(x, size, dim):
    index = lax.axis_index("dp")
    step = size // 2
    while step >= 1:
        half = x.shape[dim] // 2
        upper = (index // step) % 2
        keep = lax.dynamic_slice_in_dim(x, upper * half, half, dim)
        give = lax.dynamic_slice_in_dim(x, (1 - upper) * half, half, dim)
        got = lax.ppermute(
            give.astype(jnp.bfloat16), "dp", [(i, i ^ step) for i in range(size)]
        )
        x = keep + got.astype(jnp.float32)
        step //= 2
    return x


def local(
    patches, query_proj, output_proj, cache, block_lengths, neighbours, cotangent, *, sizes
):
    groups, zl_size, y_size = sizes
    inner = zl_size * y_size
    model = 2 * inner
    owner_count = groups * model
    group = lax.axis_index("dp")
    zh = lax.axis_index("zh")
    spot = lax.axis_index("zl") * y_size + lax.axis_index("y")
    me = group * model + zh * inner + spot
    local_blocks, block_rows, heads, width = cache.shape
    head_size = width // 2
    local_heads = query_proj.shape[1] // head_size
    features = patches.shape[1]
    columns = features // model
    slots = neighbours.shape[1]
    patch_blocks = neighbours.shape[0] // groups
    entry_count = patch_blocks * slots
    capacity = 2 * entry_count // owner_count
    row_count = patches.shape[0]
    head_scale = 1.0 / math.sqrt(head_size)
    grad_scale = 1.0 / math.sqrt(row_count * groups)

    all_ids = neighbours.reshape(groups, entry_count)
    match = all_ids // local_blocks == me
    order = jnp.arange(entry_count, dtype=jnp.int32)
    earlier = order[None, :] < order[:, None]
    rank = jnp.sum((match[:, None, :] & earlier[None]).astype(jnp.int32), axis=2)
    slot_range = jnp.arange(capacity, dtype=jnp.int32)
    placed = match[:, :, None] & (rank[:, :, None] == slot_range)
    chosen = jnp.sum(
        jnp.where(placed, (all_ids % local_blocks)[:, :, None], 0), axis=1
    ).reshape(groups * capacity)
    send_counts = jnp.sum(match.astype(jnp.int32), axis=1)

    def pack(c):
        return pack_blocks(
            chosen, send_counts, block_lengths, cache, c, groups, inner, capacity, local_heads
        ).reshape(groups * inner, capacity * 2 * block_rows, width)

    def exchange(x):
        return lax.all_to_all(
            x, ("dp", "zl", "y"), split_axis=0, concat_axis=0, tiled=True
        ).reshape(groups * inner * capacity, 2, block_rows, width)

    received = [exchange(pack(0))]
    q_other, o_other = swap(query_proj, "zh"), swap(output_proj, "zh")
    for c in range(1, local_heads):
        packed, q_other, o_other = lax.optimization_barrier((pack(c), q_other, o_other))
        received.append(exchange(packed))

    my_ids = lax.dynamic_slice_in_dim(
        neighbours, group * patch_blocks, patch_blocks, 0
    ).reshape(entry_count)
    owners = my_ids // local_blocks
    slot_of = jnp.sum(((owners[:, None] == owners[None, :]) & earlier).astype(jnp.int32), axis=1)
    source = (owners // model) * inner + owners % inner
    in_half = ((owners % model) // inner == zh).reshape(patch_blocks, slots)
    arrival = (source * capacity + slot_of).reshape(patch_blocks, slots)
    spots = jnp.arange(slots, dtype=jnp.int32)
    before = jnp.sum(
        (in_half[:, None, :] & (spots[None, :] < spots[:, None])[None]).astype(jnp.int32), axis=2
    )
    at = in_half[:, :, None] & (before[:, :, None] == spots)
    places = jnp.sum(jnp.where(at, arrival[:, :, None], 0), axis=1).reshape(entry_count)
    counts = jnp.sum(in_half.astype(jnp.int32), axis=1)

    marks = received[0][:, 0, block_rows - MARK_ROWS :, :].astype(jnp.float32)
    marks = marks[:, MARK_ROWS - 1, 0]
    rows_of = jnp.where(marks > MARK_LEAST, marks - MARK_BASE, float(block_rows)).astype(jnp.int32)
    arrivals = jnp.arange(rows_of.shape[0], dtype=jnp.int32)
    valid = jnp.sum(
        jnp.where(places[:, None] == arrivals[None, :], rows_of[None, :], 0), axis=1
    ).reshape(patch_blocks, slots)
    valid = jnp.where(spots[None, :] < counts[:, None], valid, 0)
    sizes_of = (valid + GRANULE - 1) // GRANULE
    offsets = jnp.sum(
        jnp.where(spots[None, None, :] < spots[None, :, None], sizes_of[:, None, :], 0), axis=2
    )
    tile_count = pl.cdiv(slots * block_rows, KEY_TILE)
    bias_shape = (patch_blocks, tile_count * KEY_TILE // LANES, LANES)
    key_at = LANES * lax.broadcasted_iota(jnp.int32, bias_shape, 1) + lax.broadcasted_iota(
        jnp.int32, bias_shape, 2
    )
    first_key = (offsets * GRANULE)[:, :, None, None]
    seen = (key_at[:, None] >= first_key) & (key_at[:, None] < first_key + valid[:, :, None, None])
    bias = jnp.where(jnp.any(seen, axis=1), 0.0, masked_value).astype(jnp.float32)
    tables = (places, counts, offsets.reshape(entry_count), sizes_of.reshape(entry_count))

    q_other, o_other, received[0] = lax.optimization_barrier(
        (q_other, o_other, received[0])
    )

    def both_halves(own, other):
        return jnp.where(zh == 0, own, other), jnp.where(zh == 0, other, own)

    q_both = both_halves(query_proj, q_other)
    q_wide = jnp.stack([w.reshape(features, local_heads, head_size) for w in q_both], axis=2)
    q_wide = jnp.pad(q_wide, ((0, 0), (0, 0), (0, 0), (0, LANES - head_size)))
    q_wide = q_wide.reshape(features, local_heads * 2 * LANES)
    o_both = both_halves(output_proj, o_other)
    o_wide = jnp.stack([w.reshape(local_heads, head_size, features) for w in o_both], axis=1)
    o_wide = jnp.pad(o_wide, ((0, 0), (0, 0), (LANES - head_size, 0), (0, 0)))
    o_wide = o_wide.reshape(local_heads * 2 * LANES, features)
    queries = (
        jnp.dot(patches, q_wide, preferred_element_type=jnp.float32) * head_scale
    ).astype(jnp.bfloat16)
    backs = nt_dot(cotangent, o_wide).astype(jnp.bfloat16)

    small = zl_size == 2 and y_size == 2
    own_width = local_heads * head_size
    o_blocks = jnp.stack(o_both).reshape(2, own_width, model, columns).transpose(2, 0, 1, 3)
    q_blocks = jnp.stack(q_both).reshape(2, model, columns, own_width).transpose(1, 0, 3, 2)
    blocks = lax.dynamic_slice_in_dim(
        jnp.concatenate([o_blocks, q_blocks], axis=3), zh * inner, inner, 0
    )

    part_count = 2 if patch_blocks % 2 == 0 else 1
    part_patches = patch_blocks // part_count
    results = [None] * part_count
    traded = []
    own = []
    for c in range(local_heads):
        final = c + 1 == local_heads
        if final:
            blocks, _ = lax.optimization_barrier((blocks, received[c]))
            if small and groups == inner:
                cols = [
                    jnp.stack(
                        [
                            across(
                                lax.dynamic_index_in_dim(blocks, group, 0, keepdims=False),
                                d,
                                inner,
                            )
                            for d in range(inner)
                        ]
                    )
                ]
                flip = lambda x, d: lax.ppermute(x, "dp", [(i, i ^ d) for i in range(groups)])
                cols.append(flip(cols[0], 1))
                cols += [flip(cols[0], 2), flip(cols[1], 2)]
                order = group ^ jnp.arange(inner, dtype=jnp.int32)
            else:
                whole = lax.all_gather(blocks, ("zl", "y"), axis=0, tiled=False)
                cols = [whole[:, i] for i in range(inner)]
                order = jnp.arange(inner, dtype=jnp.int32)
        outs, douts, mine = attention(
            tables, bias, queries, backs, received[c], c, slots, head_scale
        )
        theirs = swap(mine, "zh")
        parts = [
            merge(outs, douts, mine, theirs, start, part_patches, head_scale, head_size)
            for start in range(0, patch_blocks, part_patches)
        ]
        if not final:
            parts, bias = lax.optimization_barrier((parts, bias))
        merged, by_rows = [], []
        for part in parts:
            behind_rows = final and bool(merged)
            if behind_rows:
                part, _ = lax.optimization_barrier((part, merged[-1]))
            other = swap(part, "zh")
            if behind_rows:
                other, _ = lax.optimization_barrier((other, (by_rows, traded)))
            x = (part.astype(jnp.float32) + other.astype(jnp.float32)).astype(jnp.bfloat16)
            merged.append(x)
            by_rows.append(
                trade(x.reshape(inner, x.shape[0] // inner, x.shape[1]), spot, small)
            )
        if not final:
            traded.append(by_rows)
            own.append(merged)
            continue
        for i, earlier in enumerate(traded):
            results = [
                project(pieces, cols, order, before, False, i)
                for pieces, before in zip(earlier, results)
            ]
        outputs = [
            project(pieces, cols, order, before, True, c)
            for pieces, before in zip(by_rows, results)
        ]
        behind, _ = lax.optimization_barrier((merged, outputs))
        own.append(behind)
        outputs = [
            x for part in outputs for x in in_order(trade(part, spot, small), spot, small)
        ]
    attended = jnp.concatenate([x[:, :columns] for x in outputs], axis=0)
    patch_grad = jnp.concatenate([x[:, columns:] for x in outputs], axis=0)
    own = [
        jnp.concatenate([lax.dynamic_slice_in_dim(x, zh * LANES, LANES, 1) for x in xs], axis=0)
        for xs in own
    ]

    dquery = jnp.concatenate([x[:, :head_size] for x in own], axis=1)
    heads_out = jnp.concatenate([x[:, head_size:] for x in own], axis=1)
    query_term = (
        lax.dot_general(
            patches, dquery, (((0,), (0,)), ((), ())), preferred_element_type=jnp.float32
        )
        * grad_scale
    )
    output_term = (
        lax.dot_general(
            heads_out, cotangent, (((0,), (0,)), ((), ())), preferred_element_type=jnp.float32
        )
        * grad_scale
    )
    return (
        attended,
        patch_grad,
        scatter_sum(query_term, groups, 0),
        scatter_sum(output_term, groups, 1),
    )


def solution(mesh):
    groups, model = mesh.shape["dp"], mesh.shape["mp"]
    sizes = (groups, model // 4, 2)
    split = Mesh(
        mesh.devices.reshape(groups, 2, model // 4, 2), ("dp", "zh", "zl", "y")
    )
    mp = ("zh", "zl", "y")
    every = ("dp",) + mp
    return jax.shard_map(
        functools.partial(local, sizes=sizes),
        mesh=split,
        in_specs=(
            P("dp", None),
            P(None, mp),
            P(mp, None),
            P(every, None, None, None),
            P(every),
            P(),
            P("dp", None),
        ),
        out_specs=(P("dp", mp), P("dp", mp), P("dp", mp), P(mp, "dp")),
        check_vma=False,
    )
```
